128 devices in a mesh: dom: 16 (over x, y), grp: 8 (over z, core).
Axes of the slice: x: 4, y: 4, z: 4, core: 2. Of those that a mesh axis runs over, the one named last changes fastest.
Arguments:
- blocks: bfloat16 [4096, 128, 256], P(('dom', 'grp')), may hold values from -6 to 6
- tile_values: bfloat16 [4096, 16, 128, 128], P(('dom', 'grp')), may hold values from -0.125 to 0.125
- tile_cols: int32 [4096, 16], P(('dom', 'grp')), may hold values from 0 to 103, as said below
- halo_send: int32 [128, 16, 4], P(('dom', 'grp')), may hold values from 0 to 31
- halo_counts: int32 [128, 16], P(('dom', 'grp')), may hold values from 0 to 4, as said below
- grp_send: int32 [128, 2, 4], P(('dom', 'grp')), may hold values from 0 to 31
- well_send: int32 [128, 16, 4], P(('dom', 'grp')), may hold values from 0 to 31
- well_slot: int32 [2048, 4], P(('dom', 'grp')), may hold values from 0 to 63, as said below
- well_count: int32 [128], P(('dom', 'grp')), may hold values from 1 to 16
- couple_in: bfloat16 [2048, 4, 32, 128], P(('dom', 'grp')), may hold values from -0.25 to 0.25
- couple_out: bfloat16 [2048, 4, 32, 128], P(('dom', 'grp')), may hold values from -1 to 1
- well_inverse: float32 [2048, 32, 32], P(('dom', 'grp')), may hold values from -1 to 1
Outputs:
- pressure_image: bfloat16 [4096, 128, 256], P(('dom', 'grp'))
The draws below stay inside these ranges and needn't reach their ends.
Inputs may be any that keep to these rules, and one draw needn't show every extreme that they name: Column 0 of every row of tile_cols is that block row's own local index (row modulo 32). halo_counts[d, j] is 0 where j is d's own dom index; some device receives 4 from every other partition. `well_slot`: the 64 entries of each device's rows are a permutation of 0 to 63.
All inputs are finite; a program needn't handle non-finite values.
Results may differ from the reference program's by a relative error of at most 0.005.
Values may be sent and summed in bfloat16 or wider, within the bound.
A program may use at most 192 MiB of HBM per device.

```python
import jax
import jax.numpy as jnp
from jax import lax

CB = 128
NV = 256
BLK_DEV = 32
TPB = 16
HS = 4
GH = 4
SEG = 32
WSLOT = 16
WB = 4
NDEV = 128
DOMS = 16
NB = 4096
NW = 2048
WS = 4
NEXT = 104
N_DOM = 16
N_GRP = 8


def draw_tile_cols(key, part):
    first_key, second_key, third_key = jax.random.split(key, 3)
    kind_draw = jax.random.randint(first_key, (NB, TPB), 0, 4)
    local_cols = jax.random.randint(second_key, (NB, TPB), 0, BLK_DEV)
    remote_cols = jax.random.randint(third_key, (NB, TPB), BLK_DEV, NEXT)
    chosen = jnp.where(kind_draw == 0, remote_cols, local_cols)
    own_rows = jnp.arange(NB, dtype=jnp.int32) % BLK_DEV
    chosen = chosen.at[:, 0].set(own_rows)
    chosen = chosen.at[0, 1].set(NEXT - 1)
    return chosen.astype(jnp.int32)


def draw_halo_counts(key, part):
    first_key, second_key = jax.random.split(key, 2)
    live_counts = jax.random.randint(first_key, (NDEV, N_DOM), 0, HS + 1)
    device_ids = jnp.arange(NDEV, dtype=jnp.int32)[:, None]
    peer_ids = jnp.arange(N_DOM, dtype=jnp.int32)[None, :]
    full_device = jax.random.randint(second_key, (), 0, NDEV)
    live_counts = jnp.where(device_ids == full_device, HS, live_counts)
    live_counts = jnp.where(device_ids // N_GRP == peer_ids, 0, live_counts)
    return live_counts.astype(jnp.int32)


def permute_slots(slot_key):
    return jax.random.permutation(slot_key, WSLOT * WB)


def draw_well_slot(key, part):
    device_keys = jax.random.split(key, NDEV)
    perms = jax.vmap(permute_slots)(device_keys)
    return perms.reshape(NW, WB).astype(jnp.int32)


def draw_well_count(key, part):
    first_key, second_key, third_key = jax.random.split(key, 3)
    busy_mask = jax.random.randint(first_key, (NDEV,), 0, 4) == 0
    base_count = jax.random.randint(second_key, (NDEV,), 1, WSLOT // 2 + 1)
    counts = jnp.where(busy_mask, WSLOT, base_count)
    full_device = jax.random.randint(third_key, (), 0, NDEV)
    device_ids = jnp.arange(NDEV, dtype=jnp.int32)
    counts = jnp.where(device_ids == full_device, WSLOT, counts)
    counts = jnp.where(device_ids == (full_device + 1) % NDEV, 1, counts)
    return counts.astype(jnp.int32)


def with_ends(array, rng, least, high):
    shape = array.shape
    index_at = [jax.random.randint(jax.random.fold_in(rng, axis), (), 0, shape[axis]) for axis in range(len(shape))]
    array = array.at[tuple(index_at)].set(least)
    longest = shape.index(max(shape))
    index_at[longest] = (index_at[longest] + 1) % shape[longest]
    return array.at[tuple(index_at)].set(high)


def block_scale(own_key, shape, pieces, least, largest):
    factor_of, own = 1.0, jax.random.fold_in(own_key, 6)
    for axis_at, blocks in pieces:
        steps = jnp.exp(jax.random.uniform(jax.random.fold_in(own, axis_at), (blocks,), jnp.float32, least / len(pieces), largest / len(pieces)))
        factor_of = factor_of * jnp.repeat(steps, shape[axis_at] // blocks).reshape([-1 if axis == axis_at else 1 for axis in range(len(shape))])
    return factor_of


def normal_values(rng, extent, width, most, shards=(), kind=jnp.bfloat16):
    drawn = jax.random.normal(rng, extent, jnp.float32) * width
    if len(shards) > 0:
        drawn = block_scale(rng, extent, shards, -0.22, 0.18) * drawn
    return jnp.clip(drawn, min=-most, max=most).astype(kind)


def setup_inputs(seed: int = 0) -> dict:
    keys = jax.random.split(jax.random.key(seed), 13)
    blocks = normal_values(keys[0], (NB, CB, NV), 1.0, 6.0, ((0, 128),))
    tile_values = normal_values(keys[1], (NB, TPB, CB, CB), (CB * TPB) ** -0.5, 0.125, ((0, 128),))
    tile_cols = draw_tile_cols(jax.random.fold_in(keys[12], 71), 0)
    halo_send = with_ends(jax.random.randint(keys[3], (NDEV, DOMS, HS), 0, BLK_DEV), jax.random.fold_in(keys[3], 1), 0, BLK_DEV - 1).astype(jnp.int32)
    halo_counts = draw_halo_counts(jax.random.fold_in(keys[12], 71), 0)
    grp_send = with_ends(jax.random.randint(keys[5], (NDEV, 2, GH), 0, BLK_DEV), jax.random.fold_in(keys[5], 1), 0, BLK_DEV - 1).astype(jnp.int32)
    well_send = with_ends(jax.random.randint(keys[6], (NDEV, DOMS, WS), 0, BLK_DEV), jax.random.fold_in(keys[6], 1), 0, BLK_DEV - 1).astype(jnp.int32)
    well_slot = draw_well_slot(jax.random.fold_in(keys[12], 71), 0)
    well_count = draw_well_count(jax.random.fold_in(keys[12], 71), 0)
    couple_in = normal_values(keys[9], (NW, WB, SEG, CB), (CB * WB) ** -0.5, 0.25, ((0, 128),))
    couple_out = normal_values(keys[10], (NW, WB, SEG, CB), SEG ** -0.5, 1.0, ((0, 128),))
    well_inverse = normal_values(keys[11], (NW, SEG, SEG), SEG ** -0.5, 1.0, ((0, 128),), jnp.float32)
    return {"blocks": blocks, "tile_values": tile_values, "tile_cols": tile_cols, "halo_send": halo_send, "halo_counts": halo_counts, "grp_send": grp_send, "well_send": well_send, "well_slot": well_slot, "well_count": well_count, "couple_in": couple_in, "couple_out": couple_out, "well_inverse": well_inverse}


def reference(blocks, tile_values, tile_cols, halo_send, halo_counts, grp_send, well_send, well_slot, well_count, couple_in, couple_out, well_inverse):
    by_device = blocks.reshape(NDEV, BLK_DEV, CB, NV)
    tiles_dev = tile_values.reshape(NDEV, BLK_DEV, TPB, CB, CB)
    cols_dev = tile_cols.reshape(NDEV, BLK_DEV, TPB)
    slots_dev = well_slot.reshape(NDEV, WSLOT * WB)
    in_dev = couple_in.reshape(NDEV, WSLOT, WB, SEG, CB)
    out_dev = couple_out.reshape(NDEV, WSLOT, WB, SEG, CB)
    inverse_dev = well_inverse.reshape(NDEV, WSLOT, SEG, SEG)
    peer_ids = jnp.arange(N_DOM, dtype=jnp.int32)

    def owner_work(device):
        dom_index = device // N_GRP
        grp_index = device % N_GRP
        source = peer_ids * N_GRP + grp_index
        picked = well_send[source, dom_index, :]
        received = by_device[source[:, None], picked].reshape(N_DOM * WS, CB, NV)
        coupled = received[slots_dev[device]].reshape(WSLOT, WB, CB, NV)
        summed = jnp.einsum("wcsk,wckv->wsv", in_dev[device].astype(jnp.float32), coupled.astype(jnp.float32))
        live_mask = (jnp.arange(WSLOT, dtype=jnp.int32) < well_count[device]).astype(jnp.float32)
        solved = jnp.einsum("wst,wtv->wsv", inverse_dev[device], summed, precision=lax.Precision.HIGHEST)
        well_state = (solved * live_mask[:, None, None]).astype(jnp.bfloat16)
        contrib = jnp.einsum("wcsk,wsv->wckv", out_dev[device].astype(jnp.float32), well_state.astype(jnp.float32)).astype(jnp.bfloat16)
        slot_order = jnp.argsort(slots_dev[device])
        return contrib.reshape(WSLOT * WB, CB, NV)[slot_order]

    contribs = lax.map(owner_work, jnp.arange(NDEV, dtype=jnp.int32))

    def device_out(device):
        dom_index = device // N_GRP
        grp_index = device % N_GRP
        source = peer_ids * N_GRP + grp_index
        picked = halo_send[source, dom_index, :]
        halo_rows = by_device[source[:, None], picked]
        live_halo = jnp.arange(HS, dtype=jnp.int32)[None, :] < halo_counts[device][:, None]
        halo_rows = jnp.where(live_halo[:, :, None, None], halo_rows, jnp.zeros_like(halo_rows)).reshape(N_DOM * HS, CB, NV)
        lower_dev = jnp.maximum(device - 1, 0)
        upper_dev = jnp.minimum(device + 1, NDEV - 1)
        lower_rim = by_device[lower_dev][grp_send[lower_dev, 1]]
        lower_rim = jnp.where(grp_index > 0, lower_rim, jnp.zeros_like(lower_rim))
        upper_rim = by_device[upper_dev][grp_send[upper_dev, 0]]
        upper_rim = jnp.where(grp_index < N_GRP - 1, upper_rim, jnp.zeros_like(upper_rim))
        extended = jnp.concatenate([by_device[device], halo_rows, lower_rim, upper_rim], 0)
        gathered = extended[cols_dev[device]]
        product = jnp.einsum("btij,btjv->biv", tiles_dev[device].astype(jnp.float32), gathered.astype(jnp.float32))
        slot_index = dom_index * WS + jnp.arange(WS, dtype=jnp.int32)
        incoming = contribs[source[:, None], slot_index[None, :]].reshape(N_DOM * WS, CB, NV)
        targets = well_send[device].reshape(N_DOM * WS)
        result_rows = product.at[targets].add(-incoming.astype(jnp.float32))
        return result_rows.astype(jnp.bfloat16)

    outputs = lax.map(device_out, jnp.arange(NDEV, dtype=jnp.int32))
    return outputs.reshape(NB, CB, NV)
```

```python
import jax
import jax.numpy as jnp
from jax import lax
from jax.sharding import PartitionSpec as P


def padded(value, sides, width):
    for axis, dim in sides:
        devices, length = (lax.axis_size(axis), value.shape[dim])
        up = [(i, (i + 1) % devices) for i in range(devices - 1)]
        down = [(j, i) for i, j in up]
        last = lax.slice_in_dim(value, length - width, length, axis=dim)
        leading = lax.slice_in_dim(value, 0, width, axis=dim)
        before = lax.ppermute(last, axis, up)
        after = lax.ppermute(leading, axis, down)
        value = jnp.concatenate([before, value, after], axis=dim)
    return value


def local_product(extended, tile_values, tile_cols):
    gathered = extended[tile_cols]
    return jnp.einsum("btij,btjv->biv", tile_values, gathered, preferred_element_type=jnp.float32)


def well_states_of(summed, well_inverse, well_count):
    wells = summed.shape[0]
    live_mask = (jnp.arange(wells) < well_count[0]).astype(jnp.float32)
    solved = jnp.einsum("wst,wtv->wsv", well_inverse, summed, precision=lax.Precision.HIGHEST)
    return (solved * live_mask[:, None, None]).astype(jnp.bfloat16)


def subtract_incoming(product, well_send, incoming):
    targets = well_send[0].reshape(-1)
    selector = (targets[None, :] == jnp.arange(product.shape[0])[:, None]).astype(jnp.bfloat16)
    flat_rows = incoming.reshape(targets.shape[0], product.shape[1], product.shape[2])
    return product - jnp.einsum(
        "bq,qkv->bkv", selector, flat_rows, preferred_element_type=jnp.float32
    )


def on_device(
    blocks,
    tile_values,
    tile_cols,
    halo_send,
    halo_counts,
    grp_send,
    well_send,
    well_slot,
    well_count,
    couple_in,
    couple_out,
    well_inverse,
):
    dom_count = lax.axis_size("dom")
    halo_width = halo_send.shape[2]
    rim_width = grp_send.shape[2]
    slot_width = well_send.shape[2]
    cell_count = blocks.shape[1]
    vec_count = blocks.shape[2]
    wells, couplings = well_slot.shape
    seg = couple_in.shape[2]
    slot_total = dom_count * slot_width
    halo_pack = blocks[halo_send[0]]
    rim_pack = blocks[grp_send[0].reshape(-1)]
    rim_ext = padded(rim_pack, (("grp", 0),), rim_width)
    rim_rows = jnp.concatenate([rim_ext[:rim_width], rim_ext[rim_ext.shape[0] - rim_width :]], 0)
    slot_order = jnp.argsort(well_slot.reshape(-1))
    well_pack = blocks[well_send[0]]
    send_pack = jnp.concatenate([halo_pack, well_pack], 1)
    recv_pack = lax.all_to_all(send_pack, "dom", split_axis=0, concat_axis=0, tiled=True)
    halo_rows = recv_pack[:, :halo_width]
    well_rows = recv_pack[:, halo_width:]
    coupled = well_rows.reshape(slot_total, cell_count, vec_count)[well_slot.reshape(-1)]
    coupled = coupled.reshape(wells, couplings, cell_count, vec_count)
    summed = jnp.einsum("wcsk,wckv->wsv", couple_in, coupled, preferred_element_type=jnp.float32)
    well_state = well_states_of(summed, well_inverse, well_count)
    slot_well = slot_order // couplings
    state_slots = well_state[slot_well]
    out_slots = couple_out.reshape(wells * couplings, seg, cell_count)[slot_order]
    state_pack = jnp.concatenate([state_slots, out_slots], 2)
    state_pack = state_pack.reshape(dom_count, slot_width, seg, vec_count + cell_count)
    state_in = lax.all_to_all(state_pack, "dom", split_axis=0, concat_axis=0, tiled=True)
    state_in = state_in.reshape(slot_total, seg, vec_count + cell_count)
    incoming = jnp.einsum(
        "qsk,qsv->qkv",
        state_in[:, :, vec_count:],
        state_in[:, :, :vec_count],
        preferred_element_type=jnp.float32,
    ).astype(jnp.bfloat16)
    live_halo = jnp.arange(halo_width)[None, :] < halo_counts[0][:, None]
    halo_rows = jnp.where(live_halo[:, :, None, None], halo_rows, jnp.zeros_like(halo_rows))
    extended = jnp.concatenate(
        [blocks, halo_rows.reshape(dom_count * halo_width, cell_count, vec_count), rim_rows], 0
    )
    product = local_product(extended, tile_values, tile_cols)
    return subtract_incoming(product, well_send, incoming).astype(jnp.bfloat16)


def solution(mesh):
    in_specs = (
        P(("dom", "grp"), None, None),
        P(("dom", "grp"), None, None, None),
        P(("dom", "grp"), None),
        P(("dom", "grp"), None, None),
        P(("dom", "grp"), None),
        P(("dom", "grp"), None, None),
        P(("dom", "grp"), None, None),
        P(("dom", "grp"), None),
        P(("dom", "grp")),
        P(("dom", "grp"), None, None, None),
        P(("dom", "grp"), None, None, None),
        P(("dom", "grp"), None, None),
    )
    out_specs = P(("dom", "grp"), None, None)
    return jax.shard_map(
        on_device, mesh=mesh, in_specs=in_specs, out_specs=out_specs, check_vma=False
    )
```

```python
import jax
import jax.numpy as jnp
from jax import lax
from jax.sharding import PartitionSpec as P


def padded(value, sides, width):
    for axis, dim in sides:
        devices, length = (lax.axis_size(axis), value.shape[dim])
        up = [(i, (i + 1) % devices) for i in range(devices - 1)]
        down = [(j, i) for i, j in up]
        last = lax.slice_in_dim(value, length - width, length, axis=dim)
        leading = lax.slice_in_dim(value, 0, width, axis=dim)
        before = lax.ppermute(last, axis, up)
        after = lax.ppermute(leading, axis, down)
        value = jnp.concatenate([before, value, after], axis=dim)
    return value


def local_product(extended, tile_values, tile_cols):
    gathered = extended[tile_cols]
    return jnp.einsum("btij,btjv->biv", tile_values, gathered, preferred_element_type=jnp.float32)


def well_states_of(summed, well_inverse, well_count):
    wells = summed.shape[0]
    live_mask = (jnp.arange(wells) < well_count[0]).astype(jnp.float32)
    solved = jnp.einsum("wst,wtv->wsv", well_inverse, summed, precision=lax.Precision.HIGHEST)
    return (solved * live_mask[:, None, None]).astype(jnp.bfloat16)


def subtract_incoming(product, well_send, incoming):
    targets = well_send[0].reshape(-1)
    selector = (targets[None, :] == jnp.arange(product.shape[0])[:, None]).astype(jnp.bfloat16)
    flat_rows = incoming.reshape(targets.shape[0], product.shape[1], product.shape[2])
    return product - jnp.einsum(
        "bq,qkv->bkv", selector, flat_rows, preferred_element_type=jnp.float32
    )


def on_device(
    blocks,
    tile_values,
    tile_cols,
    halo_send,
    halo_counts,
    grp_send,
    well_send,
    well_slot,
    well_count,
    couple_in,
    couple_out,
    well_inverse,
):
    dom_count = lax.axis_size("dom")
    halo_width = halo_send.shape[2]
    rim_width = grp_send.shape[2]
    slot_width = well_send.shape[2]
    cell_count = blocks.shape[1]
    vec_count = blocks.shape[2]
    wells, couplings = well_slot.shape
    seg = couple_in.shape[2]
    slot_total = dom_count * slot_width
    halo_pack = blocks[halo_send[0]]
    rim_pack = blocks[grp_send[0].reshape(-1)]
    rim_ext = padded(rim_pack, (("grp", 0),), rim_width)
    rim_rows = jnp.concatenate([rim_ext[:rim_width], rim_ext[rim_ext.shape[0] - rim_width :]], 0)
    slot_order = jnp.argsort(well_slot.reshape(-1))
    slot_well = slot_order // couplings
    in_slots = couple_in.reshape(wells * couplings, seg, cell_count)[slot_order]
    in_slots = in_slots.reshape(dom_count, slot_width * seg * cell_count // vec_count, vec_count)
    halo_flat = halo_pack.reshape(dom_count, halo_width * cell_count, vec_count)
    send_pack = jnp.concatenate([halo_flat, in_slots], 1)
    recv_pack = lax.all_to_all(send_pack, "dom", split_axis=0, concat_axis=0, tiled=True)
    halo_rows = recv_pack[:, : halo_width * cell_count].reshape(dom_count, halo_width, cell_count, vec_count)
    in_recv = recv_pack[:, halo_width * cell_count :].reshape(dom_count, slot_width, seg, cell_count)
    well_pack = blocks[well_send[0]]
    partial = jnp.einsum("qcsk,qckv->qcsv", in_recv, well_pack, preferred_element_type=jnp.float32)
    partial_in = lax.all_to_all(partial, "dom", split_axis=0, concat_axis=0, tiled=True)
    partial_in = partial_in.reshape(slot_total, seg, vec_count)
    summed = jnp.sum(partial_in[well_slot.reshape(-1)].reshape(wells, couplings, seg, vec_count), axis=1)
    well_state = well_states_of(summed, well_inverse, well_count)
    state_slots = well_state[slot_well]
    out_slots = couple_out.reshape(wells * couplings, seg, cell_count)[slot_order]
    state_pack = jnp.concatenate([state_slots, out_slots], 2)
    state_pack = state_pack.reshape(dom_count, slot_width, seg, vec_count + cell_count)
    state_in = lax.all_to_all(state_pack, "dom", split_axis=0, concat_axis=0, tiled=True)
    state_in = state_in.reshape(slot_total, seg, vec_count + cell_count)
    incoming = jnp.einsum(
        "qsk,qsv->qkv",
        state_in[:, :, vec_count:],
        state_in[:, :, :vec_count],
        preferred_element_type=jnp.float32,
    ).astype(jnp.bfloat16)
    live_halo = jnp.arange(halo_width)[None, :] < halo_counts[0][:, None]
    halo_rows = jnp.where(live_halo[:, :, None, None], halo_rows, jnp.zeros_like(halo_rows))
    extended = jnp.concatenate(
        [blocks, halo_rows.reshape(dom_count * halo_width, cell_count, vec_count), rim_rows], 0
    )
    product = local_product(extended, tile_values, tile_cols)
    return subtract_incoming(product, well_send, incoming).astype(jnp.bfloat16)


def solution(mesh):
    in_specs = (
        P(("dom", "grp"), None, None),
        P(("dom", "grp"), None, None, None),
        P(("dom", "grp"), None),
        P(("dom", "grp"), None, None),
        P(("dom", "grp"), None),
        P(("dom", "grp"), None, None),
        P(("dom", "grp"), None, None),
        P(("dom", "grp"), None),
        P(("dom", "grp")),
        P(("dom", "grp"), None, None, None),
        P(("dom", "grp"), None, None, None),
        P(("dom", "grp"), None, None),
    )
    out_specs = P(("dom", "grp"), None, None)
    return jax.shard_map(
        on_device, mesh=mesh, in_specs=in_specs, out_specs=out_specs, check_vma=False
    )
```

```python
import jax
import jax.numpy as jnp
from jax import lax
from jax.sharding import PartitionSpec as P
from jax.experimental import pallas as pl
from jax.experimental.pallas import tpu as pltpu


def padded(value, sides, width):
    for axis, dim in sides:
        devices, length = (lax.axis_size(axis), value.shape[dim])
        up = [(i, (i + 1) % devices) for i in range(devices - 1)]
        down = [(j, i) for i, j in up]
        last = lax.slice_in_dim(value, length - width, length, axis=dim)
        leading = lax.slice_in_dim(value, 0, width, axis=dim)
        before = lax.ppermute(last, axis, up)
        after = lax.ppermute(leading, axis, down)
        value = jnp.concatenate([before, value, after], axis=dim)
    return value


def product_kernel(cols_ref, ext_ref, tiles_ref, out_ref):
    rows, tiles_per_row = tiles_ref.shape[0], tiles_ref.shape[1]
    first = pl.program_id(0) * rows
    for r in range(rows):
        acc = jnp.zeros(out_ref.shape[1:], jnp.float32)
        for t in range(tiles_per_row):
            col = cols_ref[(first + r) * tiles_per_row + t]
            acc = acc + jnp.dot(tiles_ref[r, t], ext_ref[col], preferred_element_type=jnp.float32)
        out_ref[r] = acc


def local_product(extended, tile_values, tile_cols):
    block_rows, tiles_per_row, cells, _ = tile_values.shape
    ext_blocks, _, vecs = extended.shape
    rows = 4
    grid_spec = pltpu.PrefetchScalarGridSpec(
        num_scalar_prefetch=1,
        grid=(block_rows // rows,),
        in_specs=[
            pl.BlockSpec((ext_blocks, cells, vecs), lambda k, cols: (0, 0, 0)),
            pl.BlockSpec((rows, tiles_per_row, cells, cells), lambda k, cols: (k, 0, 0, 0)),
        ],
        out_specs=pl.BlockSpec((rows, cells, vecs), lambda k, cols: (k, 0, 0)),
    )
    flops = 2 * block_rows * tiles_per_row * cells * cells * vecs
    moved = tile_values.size * 2 + extended.size * 2 + block_rows * cells * vecs * 4
    return pl.pallas_call(
        product_kernel,
        out_shape=jax.ShapeDtypeStruct((block_rows, cells, vecs), jnp.float32),
        grid_spec=grid_spec,
        cost_estimate=pl.CostEstimate(flops=flops, transcendentals=0, bytes_accessed=moved),
    )(tile_cols.reshape(-1), extended, tile_values)


def well_states_of(summed, well_inverse, well_count):
    wells = summed.shape[0]
    live_mask = (jnp.arange(wells) < well_count[0]).astype(jnp.float32)
    solved = jnp.einsum("wst,wtv->wsv", well_inverse, summed, precision=lax.Precision.HIGHEST)
    return (solved * live_mask[:, None, None]).astype(jnp.bfloat16)


def subtract_incoming(product, well_send, incoming):
    targets = well_send[0].reshape(-1)
    selector = (targets[None, :] == jnp.arange(product.shape[0])[:, None]).astype(jnp.bfloat16)
    flat_rows = incoming.reshape(targets.shape[0], product.shape[1], product.shape[2])
    return product - jnp.einsum(
        "bq,qkv->bkv", selector, flat_rows, preferred_element_type=jnp.float32
    )


def on_device(
    blocks,
    tile_values,
    tile_cols,
    halo_send,
    halo_counts,
    grp_send,
    well_send,
    well_slot,
    well_count,
    couple_in,
    couple_out,
    well_inverse,
):
    dom_count = lax.axis_size("dom")
    halo_width = halo_send.shape[2]
    rim_width = grp_send.shape[2]
    slot_width = well_send.shape[2]
    cell_count = blocks.shape[1]
    vec_count = blocks.shape[2]
    wells, couplings = well_slot.shape
    seg = couple_in.shape[2]
    slot_total = dom_count * slot_width
    halo_pack = blocks[halo_send[0]]
    rim_pack = blocks[grp_send[0].reshape(-1)]
    rim_ext = padded(rim_pack, (("grp", 0),), rim_width)
    rim_rows = jnp.concatenate([rim_ext[:rim_width], rim_ext[rim_ext.shape[0] - rim_width :]], 0)
    slot_order = jnp.argsort(well_slot.reshape(-1))
    slot_well = slot_order // couplings
    in_slots = couple_in.reshape(wells * couplings, seg, cell_count)[slot_order]
    in_slots = in_slots.reshape(dom_count, slot_width * seg * cell_count // vec_count, vec_count)
    halo_flat = halo_pack.reshape(dom_count, halo_width * cell_count, vec_count)
    send_pack = jnp.concatenate([halo_flat, in_slots], 1)
    recv_pack = lax.all_to_all(send_pack, "dom", split_axis=0, concat_axis=0, tiled=True)
    halo_rows = recv_pack[:, : halo_width * cell_count].reshape(dom_count, halo_width, cell_count, vec_count)
    in_recv = recv_pack[:, halo_width * cell_count :].reshape(dom_count, slot_width, seg, cell_count)
    well_pack = blocks[well_send[0]]
    partial = jnp.einsum("qcsk,qckv->qcsv", in_recv, well_pack, preferred_element_type=jnp.float32)
    partial_in = lax.all_to_all(partial, "dom", split_axis=0, concat_axis=0, tiled=True)
    partial_in = partial_in.reshape(slot_total, seg, vec_count)
    summed = jnp.sum(partial_in[well_slot.reshape(-1)].reshape(wells, couplings, seg, vec_count), axis=1)
    well_state = well_states_of(summed, well_inverse, well_count)
    state_slots = well_state[slot_well]
    out_slots = couple_out.reshape(wells * couplings, seg, cell_count)[slot_order]
    state_pack = jnp.concatenate([state_slots, out_slots], 2)
    state_pack = state_pack.reshape(dom_count, slot_width, seg, vec_count + cell_count)
    state_in = lax.all_to_all(state_pack, "dom", split_axis=0, concat_axis=0, tiled=True)
    state_in = state_in.reshape(slot_total, seg, vec_count + cell_count)
    incoming = jnp.einsum(
        "qsk,qsv->qkv",
        state_in[:, :, vec_count:],
        state_in[:, :, :vec_count],
        preferred_element_type=jnp.float32,
    ).astype(jnp.bfloat16)
    live_halo = jnp.arange(halo_width)[None, :] < halo_counts[0][:, None]
    halo_rows = jnp.where(live_halo[:, :, None, None], halo_rows, jnp.zeros_like(halo_rows))
    extended = jnp.concatenate(
        [blocks, halo_rows.reshape(dom_count * halo_width, cell_count, vec_count), rim_rows], 0
    )
    product = local_product(extended, tile_values, tile_cols)
    return subtract_incoming(product, well_send, incoming).astype(jnp.bfloat16)


def solution(mesh):
    in_specs = (
        P(("dom", "grp"), None, None),
        P(("dom", "grp"), None, None, None),
        P(("dom", "grp"), None),
        P(("dom", "grp"), None, None),
        P(("dom", "grp"), None),
        P(("dom", "grp"), None, None),
        P(("dom", "grp"), None, None),
        P(("dom", "grp"), None),
        P(("dom", "grp")),
        P(("dom", "grp"), None, None, None),
        P(("dom", "grp"), None, None, None),
        P(("dom", "grp"), None, None),
    )
    out_specs = P(("dom", "grp"), None, None)
    return jax.shard_map(
        on_device, mesh=mesh, in_specs=in_specs, out_specs=out_specs, check_vma=False
    )
```

```python
import jax
import jax.numpy as jnp
from jax import lax
from jax.sharding import PartitionSpec as P
from jax.experimental import pallas as pl
from jax.experimental.pallas import tpu as pltpu


def padded(value, sides, width):
    for axis, dim in sides:
        devices, length = (lax.axis_size(axis), value.shape[dim])
        up = [(i, (i + 1) % devices) for i in range(devices - 1)]
        down = [(j, i) for i, j in up]
        last = lax.slice_in_dim(value, length - width, length, axis=dim)
        leading = lax.slice_in_dim(value, 0, width, axis=dim)
        before = lax.ppermute(last, axis, up)
        after = lax.ppermute(leading, axis, down)
        value = jnp.concatenate([before, value, after], axis=dim)
    return value


def product_kernel(cols_ref, ext_ref, tiles_ref, out_ref):
    rows, tiles_per_row = tiles_ref.shape[0], tiles_ref.shape[1]
    first = pl.program_id(0) * rows
    for r in range(rows):
        acc = jnp.zeros(out_ref.shape[1:], jnp.float32)
        for t in range(tiles_per_row):
            col = cols_ref[(first + r) * tiles_per_row + t]
            acc = acc + jnp.dot(tiles_ref[r, t], ext_ref[col], preferred_element_type=jnp.float32)
        out_ref[r] = acc


def local_product(extended, tile_values, tile_cols):
    block_rows, tiles_per_row, cells, _ = tile_values.shape
    ext_blocks, _, vecs = extended.shape
    rows = 4
    grid_spec = pltpu.PrefetchScalarGridSpec(
        num_scalar_prefetch=1,
        grid=(block_rows // rows,),
        in_specs=[
            pl.BlockSpec((ext_blocks, cells, vecs), lambda k, cols: (0, 0, 0)),
            pl.BlockSpec((rows, tiles_per_row, cells, cells), lambda k, cols: (k, 0, 0, 0)),
        ],
        out_specs=pl.BlockSpec((rows, cells, vecs), lambda k, cols: (k, 0, 0)),
    )
    flops = 2 * block_rows * tiles_per_row * cells * cells * vecs
    moved = tile_values.size * 2 + extended.size * 2 + block_rows * cells * vecs * 4
    return pl.pallas_call(
        product_kernel,
        out_shape=jax.ShapeDtypeStruct((block_rows, cells, vecs), jnp.float32),
        grid_spec=grid_spec,
        cost_estimate=pl.CostEstimate(flops=flops, transcendentals=0, bytes_accessed=moved),
    )(tile_cols.reshape(-1), extended, tile_values)


def exchange_kernel(send_ref, recv_ref, send_sems, recv_sems, own_sem):
    count = send_ref.shape[0]
    me = lax.axis_index("dom")
    grp = lax.axis_index("grp")
    barrier = pltpu.get_barrier_semaphore()
    for step in range(1, count):
        peer = lax.rem(me + step, count)
        pl.semaphore_signal(
            barrier, inc=1, device_id=(peer, grp), device_id_type=pl.DeviceIdType.MESH
        )
    pl.semaphore_wait(barrier, count - 1)
    own = pltpu.make_async_copy(send_ref.at[me], recv_ref.at[me], own_sem)
    own.start()
    copies = []
    for step in range(1, count):
        peer = lax.rem(me + step, count)
        copy = pltpu.make_async_remote_copy(
            src_ref=send_ref.at[peer],
            dst_ref=recv_ref.at[me],
            send_sem=send_sems.at[step],
            recv_sem=recv_sems.at[step],
            device_id=(peer, grp),
            device_id_type=pl.DeviceIdType.MESH,
        )
        copy.start()
        copies.append(copy)
    for copy in copies:
        copy.wait_send()
    for copy in copies:
        copy.wait_recv()
    own.wait()


def dom_exchange(value, collective):
    count = value.shape[0]
    return pl.pallas_call(
        exchange_kernel,
        out_shape=jax.ShapeDtypeStruct(value.shape, value.dtype),
        in_specs=[pl.BlockSpec(memory_space=pl.ANY)],
        out_specs=pl.BlockSpec(memory_space=pl.ANY),
        scratch_shapes=[
            pltpu.SemaphoreType.DMA((count,)),
            pltpu.SemaphoreType.DMA((count,)),
            pltpu.SemaphoreType.DMA,
        ],
        compiler_params=pltpu.CompilerParams(collective_id=collective, has_side_effects=True),
    )(value)


def well_states_of(summed, well_inverse, well_count):
    wells = summed.shape[0]
    live_mask = (jnp.arange(wells) < well_count[0]).astype(jnp.float32)
    solved = jnp.einsum("wst,wtv->wsv", well_inverse, summed, precision=lax.Precision.HIGHEST)
    return (solved * live_mask[:, None, None]).astype(jnp.bfloat16)


def subtract_incoming(product, well_send, incoming):
    targets = well_send[0].reshape(-1)
    selector = (targets[None, :] == jnp.arange(product.shape[0])[:, None]).astype(jnp.bfloat16)
    flat_rows = incoming.reshape(targets.shape[0], product.shape[1], product.shape[2])
    return product - jnp.einsum(
        "bq,qkv->bkv", selector, flat_rows, preferred_element_type=jnp.float32
    )


def on_device(
    blocks,
    tile_values,
    tile_cols,
    halo_send,
    halo_counts,
    grp_send,
    well_send,
    well_slot,
    well_count,
    couple_in,
    couple_out,
    well_inverse,
):
    dom_count = lax.axis_size("dom")
    halo_width = halo_send.shape[2]
    rim_width = grp_send.shape[2]
    slot_width = well_send.shape[2]
    cell_count = blocks.shape[1]
    vec_count = blocks.shape[2]
    wells, couplings = well_slot.shape
    seg = couple_in.shape[2]
    slot_total = dom_count * slot_width
    halo_pack = blocks[halo_send[0]]
    rim_pack = blocks[grp_send[0].reshape(-1)]
    rim_ext = padded(rim_pack, (("grp", 0),), rim_width)
    rim_rows = jnp.concatenate([rim_ext[:rim_width], rim_ext[rim_ext.shape[0] - rim_width :]], 0)
    slot_order = jnp.argsort(well_slot.reshape(-1))
    slot_well = slot_order // couplings
    in_slots = couple_in.reshape(wells * couplings, seg, cell_count)[slot_order]
    in_slots = in_slots.reshape(dom_count, slot_width * seg * cell_count // vec_count, vec_count)
    halo_flat = halo_pack.reshape(dom_count, halo_width * cell_count, vec_count)
    send_pack = jnp.concatenate([halo_flat, in_slots], 1)
    recv_pack = dom_exchange(send_pack, 0)
    halo_rows = recv_pack[:, : halo_width * cell_count].reshape(dom_count, halo_width, cell_count, vec_count)
    in_recv = recv_pack[:, halo_width * cell_count :].reshape(dom_count, slot_width, seg, cell_count)
    well_pack = blocks[well_send[0]]
    partial = jnp.einsum("qcsk,qckv->qcsv", in_recv, well_pack, preferred_element_type=jnp.float32)
    partial_in = lax.all_to_all(partial, "dom", split_axis=0, concat_axis=0, tiled=True)
    partial_in = partial_in.reshape(slot_total, seg, vec_count)
    summed = jnp.sum(partial_in[well_slot.reshape(-1)].reshape(wells, couplings, seg, vec_count), axis=1)
    well_state = well_states_of(summed, well_inverse, well_count)
    state_slots = well_state[slot_well]
    out_slots = couple_out.reshape(wells * couplings, seg, cell_count)[slot_order]
    state_pack = jnp.concatenate([state_slots, out_slots], 2)
    state_pack = state_pack.reshape(dom_count, slot_width, seg, vec_count + cell_count)
    state_in = lax.all_to_all(state_pack, "dom", split_axis=0, concat_axis=0, tiled=True)
    state_in = state_in.reshape(slot_total, seg, vec_count + cell_count)
    incoming = jnp.einsum(
        "qsk,qsv->qkv",
        state_in[:, :, vec_count:],
        state_in[:, :, :vec_count],
        preferred_element_type=jnp.float32,
    ).astype(jnp.bfloat16)
    live_halo = jnp.arange(halo_width)[None, :] < halo_counts[0][:, None]
    halo_rows = jnp.where(live_halo[:, :, None, None], halo_rows, jnp.zeros_like(halo_rows))
    extended = jnp.concatenate(
        [blocks, halo_rows.reshape(dom_count * halo_width, cell_count, vec_count), rim_rows], 0
    )
    product = local_product(extended, tile_values, tile_cols)
    return subtract_incoming(product, well_send, incoming).astype(jnp.bfloat16)


def solution(mesh):
    in_specs = (
        P(("dom", "grp"), None, None),
        P(("dom", "grp"), None, None, None),
        P(("dom", "grp"), None),
        P(("dom", "grp"), None, None),
        P(("dom", "grp"), None),
        P(("dom", "grp"), None, None),
        P(("dom", "grp"), None, None),
        P(("dom", "grp"), None),
        P(("dom", "grp")),
        P(("dom", "grp"), None, None, None),
        P(("dom", "grp"), None, None, None),
        P(("dom", "grp"), None, None),
    )
    out_specs = P(("dom", "grp"), None, None)
    return jax.shard_map(
        on_device, mesh=mesh, in_specs=in_specs, out_specs=out_specs, check_vma=False
    )
```

```python
import jax
import jax.numpy as jnp
from jax import lax
from jax.sharding import PartitionSpec as P
from jax.experimental import pallas as pl
from jax.experimental.pallas import tpu as pltpu


def padded(value, sides, width):
    for axis, dim in sides:
        devices, length = (lax.axis_size(axis), value.shape[dim])
        up = [(i, (i + 1) % devices) for i in range(devices - 1)]
        down = [(j, i) for i, j in up]
        last = lax.slice_in_dim(value, length - width, length, axis=dim)
        leading = lax.slice_in_dim(value, 0, width, axis=dim)
        before = lax.ppermute(last, axis, up)
        after = lax.ppermute(leading, axis, down)
        value = jnp.concatenate([before, value, after], axis=dim)
    return value


def product_kernel(cols_ref, ext_ref, tiles_ref, out_ref):
    rows, tiles_per_row = tiles_ref.shape[0], tiles_ref.shape[1]
    first = pl.program_id(0) * rows
    for r in range(rows):
        acc = jnp.zeros(out_ref.shape[1:], jnp.float32)
        for t in range(tiles_per_row):
            col = cols_ref[(first + r) * tiles_per_row + t]
            acc = acc + jnp.dot(tiles_ref[r, t], ext_ref[col], preferred_element_type=jnp.float32)
        out_ref[r] = acc


def local_product(extended, tile_values, tile_cols):
    block_rows, tiles_per_row, cells, _ = tile_values.shape
    ext_blocks, _, vecs = extended.shape
    rows = 4
    grid_spec = pltpu.PrefetchScalarGridSpec(
        num_scalar_prefetch=1,
        grid=(block_rows // rows,),
        in_specs=[
            pl.BlockSpec((ext_blocks, cells, vecs), lambda k, cols: (0, 0, 0)),
            pl.BlockSpec((rows, tiles_per_row, cells, cells), lambda k, cols: (k, 0, 0, 0)),
        ],
        out_specs=pl.BlockSpec((rows, cells, vecs), lambda k, cols: (k, 0, 0)),
    )
    flops = 2 * block_rows * tiles_per_row * cells * cells * vecs
    moved = tile_values.size * 2 + extended.size * 2 + block_rows * cells * vecs * 4
    return pl.pallas_call(
        product_kernel,
        out_shape=jax.ShapeDtypeStruct((block_rows, cells, vecs), jnp.float32),
        grid_spec=grid_spec,
        cost_estimate=pl.CostEstimate(flops=flops, transcendentals=0, bytes_accessed=moved),
    )(tile_cols.reshape(-1), extended, tile_values)


def well_states_of(summed, well_inverse, well_count):
    wells = summed.shape[0]
    live_mask = (jnp.arange(wells) < well_count[0]).astype(jnp.float32)
    solved = jnp.einsum("wst,wtv->wsv", well_inverse, summed, precision=lax.Precision.HIGHEST)
    return (solved * live_mask[:, None, None]).astype(jnp.bfloat16)


def subtract_incoming(product, well_send, incoming):
    targets = well_send[0].reshape(-1)
    selector = (targets[None, :] == jnp.arange(product.shape[0])[:, None]).astype(jnp.bfloat16)
    flat_rows = incoming.reshape(targets.shape[0], product.shape[1], product.shape[2])
    return product - jnp.einsum(
        "bq,qkv->bkv", selector, flat_rows, preferred_element_type=jnp.float32
    )


def on_device(
    blocks,
    tile_values,
    tile_cols,
    halo_send,
    halo_counts,
    grp_send,
    well_send,
    well_slot,
    well_count,
    couple_in,
    couple_out,
    well_inverse,
):
    dom_count = lax.axis_size("dom")
    halo_width = halo_send.shape[2]
    rim_width = grp_send.shape[2]
    slot_width = well_send.shape[2]
    cell_count = blocks.shape[1]
    vec_count = blocks.shape[2]
    wells, couplings = well_slot.shape
    seg = couple_in.shape[2]
    slot_total = dom_count * slot_width
    halo_pack = blocks[halo_send[0]]
    rim_pack = blocks[grp_send[0].reshape(-1)]
    rim_ext = padded(rim_pack, (("grp", 0),), rim_width)
    rim_rows = jnp.concatenate([rim_ext[:rim_width], rim_ext[rim_ext.shape[0] - rim_width :]], 0)
    slot_order = jnp.argsort(well_slot.reshape(-1))
    slot_well = slot_order // couplings
    in_slots = couple_in.reshape(wells * couplings, seg, cell_count)[slot_order]
    in_slots = in_slots.reshape(dom_count, slot_width * seg * cell_count // vec_count, vec_count)
    halo_flat = halo_pack.reshape(dom_count, halo_width * cell_count, vec_count)
    send_pack = jnp.concatenate([halo_flat, in_slots], 1)
    recv_pack = lax.all_to_all(send_pack, "dom", split_axis=0, concat_axis=0, tiled=True)
    halo_rows = recv_pack[:, : halo_width * cell_count].reshape(dom_count, halo_width, cell_count, vec_count)
    in_recv = recv_pack[:, halo_width * cell_count :].reshape(dom_count, slot_width, seg, cell_count)
    well_pack = blocks[well_send[0]]
    partial = jnp.einsum("qcsk,qckv->qcsv", in_recv, well_pack, preferred_element_type=jnp.float32)
    partial_in = lax.all_to_all(partial.astype(jnp.bfloat16), "dom", split_axis=0, concat_axis=0, tiled=True)
    partial_in = partial_in.reshape(slot_total, seg, vec_count).astype(jnp.float32)
    summed = jnp.sum(partial_in[well_slot.reshape(-1)].reshape(wells, couplings, seg, vec_count), axis=1)
    well_state = well_states_of(summed, well_inverse, well_count)
    state_slots = well_state[slot_well]
    out_slots = couple_out.reshape(wells * couplings, seg, cell_count)[slot_order]
    state_pack = jnp.concatenate([state_slots, out_slots], 2)
    state_pack = state_pack.reshape(dom_count, slot_width, seg, vec_count + cell_count)
    state_in = lax.all_to_all(state_pack, "dom", split_axis=0, concat_axis=0, tiled=True)
    state_in = state_in.reshape(slot_total, seg, vec_count + cell_count)
    incoming = jnp.einsum(
        "qsk,qsv->qkv",
        state_in[:, :, vec_count:],
        state_in[:, :, :vec_count],
        preferred_element_type=jnp.float32,
    ).astype(jnp.bfloat16)
    live_halo = jnp.arange(halo_width)[None, :] < halo_counts[0][:, None]
    halo_rows = jnp.where(live_halo[:, :, None, None], halo_rows, jnp.zeros_like(halo_rows))
    extended = jnp.concatenate(
        [blocks, halo_rows.reshape(dom_count * halo_width, cell_count, vec_count), rim_rows], 0
    )
    product = local_product(extended, tile_values, tile_cols)
    return subtract_incoming(product, well_send, incoming).astype(jnp.bfloat16)


def solution(mesh):
    in_specs = (
        P(("dom", "grp"), None, None),
        P(("dom", "grp"), None, None, None),
        P(("dom", "grp"), None),
        P(("dom", "grp"), None, None),
        P(("dom", "grp"), None),
        P(("dom", "grp"), None, None),
        P(("dom", "grp"), None, None),
        P(("dom", "grp"), None),
        P(("dom", "grp")),
        P(("dom", "grp"), None, None, None),
        P(("dom", "grp"), None, None, None),
        P(("dom", "grp"), None, None),
    )
    out_specs = P(("dom", "grp"), None, None)
    return jax.shard_map(
        on_device, mesh=mesh, in_specs=in_specs, out_specs=out_specs, check_vma=False
    )
```

```python
import jax
import jax.numpy as jnp
from jax import lax
from jax.sharding import PartitionSpec as P
from jax.experimental import pallas as pl
from jax.experimental.pallas import tpu as pltpu


def padded(value, sides, width):
    for axis, dim in sides:
        devices, length = (lax.axis_size(axis), value.shape[dim])
        up = [(i, (i + 1) % devices) for i in range(devices - 1)]
        down = [(j, i) for i, j in up]
        last = lax.slice_in_dim(value, length - width, length, axis=dim)
        leading = lax.slice_in_dim(value, 0, width, axis=dim)
        before = lax.ppermute(last, axis, up)
        after = lax.ppermute(leading, axis, down)
        value = jnp.concatenate([before, value, after], axis=dim)
    return value


def product_kernel(cols_ref, ext_ref, tiles_ref, out_ref):
    rows, tiles_per_row = tiles_ref.shape[0], tiles_ref.shape[1]
    first = pl.program_id(0) * rows
    for r in range(rows):
        acc = jnp.zeros(out_ref.shape[1:], jnp.float32)
        for t in range(tiles_per_row):
            col = cols_ref[(first + r) * tiles_per_row + t]
            acc = acc + jnp.dot(tiles_ref[r, t], ext_ref[col], preferred_element_type=jnp.float32)
        out_ref[r] = acc


def local_product(extended, tile_values, tile_cols):
    block_rows, tiles_per_row, cells, _ = tile_values.shape
    ext_blocks, _, vecs = extended.shape
    rows = 4
    grid_spec = pltpu.PrefetchScalarGridSpec(
        num_scalar_prefetch=1,
        grid=(block_rows // rows,),
        in_specs=[
            pl.BlockSpec((ext_blocks, cells, vecs), lambda k, cols: (0, 0, 0)),
            pl.BlockSpec((rows, tiles_per_row, cells, cells), lambda k, cols: (k, 0, 0, 0)),
        ],
        out_specs=pl.BlockSpec((rows, cells, vecs), lambda k, cols: (k, 0, 0)),
    )
    flops = 2 * block_rows * tiles_per_row * cells * cells * vecs
    moved = tile_values.size * 2 + extended.size * 2 + block_rows * cells * vecs * 4
    return pl.pallas_call(
        product_kernel,
        out_shape=jax.ShapeDtypeStruct((block_rows, cells, vecs), jnp.float32),
        grid_spec=grid_spec,
        cost_estimate=pl.CostEstimate(flops=flops, transcendentals=0, bytes_accessed=moved),
    )(tile_cols.reshape(-1), extended, tile_values)


SIDE = 4
NEAR = ((1, 0), (3, 0), (0, 1), (0, 3), (1, 1), (1, 3), (3, 1), (3, 3))
RELAYED = (
    ((2, 0), (1, 0), 0), ((2, 0), (3, 0), 1),
    ((2, 1), (1, 0), 0), ((2, 1), (3, 0), 1),
    ((2, 3), (1, 0), 0), ((2, 3), (3, 0), 1),
    ((0, 2), (0, 1), 0), ((0, 2), (0, 3), 1),
    ((1, 2), (0, 1), 0), ((1, 2), (0, 3), 1),
    ((3, 2), (0, 1), 0), ((3, 2), (0, 3), 1),
    ((2, 2), (1, 1), 0), ((2, 2), (3, 3), 1),
)


def exchange_kernel(send_ref, recv_ref, relay_ref, near_send, near_recv, leg_send, leg_recv,
                    fwd_send, fwd_recv, own_sem):
    me = lax.axis_index("dom")
    grp = lax.axis_index("grp")
    row, col = me // SIDE, me % SIDE
    half = send_ref.shape[1] // 2

    def at(offset):
        return ((row + offset[0]) % SIDE) * SIDE + (col + offset[1]) % SIDE

    def remote(src, dst, send_sem, recv_sem, offset):
        return pltpu.make_async_remote_copy(
            src_ref=src, dst_ref=dst, send_sem=send_sem, recv_sem=recv_sem,
            device_id=(at(offset), grp), device_id_type=pl.DeviceIdType.MESH,
        )

    barrier = pltpu.get_barrier_semaphore()
    for offset in NEAR:
        pl.semaphore_signal(
            barrier, inc=1, device_id=(at(offset), grp), device_id_type=pl.DeviceIdType.MESH
        )
    pl.semaphore_wait(barrier, len(NEAR))
    own = pltpu.make_async_copy(send_ref.at[me], recv_ref.at[me], own_sem)
    own.start()
    legs = []
    for k, (target, relay, part) in enumerate(RELAYED):
        leg = remote(send_ref.at[at(target), pl.ds(part * half, half)], relay_ref.at[k],
                     leg_send.at[k], leg_recv.at[k], relay)
        leg.start()
        legs.append(leg)
    nears = []
    for k, offset in enumerate(NEAR):
        near = remote(send_ref.at[at(offset)], recv_ref.at[me], near_send.at[k], near_recv.at[k], offset)
        near.start()
        nears.append(near)
    fwds = []
    for k, (target, relay, part) in enumerate(RELAYED):
        legs[k].wait_recv()
        source = at(((SIDE - relay[0]) % SIDE, (SIDE - relay[1]) % SIDE))
        onward = ((target[0] - relay[0]) % SIDE, (target[1] - relay[1]) % SIDE)
        fwd = remote(relay_ref.at[k], recv_ref.at[source, pl.ds(part * half, half)],
                     fwd_send.at[k], fwd_recv.at[k], onward)
        fwd.start()
        fwds.append(fwd)
    for leg in legs:
        leg.wait_send()
    for near in nears:
        near.wait_send()
    for near in nears:
        near.wait_recv()
    for fwd in fwds:
        fwd.wait_send()
    for fwd in fwds:
        fwd.wait_recv()
    own.wait()


def dom_exchange(value, collective):
    count, rows, lanes = value.shape
    relay_shape = jax.ShapeDtypeStruct((len(RELAYED), rows // 2, lanes), value.dtype)
    recv, _ = pl.pallas_call(
        exchange_kernel,
        out_shape=(jax.ShapeDtypeStruct(value.shape, value.dtype), relay_shape),
        in_specs=[pl.BlockSpec(memory_space=pl.ANY)],
        out_specs=(pl.BlockSpec(memory_space=pl.ANY), pl.BlockSpec(memory_space=pl.ANY)),
        scratch_shapes=[
            pltpu.SemaphoreType.DMA((len(NEAR),)),
            pltpu.SemaphoreType.DMA((len(NEAR),)),
            pltpu.SemaphoreType.DMA((len(RELAYED),)),
            pltpu.SemaphoreType.DMA((len(RELAYED),)),
            pltpu.SemaphoreType.DMA((len(RELAYED),)),
            pltpu.SemaphoreType.DMA((len(RELAYED),)),
            pltpu.SemaphoreType.DMA,
        ],
        compiler_params=pltpu.CompilerParams(collective_id=collective, has_side_effects=True),
    )(value)
    return recv


def well_states_of(summed, well_inverse, well_count):
    wells = summed.shape[0]
    live_mask = (jnp.arange(wells) < well_count[0]).astype(jnp.float32)
    solved = jnp.einsum("wst,wtv->wsv", well_inverse, summed, precision=lax.Precision.HIGHEST)
    return (solved * live_mask[:, None, None]).astype(jnp.bfloat16)


def subtract_incoming(product, well_send, incoming):
    targets = well_send[0].reshape(-1)
    selector = (targets[None, :] == jnp.arange(product.shape[0])[:, None]).astype(jnp.bfloat16)
    flat_rows = incoming.reshape(targets.shape[0], product.shape[1], product.shape[2])
    return product - jnp.einsum(
        "bq,qkv->bkv", selector, flat_rows, preferred_element_type=jnp.float32
    )


def on_device(
    blocks,
    tile_values,
    tile_cols,
    halo_send,
    halo_counts,
    grp_send,
    well_send,
    well_slot,
    well_count,
    couple_in,
    couple_out,
    well_inverse,
):
    dom_count = lax.axis_size("dom")
    halo_width = halo_send.shape[2]
    rim_width = grp_send.shape[2]
    slot_width = well_send.shape[2]
    cell_count = blocks.shape[1]
    vec_count = blocks.shape[2]
    wells, couplings = well_slot.shape
    seg = couple_in.shape[2]
    slot_total = dom_count * slot_width
    halo_pack = blocks[halo_send[0]]
    rim_pack = blocks[grp_send[0].reshape(-1)]
    rim_ext = padded(rim_pack, (("grp", 0),), rim_width)
    rim_rows = jnp.concatenate([rim_ext[:rim_width], rim_ext[rim_ext.shape[0] - rim_width :]], 0)
    slot_order = jnp.argsort(well_slot.reshape(-1))
    slot_well = slot_order // couplings
    in_slots = couple_in.reshape(wells * couplings, seg, cell_count)[slot_order]
    in_slots = in_slots.reshape(dom_count, slot_width * seg * cell_count // vec_count, vec_count)
    halo_flat = halo_pack.reshape(dom_count, halo_width * cell_count, vec_count)
    send_pack = jnp.concatenate([halo_flat, in_slots], 1)
    recv_pack = dom_exchange(send_pack, 0)
    halo_rows = recv_pack[:, : halo_width * cell_count].reshape(dom_count, halo_width, cell_count, vec_count)
    in_recv = recv_pack[:, halo_width * cell_count :].reshape(dom_count, slot_width, seg, cell_count)
    well_pack = blocks[well_send[0]]
    partial = jnp.einsum("qcsk,qckv->qcsv", in_recv, well_pack, preferred_element_type=jnp.float32)
    partial_in = lax.all_to_all(partial, "dom", split_axis=0, concat_axis=0, tiled=True)
    partial_in = partial_in.reshape(slot_total, seg, vec_count)
    summed = jnp.sum(partial_in[well_slot.reshape(-1)].reshape(wells, couplings, seg, vec_count), axis=1)
    well_state = well_states_of(summed, well_inverse, well_count)
    state_slots = well_state[slot_well]
    out_slots = couple_out.reshape(wells * couplings, seg, cell_count)[slot_order]
    state_pack = jnp.concatenate([state_slots, out_slots], 2)
    state_pack = state_pack.reshape(dom_count, slot_width, seg, vec_count + cell_count)
    state_in = lax.all_to_all(state_pack, "dom", split_axis=0, concat_axis=0, tiled=True)
    state_in = state_in.reshape(slot_total, seg, vec_count + cell_count)
    incoming = jnp.einsum(
        "qsk,qsv->qkv",
        state_in[:, :, vec_count:],
        state_in[:, :, :vec_count],
        preferred_element_type=jnp.float32,
    ).astype(jnp.bfloat16)
    live_halo = jnp.arange(halo_width)[None, :] < halo_counts[0][:, None]
    halo_rows = jnp.where(live_halo[:, :, None, None], halo_rows, jnp.zeros_like(halo_rows))
    extended = jnp.concatenate(
        [blocks, halo_rows.reshape(dom_count * halo_width, cell_count, vec_count), rim_rows], 0
    )
    product = local_product(extended, tile_values, tile_cols)
    return subtract_incoming(product, well_send, incoming).astype(jnp.bfloat16)


def solution(mesh):
    in_specs = (
        P(("dom", "grp"), None, None),
        P(("dom", "grp"), None, None, None),
        P(("dom", "grp"), None),
        P(("dom", "grp"), None, None),
        P(("dom", "grp"), None),
        P(("dom", "grp"), None, None),
        P(("dom", "grp"), None, None),
        P(("dom", "grp"), None),
        P(("dom", "grp")),
        P(("dom", "grp"), None, None, None),
        P(("dom", "grp"), None, None, None),
        P(("dom", "grp"), None, None),
    )
    out_specs = P(("dom", "grp"), None, None)
    return jax.shard_map(
        on_device, mesh=mesh, in_specs=in_specs, out_specs=out_specs, check_vma=False
    )
```

```python
import jax
import jax.numpy as jnp
from jax import lax
from jax.sharding import PartitionSpec as P
from jax.experimental import pallas as pl
from jax.experimental.pallas import tpu as pltpu


def padded(value, sides, width):
    for axis, dim in sides:
        devices, length = (lax.axis_size(axis), value.shape[dim])
        up = [(i, (i + 1) % devices) for i in range(devices - 1)]
        down = [(j, i) for i, j in up]
        last = lax.slice_in_dim(value, length - width, length, axis=dim)
        leading = lax.slice_in_dim(value, 0, width, axis=dim)
        before = lax.ppermute(last, axis, up)
        after = lax.ppermute(leading, axis, down)
        value = jnp.concatenate([before, value, after], axis=dim)
    return value


def product_kernel(cols_ref, ext_ref, tiles_ref, out_ref):
    rows, tiles_per_row = tiles_ref.shape[0], tiles_ref.shape[1]
    first = pl.program_id(0) * rows
    for r in range(rows):
        acc = jnp.zeros(out_ref.shape[1:], jnp.float32)
        for t in range(tiles_per_row):
            col = cols_ref[(first + r) * tiles_per_row + t]
            acc = acc + jnp.dot(tiles_ref[r, t], ext_ref[col], preferred_element_type=jnp.float32)
        out_ref[r] = acc


def local_product(extended, tile_values, tile_cols):
    block_rows, tiles_per_row, cells, _ = tile_values.shape
    ext_blocks, _, vecs = extended.shape
    rows = 4
    grid_spec = pltpu.PrefetchScalarGridSpec(
        num_scalar_prefetch=1,
        grid=(block_rows // rows,),
        in_specs=[
            pl.BlockSpec((ext_blocks, cells, vecs), lambda k, cols: (0, 0, 0)),
            pl.BlockSpec((rows, tiles_per_row, cells, cells), lambda k, cols: (k, 0, 0, 0)),
        ],
        out_specs=pl.BlockSpec((rows, cells, vecs), lambda k, cols: (k, 0, 0)),
    )
    flops = 2 * block_rows * tiles_per_row * cells * cells * vecs
    moved = tile_values.size * 2 + extended.size * 2 + block_rows * cells * vecs * 4
    return pl.pallas_call(
        product_kernel,
        out_shape=jax.ShapeDtypeStruct((block_rows, cells, vecs), jnp.float32),
        grid_spec=grid_spec,
        cost_estimate=pl.CostEstimate(flops=flops, transcendentals=0, bytes_accessed=moved),
    )(tile_cols.reshape(-1), extended, tile_values)


SIDE = 4
NEAR = ((1, 0), (3, 0), (0, 1), (0, 3), (1, 1), (1, 3), (3, 1), (3, 3))
RELAYED = (
    ((2, 0), (1, 0), 0), ((2, 0), (3, 0), 1),
    ((2, 1), (1, 0), 0), ((2, 1), (3, 0), 1),
    ((2, 3), (1, 0), 0), ((2, 3), (3, 0), 1),
    ((0, 2), (0, 1), 0), ((0, 2), (0, 3), 1),
    ((1, 2), (0, 1), 0), ((1, 2), (0, 3), 1),
    ((3, 2), (0, 1), 0), ((3, 2), (0, 3), 1),
    ((2, 2), (1, 1), 0), ((2, 2), (3, 3), 1),
)


def exchange_kernel(*refs):
    parts = (len(refs) - 7) // 3
    send_refs, recv_refs, relay_refs = refs[:parts], refs[parts : 2 * parts], refs[2 * parts : 3 * parts]
    near_send, near_recv, leg_send, leg_recv, fwd_send, fwd_recv, own_sems = refs[3 * parts :]
    me = lax.axis_index("dom")
    grp = lax.axis_index("grp")
    row, col = me // SIDE, me % SIDE

    def at(offset):
        return ((row + offset[0]) % SIDE) * SIDE + (col + offset[1]) % SIDE

    def remote(src, dst, send_sem, recv_sem, offset):
        return pltpu.make_async_remote_copy(
            src_ref=src, dst_ref=dst, send_sem=send_sem, recv_sem=recv_sem,
            device_id=(at(offset), grp), device_id_type=pl.DeviceIdType.MESH,
        )

    barrier = pltpu.get_barrier_semaphore()
    for offset in NEAR:
        pl.semaphore_signal(
            barrier, inc=1, device_id=(at(offset), grp), device_id_type=pl.DeviceIdType.MESH
        )
    pl.semaphore_wait(barrier, len(NEAR))
    owns = []
    for p in range(parts):
        own = pltpu.make_async_copy(send_refs[p].at[me], recv_refs[p].at[me], own_sems.at[p])
        own.start()
        owns.append(own)
    legs = []
    for k, (target, relay, part) in enumerate(RELAYED):
        for p in range(parts):
            half = send_refs[p].shape[1] // 2
            leg = remote(send_refs[p].at[at(target), pl.ds(part * half, half)], relay_refs[p].at[k],
                         leg_send.at[p, k], leg_recv.at[p, k], relay)
            leg.start()
            legs.append(leg)
    nears = []
    for k, offset in enumerate(NEAR):
        for p in range(parts):
            near = remote(send_refs[p].at[at(offset)], recv_refs[p].at[me],
                          near_send.at[p, k], near_recv.at[p, k], offset)
            near.start()
            nears.append(near)
    fwds = []
    for k, (target, relay, part) in enumerate(RELAYED):
        source = at(((SIDE - relay[0]) % SIDE, (SIDE - relay[1]) % SIDE))
        onward = ((target[0] - relay[0]) % SIDE, (target[1] - relay[1]) % SIDE)
        for p in range(parts):
            half = send_refs[p].shape[1] // 2
            legs[k * parts + p].wait_recv()
            fwd = remote(relay_refs[p].at[k], recv_refs[p].at[source, pl.ds(part * half, half)],
                         fwd_send.at[p, k], fwd_recv.at[p, k], onward)
            fwd.start()
            fwds.append(fwd)
    for leg in legs:
        leg.wait_send()
    for near in nears:
        near.wait_send()
    for near in nears:
        near.wait_recv()
    for fwd in fwds:
        fwd.wait_send()
    for fwd in fwds:
        fwd.wait_recv()
    for own in owns:
        own.wait()


def dom_exchange(values, collective):
    parts = len(values)
    outs = [jax.ShapeDtypeStruct(v.shape, v.dtype) for v in values]
    relays = [jax.ShapeDtypeStruct((len(RELAYED), v.shape[1] // 2, v.shape[2]), v.dtype) for v in values]
    any_spec = pl.BlockSpec(memory_space=pl.ANY)
    result = pl.pallas_call(
        exchange_kernel,
        out_shape=tuple(outs + relays),
        in_specs=[any_spec] * parts,
        out_specs=tuple([any_spec] * (2 * parts)),
        scratch_shapes=[
            pltpu.SemaphoreType.DMA((parts, len(NEAR))),
            pltpu.SemaphoreType.DMA((parts, len(NEAR))),
            pltpu.SemaphoreType.DMA((parts, len(RELAYED))),
            pltpu.SemaphoreType.DMA((parts, len(RELAYED))),
            pltpu.SemaphoreType.DMA((parts, len(RELAYED))),
            pltpu.SemaphoreType.DMA((parts, len(RELAYED))),
            pltpu.SemaphoreType.DMA((parts,)),
        ],
        compiler_params=pltpu.CompilerParams(collective_id=collective, has_side_effects=True),
    )(*values)
    return result[:parts]


def finish_kernel(targets_ref, product_ref, state_ref, out_ref, acc_ref):
    vecs = out_ref.shape[2]
    acc_ref[...] = product_ref[...]

    def subtract(q, carry):
        state = state_ref[q]
        contrib = lax.dot_general(
            state[:, vecs:], state[:, :vecs], (((0,), (0,)), ((), ())),
            preferred_element_type=jnp.float32,
        ).astype(jnp.bfloat16)
        target = targets_ref[q]
        acc_ref[target] = acc_ref[target] - contrib.astype(jnp.float32)
        return carry

    lax.fori_loop(0, state_ref.shape[0], subtract, 0)
    out_ref[...] = acc_ref[...].astype(out_ref.dtype)


def finish(product, state_in, targets):
    vmem = pl.BlockSpec(memory_space=pltpu.VMEM)
    smem = pl.BlockSpec(memory_space=pltpu.SMEM)
    return pl.pallas_call(
        finish_kernel,
        out_shape=jax.ShapeDtypeStruct(product.shape, jnp.bfloat16),
        in_specs=[smem, vmem, vmem],
        out_specs=vmem,
        scratch_shapes=[pltpu.VMEM(product.shape, jnp.float32)],
    )(targets, product, state_in)


def well_states_of(summed, well_inverse, well_count):
    wells = summed.shape[0]
    live_mask = (jnp.arange(wells) < well_count[0]).astype(jnp.float32)
    solved = jnp.einsum("wst,wtv->wsv", well_inverse, summed, precision=lax.Precision.HIGHEST)
    return (solved * live_mask[:, None, None]).astype(jnp.bfloat16)


def subtract_incoming(product, well_send, incoming):
    targets = well_send[0].reshape(-1)
    selector = (targets[None, :] == jnp.arange(product.shape[0])[:, None]).astype(jnp.bfloat16)
    flat_rows = incoming.reshape(targets.shape[0], product.shape[1], product.shape[2])
    return product - jnp.einsum(
        "bq,qkv->bkv", selector, flat_rows, preferred_element_type=jnp.float32
    )


def on_device(
    blocks,
    tile_values,
    tile_cols,
    halo_send,
    halo_counts,
    grp_send,
    well_send,
    well_slot,
    well_count,
    couple_in,
    couple_out,
    well_inverse,
):
    dom_count = lax.axis_size("dom")
    halo_width = halo_send.shape[2]
    rim_width = grp_send.shape[2]
    slot_width = well_send.shape[2]
    cell_count = blocks.shape[1]
    vec_count = blocks.shape[2]
    wells, couplings = well_slot.shape
    seg = couple_in.shape[2]
    slot_total = dom_count * slot_width
    halo_pack = blocks[halo_send[0]]
    rim_pack = blocks[grp_send[0].reshape(-1)]
    rim_ext = padded(rim_pack, (("grp", 0),), rim_width)
    rim_rows = jnp.concatenate([rim_ext[:rim_width], rim_ext[rim_ext.shape[0] - rim_width :]], 0)
    slot_order = jnp.argsort(well_slot.reshape(-1))
    slot_well = slot_order // couplings
    in_slots = couple_in.reshape(wells * couplings, seg, cell_count)[slot_order]
    in_slots = in_slots.reshape(dom_count, slot_width * seg * cell_count // vec_count, vec_count)
    halo_flat = halo_pack.reshape(dom_count, halo_width * cell_count, vec_count)
    halo_recv, in_recv = dom_exchange([halo_flat, in_slots], 0)
    halo_rows = halo_recv.reshape(dom_count, halo_width, cell_count, vec_count)
    in_recv = in_recv.reshape(dom_count, slot_width, seg, cell_count)
    well_pack = blocks[well_send[0]]
    partial = jnp.einsum("qcsk,qckv->qcsv", in_recv, well_pack, preferred_element_type=jnp.float32)
    partial_in = lax.all_to_all(partial, "dom", split_axis=0, concat_axis=0, tiled=True)
    partial_in = partial_in.reshape(slot_total, seg, vec_count)
    summed = jnp.sum(partial_in[well_slot.reshape(-1)].reshape(wells, couplings, seg, vec_count), axis=1)
    well_state = well_states_of(summed, well_inverse, well_count)
    state_slots = well_state[slot_well]
    out_slots = couple_out.reshape(wells * couplings, seg, cell_count)[slot_order]
    state_pack = jnp.concatenate([state_slots, out_slots], 2)
    state_pack = state_pack.reshape(dom_count, slot_width, seg, vec_count + cell_count)
    state_in = lax.all_to_all(state_pack, "dom", split_axis=0, concat_axis=0, tiled=True)
    state_in = state_in.reshape(slot_total, seg, vec_count + cell_count)
    live_halo = jnp.arange(halo_width)[None, :] < halo_counts[0][:, None]
    halo_rows = jnp.where(live_halo[:, :, None, None], halo_rows, jnp.zeros_like(halo_rows))
    extended = jnp.concatenate(
        [blocks, halo_rows.reshape(dom_count * halo_width, cell_count, vec_count), rim_rows], 0
    )
    product = local_product(extended, tile_values, tile_cols)
    return finish(product, state_in, well_send[0].reshape(-1))


def solution(mesh):
    in_specs = (
        P(("dom", "grp"), None, None),
        P(("dom", "grp"), None, None, None),
        P(("dom", "grp"), None),
        P(("dom", "grp"), None, None),
        P(("dom", "grp"), None),
        P(("dom", "grp"), None, None),
        P(("dom", "grp"), None, None),
        P(("dom", "grp"), None),
        P(("dom", "grp")),
        P(("dom", "grp"), None, None, None),
        P(("dom", "grp"), None, None, None),
        P(("dom", "grp"), None, None),
    )
    out_specs = P(("dom", "grp"), None, None)
    return jax.shard_map(
        on_device, mesh=mesh, in_specs=in_specs, out_specs=out_specs, check_vma=False
    )
```

```python
import jax
import jax.numpy as jnp
from jax import lax
from jax.sharding import PartitionSpec as P
from jax.experimental import pallas as pl
from jax.experimental.pallas import tpu as pltpu


def padded(value, sides, width):
    for axis, dim in sides:
        devices, length = (lax.axis_size(axis), value.shape[dim])
        up = [(i, (i + 1) % devices) for i in range(devices - 1)]
        down = [(j, i) for i, j in up]
        last = lax.slice_in_dim(value, length - width, length, axis=dim)
        leading = lax.slice_in_dim(value, 0, width, axis=dim)
        before = lax.ppermute(last, axis, up)
        after = lax.ppermute(leading, axis, down)
        value = jnp.concatenate([before, value, after], axis=dim)
    return value


def product_kernel(cols_ref, ext_ref, tiles_ref, out_ref):
    rows, tiles_per_row = tiles_ref.shape[0], tiles_ref.shape[1]
    first = pl.program_id(0) * rows
    for r in range(rows):
        acc = jnp.zeros(out_ref.shape[1:], jnp.float32)
        for t in range(tiles_per_row):
            col = cols_ref[(first + r) * tiles_per_row + t]
            acc = acc + jnp.dot(tiles_ref[r, t], ext_ref[col], preferred_element_type=jnp.float32)
        out_ref[r] = acc


def local_product(extended, tile_values, tile_cols):
    block_rows, tiles_per_row, cells, _ = tile_values.shape
    ext_blocks, _, vecs = extended.shape
    rows = 4
    grid_spec = pltpu.PrefetchScalarGridSpec(
        num_scalar_prefetch=1,
        grid=(block_rows // rows,),
        in_specs=[
            pl.BlockSpec((ext_blocks, cells, vecs), lambda k, cols: (0, 0, 0)),
            pl.BlockSpec((rows, tiles_per_row, cells, cells), lambda k, cols: (k, 0, 0, 0)),
        ],
        out_specs=pl.BlockSpec((rows, cells, vecs), lambda k, cols: (k, 0, 0)),
    )
    flops = 2 * block_rows * tiles_per_row * cells * cells * vecs
    moved = tile_values.size * 2 + extended.size * 2 + block_rows * cells * vecs * 4
    return pl.pallas_call(
        product_kernel,
        out_shape=jax.ShapeDtypeStruct((block_rows, cells, vecs), jnp.float32),
        grid_spec=grid_spec,
        cost_estimate=pl.CostEstimate(flops=flops, transcendentals=0, bytes_accessed=moved),
    )(tile_cols.reshape(-1), extended, tile_values)


SIDE = 4
NEAR = ((1, 0), (3, 0), (0, 1), (0, 3), (1, 1), (1, 3), (3, 1), (3, 3))
RELAYED = (
    ((2, 0), (1, 0), 0), ((2, 0), (3, 0), 1),
    ((2, 1), (1, 0), 0), ((2, 1), (3, 0), 1),
    ((2, 3), (1, 0), 0), ((2, 3), (3, 0), 1),
    ((0, 2), (0, 1), 0), ((0, 2), (0, 3), 1),
    ((1, 2), (0, 1), 0), ((1, 2), (0, 3), 1),
    ((3, 2), (0, 1), 0), ((3, 2), (0, 3), 1),
    ((2, 2), (1, 1), 0), ((2, 2), (3, 3), 1),
)


def exchange_kernel(*refs):
    parts = (len(refs) - 7) // 3
    send_refs, recv_refs, relay_refs = refs[:parts], refs[parts : 2 * parts], refs[2 * parts : 3 * parts]
    near_send, near_recv, leg_send, leg_recv, fwd_send, fwd_recv, own_sems = refs[3 * parts :]
    me = lax.axis_index("dom")
    grp = lax.axis_index("grp")
    row, col = me // SIDE, me % SIDE

    def at(offset):
        return ((row + offset[0]) % SIDE) * SIDE + (col + offset[1]) % SIDE

    def remote(src, dst, send_sem, recv_sem, offset):
        return pltpu.make_async_remote_copy(
            src_ref=src, dst_ref=dst, send_sem=send_sem, recv_sem=recv_sem,
            device_id=(at(offset), grp), device_id_type=pl.DeviceIdType.MESH,
        )

    barrier = pltpu.get_barrier_semaphore()
    for offset in NEAR:
        pl.semaphore_signal(
            barrier, inc=1, device_id=(at(offset), grp), device_id_type=pl.DeviceIdType.MESH
        )
    pl.semaphore_wait(barrier, len(NEAR))
    owns = []
    for p in range(parts):
        own = pltpu.make_async_copy(send_refs[p].at[me], recv_refs[p].at[me], own_sems.at[p])
        own.start()
        owns.append(own)
    legs = []
    for k, (target, relay, part) in enumerate(RELAYED):
        for p in range(parts):
            half = send_refs[p].shape[1] // 2
            leg = remote(send_refs[p].at[at(target), pl.ds(part * half, half)], relay_refs[p].at[k],
                         leg_send.at[p, k], leg_recv.at[p, k], relay)
            leg.start()
            legs.append(leg)
    nears = []
    for k, offset in enumerate(NEAR):
        for p in range(parts):
            near = remote(send_refs[p].at[at(offset)], recv_refs[p].at[me],
                          near_send.at[p, k], near_recv.at[p, k], offset)
            near.start()
            nears.append(near)
    fwds = []
    for k, (target, relay, part) in enumerate(RELAYED):
        source = at(((SIDE - relay[0]) % SIDE, (SIDE - relay[1]) % SIDE))
        onward = ((target[0] - relay[0]) % SIDE, (target[1] - relay[1]) % SIDE)
        for p in range(parts):
            half = send_refs[p].shape[1] // 2
            legs[k * parts + p].wait_recv()
            fwd = remote(relay_refs[p].at[k], recv_refs[p].at[source, pl.ds(part * half, half)],
                         fwd_send.at[p, k], fwd_recv.at[p, k], onward)
            fwd.start()
            fwds.append(fwd)
    for leg in legs:
        leg.wait_send()
    for near in nears:
        near.wait_send()
    for near in nears:
        near.wait_recv()
    for fwd in fwds:
        fwd.wait_send()
    for fwd in fwds:
        fwd.wait_recv()
    for own in owns:
        own.wait()


def dom_exchange(values, collective):
    parts = len(values)
    outs = [jax.ShapeDtypeStruct(v.shape, v.dtype) for v in values]
    relays = [jax.ShapeDtypeStruct((len(RELAYED), v.shape[1] // 2, v.shape[2]), v.dtype) for v in values]
    any_spec = pl.BlockSpec(memory_space=pl.ANY)
    result = pl.pallas_call(
        exchange_kernel,
        out_shape=tuple(outs + relays),
        in_specs=[any_spec] * parts,
        out_specs=tuple([any_spec] * (2 * parts)),
        scratch_shapes=[
            pltpu.SemaphoreType.DMA((parts, len(NEAR))),
            pltpu.SemaphoreType.DMA((parts, len(NEAR))),
            pltpu.SemaphoreType.DMA((parts, len(RELAYED))),
            pltpu.SemaphoreType.DMA((parts, len(RELAYED))),
            pltpu.SemaphoreType.DMA((parts, len(RELAYED))),
            pltpu.SemaphoreType.DMA((parts, len(RELAYED))),
            pltpu.SemaphoreType.DMA((parts,)),
        ],
        compiler_params=pltpu.CompilerParams(collective_id=collective, has_side_effects=True),
    )(*values)
    return result[:parts]


def well_states_of(summed, well_inverse, well_count):
    wells = summed.shape[0]
    live_mask = (jnp.arange(wells) < well_count[0]).astype(jnp.float32)
    solved = jnp.einsum("wst,wtv->wsv", well_inverse, summed, precision=lax.Precision.HIGHEST)
    return (solved * live_mask[:, None, None]).astype(jnp.bfloat16)


def subtract_incoming(product, well_send, incoming):
    targets = well_send[0].reshape(-1)
    selector = (targets[None, :] == jnp.arange(product.shape[0])[:, None]).astype(jnp.bfloat16)
    flat_rows = incoming.reshape(targets.shape[0], product.shape[1], product.shape[2])
    return product - jnp.einsum(
        "bq,qkv->bkv", selector, flat_rows, preferred_element_type=jnp.float32
    )


def on_device(
    blocks,
    tile_values,
    tile_cols,
    halo_send,
    halo_counts,
    grp_send,
    well_send,
    well_slot,
    well_count,
    couple_in,
    couple_out,
    well_inverse,
):
    dom_count = lax.axis_size("dom")
    halo_width = halo_send.shape[2]
    rim_width = grp_send.shape[2]
    slot_width = well_send.shape[2]
    cell_count = blocks.shape[1]
    vec_count = blocks.shape[2]
    wells, couplings = well_slot.shape
    seg = couple_in.shape[2]
    slot_total = dom_count * slot_width
    halo_pack = blocks[halo_send[0]]
    rim_pack = blocks[grp_send[0].reshape(-1)]
    rim_ext = padded(rim_pack, (("grp", 0),), rim_width)
    rim_rows = jnp.concatenate([rim_ext[:rim_width], rim_ext[rim_ext.shape[0] - rim_width :]], 0)
    slot_order = jnp.argsort(well_slot.reshape(-1))
    slot_well = slot_order // couplings
    in_slots = couple_in.reshape(wells * couplings, seg, cell_count)[slot_order]
    in_slots = in_slots.reshape(dom_count, slot_width * seg * cell_count // vec_count, vec_count)
    halo_flat = halo_pack.reshape(dom_count, halo_width * cell_count, vec_count)
    (in_recv,) = dom_exchange([in_slots], 0)
    in_recv = in_recv.reshape(dom_count, slot_width, seg, cell_count)
    well_pack = blocks[well_send[0]]
    partial = jnp.einsum("qcsk,qckv->qcsv", in_recv, well_pack, preferred_element_type=jnp.float32)
    partial_in = lax.all_to_all(partial, "dom", split_axis=0, concat_axis=0, tiled=True)
    (halo_recv,) = dom_exchange([halo_flat], 1)
    partial_in = partial_in.reshape(slot_total, seg, vec_count)
    summed = jnp.sum(partial_in[well_slot.reshape(-1)].reshape(wells, couplings, seg, vec_count), axis=1)
    well_state = well_states_of(summed, well_inverse, well_count)
    state_slots = well_state[slot_well]
    out_slots = couple_out.reshape(wells * couplings, seg, cell_count)[slot_order]
    state_pack = jnp.concatenate([state_slots, out_slots], 2)
    state_pack = state_pack.reshape(dom_count, slot_width, seg, vec_count + cell_count)
    state_in = lax.all_to_all(state_pack, "dom", split_axis=0, concat_axis=0, tiled=True)
    state_in = state_in.reshape(slot_total, seg, vec_count + cell_count)
    halo_rows = halo_recv.reshape(dom_count, halo_width, cell_count, vec_count)
    live_halo = jnp.arange(halo_width)[None, :] < halo_counts[0][:, None]
    halo_rows = jnp.where(live_halo[:, :, None, None], halo_rows, jnp.zeros_like(halo_rows))
    extended = jnp.concatenate(
        [blocks, halo_rows.reshape(dom_count * halo_width, cell_count, vec_count), rim_rows], 0
    )
    product = local_product(extended, tile_values, tile_cols)
    incoming = jnp.einsum(
        "qsk,qsv->qkv",
        state_in[:, :, vec_count:],
        state_in[:, :, :vec_count],
        preferred_element_type=jnp.float32,
    ).astype(jnp.bfloat16)
    return subtract_incoming(product, well_send, incoming).astype(jnp.bfloat16)


def solution(mesh):
    in_specs = (
        P(("dom", "grp"), None, None),
        P(("dom", "grp"), None, None, None),
        P(("dom", "grp"), None),
        P(("dom", "grp"), None, None),
        P(("dom", "grp"), None),
        P(("dom", "grp"), None, None),
        P(("dom", "grp"), None, None),
        P(("dom", "grp"), None),
        P(("dom", "grp")),
        P(("dom", "grp"), None, None, None),
        P(("dom", "grp"), None, None, None),
        P(("dom", "grp"), None, None),
    )
    out_specs = P(("dom", "grp"), None, None)
    return jax.shard_map(
        on_device, mesh=mesh, in_specs=in_specs, out_specs=out_specs, check_vma=False
    )
```

```python
import jax
import jax.numpy as jnp
from jax import lax
from jax.sharding import PartitionSpec as P
from jax.experimental import pallas as pl
from jax.experimental.pallas import tpu as pltpu


def padded(value, sides, width):
    for axis, dim in sides:
        devices, length = (lax.axis_size(axis), value.shape[dim])
        up = [(i, (i + 1) % devices) for i in range(devices - 1)]
        down = [(j, i) for i, j in up]
        last = lax.slice_in_dim(value, length - width, length, axis=dim)
        leading = lax.slice_in_dim(value, 0, width, axis=dim)
        before = lax.ppermute(last, axis, up)
        after = lax.ppermute(leading, axis, down)
        value = jnp.concatenate([before, value, after], axis=dim)
    return value


def product_kernel(cols_ref, live_ref, ext_ref, tiles_ref, out_ref):
    rows, tiles_per_row = tiles_ref.shape[0], tiles_ref.shape[1]
    first = pl.program_id(0) * rows
    for r in range(rows):
        acc = jnp.zeros(out_ref.shape[1:], jnp.float32)
        for t in range(tiles_per_row):
            col = cols_ref[(first + r) * tiles_per_row + t]
            scale = live_ref[col].astype(jnp.float32)
            acc = acc + scale * jnp.dot(tiles_ref[r, t], ext_ref[col], preferred_element_type=jnp.float32)
        out_ref[r] = acc


def local_product(extended, live, tile_values, tile_cols):
    block_rows, tiles_per_row, cells, _ = tile_values.shape
    ext_blocks, _, vecs = extended.shape
    rows = 4
    grid_spec = pltpu.PrefetchScalarGridSpec(
        num_scalar_prefetch=2,
        grid=(block_rows // rows,),
        in_specs=[
            pl.BlockSpec((ext_blocks, cells, vecs), lambda k, cols, live: (0, 0, 0)),
            pl.BlockSpec((rows, tiles_per_row, cells, cells), lambda k, cols, live: (k, 0, 0, 0)),
        ],
        out_specs=pl.BlockSpec((rows, cells, vecs), lambda k, cols, live: (k, 0, 0)),
    )
    flops = 2 * block_rows * tiles_per_row * cells * cells * vecs
    moved = tile_values.size * 2 + extended.size * 2 + block_rows * cells * vecs * 4
    return pl.pallas_call(
        product_kernel,
        out_shape=jax.ShapeDtypeStruct((block_rows, cells, vecs), jnp.float32),
        grid_spec=grid_spec,
        cost_estimate=pl.CostEstimate(flops=flops, transcendentals=0, bytes_accessed=moved),
    )(tile_cols.reshape(-1), live, extended, tile_values)


def partial_kernel(index_ref, couple_ref, blocks_ref, out_ref):
    for q in range(out_ref.shape[0]):
        out_ref[q] = jnp.dot(
            couple_ref[q], blocks_ref[index_ref[q]], preferred_element_type=jnp.float32
        )


def partial_sums(index, couple, blocks):
    slots, seg, _ = couple.shape
    vmem = pl.BlockSpec(memory_space=pltpu.VMEM)
    return pl.pallas_call(
        partial_kernel,
        out_shape=jax.ShapeDtypeStruct((slots, seg, blocks.shape[2]), jnp.float32),
        in_specs=[pl.BlockSpec(memory_space=pltpu.SMEM), vmem, vmem],
        out_specs=vmem,
    )(index, couple, blocks)


SIDE = 4
NEAR = ((1, 0), (3, 0), (0, 1), (0, 3), (1, 1), (1, 3), (3, 1), (3, 3))
RELAYED = (
    ((2, 0), (1, 0), 0), ((2, 0), (3, 0), 1),
    ((2, 1), (1, 0), 0), ((2, 1), (3, 0), 1),
    ((2, 3), (1, 0), 0), ((2, 3), (3, 0), 1),
    ((0, 2), (0, 1), 0), ((0, 2), (0, 3), 1),
    ((1, 2), (0, 1), 0), ((1, 2), (0, 3), 1),
    ((3, 2), (0, 1), 0), ((3, 2), (0, 3), 1),
    ((2, 2), (1, 1), 0), ((2, 2), (3, 3), 1),
)


def exchange_kernel(*refs):
    parts = (len(refs) - 7) // 3
    send_refs, recv_refs, relay_refs = refs[:parts], refs[parts : 2 * parts], refs[2 * parts : 3 * parts]
    near_send, near_recv, leg_send, leg_recv, fwd_send, fwd_recv, own_sems = refs[3 * parts :]
    me = lax.axis_index("dom")
    grp = lax.axis_index("grp")
    row, col = me // SIDE, me % SIDE

    def at(offset):
        return ((row + offset[0]) % SIDE) * SIDE + (col + offset[1]) % SIDE

    def remote(src, dst, send_sem, recv_sem, offset):
        return pltpu.make_async_remote_copy(
            src_ref=src, dst_ref=dst, send_sem=send_sem, recv_sem=recv_sem,
            device_id=(at(offset), grp), device_id_type=pl.DeviceIdType.MESH,
        )

    barrier = pltpu.get_barrier_semaphore()
    for offset in NEAR:
        pl.semaphore_signal(
            barrier, inc=1, device_id=(at(offset), grp), device_id_type=pl.DeviceIdType.MESH
        )
    pl.semaphore_wait(barrier, len(NEAR))
    owns = []
    for p in range(parts):
        own = pltpu.make_async_copy(send_refs[p].at[me], recv_refs[p].at[me], own_sems.at[p])
        own.start()
        owns.append(own)
    legs = []
    for k, (target, relay, part) in enumerate(RELAYED):
        for p in range(parts):
            half = send_refs[p].shape[1] // 2
            leg = remote(send_refs[p].at[at(target), pl.ds(part * half, half)], relay_refs[p].at[k],
                         leg_send.at[p, k], leg_recv.at[p, k], relay)
            leg.start()
            legs.append(leg)
    nears = []
    for k, offset in enumerate(NEAR):
        for p in range(parts):
            near = remote(send_refs[p].at[at(offset)], recv_refs[p].at[me],
                          near_send.at[p, k], near_recv.at[p, k], offset)
            near.start()
            nears.append(near)
    fwds = []
    for k, (target, relay, part) in enumerate(RELAYED):
        source = at(((SIDE - relay[0]) % SIDE, (SIDE - relay[1]) % SIDE))
        onward = ((target[0] - relay[0]) % SIDE, (target[1] - relay[1]) % SIDE)
        for p in range(parts):
            half = send_refs[p].shape[1] // 2
            legs[k * parts + p].wait_recv()
            fwd = remote(relay_refs[p].at[k], recv_refs[p].at[source, pl.ds(part * half, half)],
                         fwd_send.at[p, k], fwd_recv.at[p, k], onward)
            fwd.start()
            fwds.append(fwd)
    for leg in legs:
        leg.wait_send()
    for near in nears:
        near.wait_send()
    for near in nears:
        near.wait_recv()
    for fwd in fwds:
        fwd.wait_send()
    for fwd in fwds:
        fwd.wait_recv()
    for own in owns:
        own.wait()


def dom_exchange(values, collective):
    parts = len(values)
    outs = [jax.ShapeDtypeStruct(v.shape, v.dtype) for v in values]
    relays = [jax.ShapeDtypeStruct((len(RELAYED), v.shape[1] // 2, v.shape[2]), v.dtype) for v in values]
    any_spec = pl.BlockSpec(memory_space=pl.ANY)
    result = pl.pallas_call(
        exchange_kernel,
        out_shape=tuple(outs + relays),
        in_specs=[any_spec] * parts,
        out_specs=tuple([any_spec] * (2 * parts)),
        scratch_shapes=[
            pltpu.SemaphoreType.DMA((parts, len(NEAR))),
            pltpu.SemaphoreType.DMA((parts, len(NEAR))),
            pltpu.SemaphoreType.DMA((parts, len(RELAYED))),
            pltpu.SemaphoreType.DMA((parts, len(RELAYED))),
            pltpu.SemaphoreType.DMA((parts, len(RELAYED))),
            pltpu.SemaphoreType.DMA((parts, len(RELAYED))),
            pltpu.SemaphoreType.DMA((parts,)),
        ],
        compiler_params=pltpu.CompilerParams(collective_id=collective, has_side_effects=True),
    )(*values)
    return result[:parts]


def well_states_of(summed, well_inverse, well_count):
    wells = summed.shape[0]
    live_mask = (jnp.arange(wells) < well_count[0]).astype(jnp.float32)
    solved = jnp.einsum("wst,wtv->wsv", well_inverse, summed, precision=lax.Precision.HIGHEST)
    return (solved * live_mask[:, None, None]).astype(jnp.bfloat16)


def subtract_incoming(product, well_send, incoming):
    targets = well_send[0].reshape(-1)
    selector = (targets[None, :] == jnp.arange(product.shape[0])[:, None]).astype(jnp.bfloat16)
    flat_rows = incoming.reshape(targets.shape[0], product.shape[1], product.shape[2])
    return product - jnp.einsum(
        "bq,qkv->bkv", selector, flat_rows, preferred_element_type=jnp.float32
    )


def on_device(
    blocks,
    tile_values,
    tile_cols,
    halo_send,
    halo_counts,
    grp_send,
    well_send,
    well_slot,
    well_count,
    couple_in,
    couple_out,
    well_inverse,
):
    dom_count = lax.axis_size("dom")
    halo_width = halo_send.shape[2]
    rim_width = grp_send.shape[2]
    slot_width = well_send.shape[2]
    cell_count = blocks.shape[1]
    vec_count = blocks.shape[2]
    wells, couplings = well_slot.shape
    seg = couple_in.shape[2]
    slot_total = dom_count * slot_width
    halo_pack = blocks[halo_send[0]]
    rim_pack = blocks[grp_send[0].reshape(-1)]
    rim_ext = padded(rim_pack, (("grp", 0),), rim_width)
    rim_rows = jnp.concatenate([rim_ext[:rim_width], rim_ext[rim_ext.shape[0] - rim_width :]], 0)
    slot_order = jnp.argsort(well_slot.reshape(-1))
    slot_well = slot_order // couplings
    in_slots = couple_in.reshape(wells * couplings, seg, cell_count)[slot_order]
    in_slots = in_slots.reshape(dom_count, slot_width * seg * cell_count // vec_count, vec_count)
    halo_flat = halo_pack.reshape(dom_count, halo_width * cell_count, vec_count)
    (in_recv,) = dom_exchange([in_slots], 0)
    in_recv = in_recv.reshape(dom_count, slot_width, seg, cell_count)
    partial = partial_sums(
        well_send[0].reshape(-1), in_recv.reshape(slot_total, seg, cell_count), blocks
    ).reshape(dom_count, slot_width, seg, vec_count)
    partial_in = lax.all_to_all(partial, "dom", split_axis=0, concat_axis=0, tiled=True)
    (halo_recv,) = dom_exchange([halo_flat], 1)
    partial_in = partial_in.reshape(slot_total, seg, vec_count)
    summed = jnp.sum(partial_in[well_slot.reshape(-1)].reshape(wells, couplings, seg, vec_count), axis=1)
    well_state = well_states_of(summed, well_inverse, well_count)
    state_slots = well_state[slot_well]
    out_slots = couple_out.reshape(wells * couplings, seg, cell_count)[slot_order]
    state_pack = jnp.concatenate([state_slots, out_slots], 2)
    state_pack = state_pack.reshape(dom_count, slot_width, seg, vec_count + cell_count)
    state_in = lax.all_to_all(state_pack, "dom", split_axis=0, concat_axis=0, tiled=True)
    state_in = state_in.reshape(slot_total, seg, vec_count + cell_count)
    halo_rows = halo_recv.reshape(dom_count, halo_width, cell_count, vec_count)
    live_halo = (jnp.arange(halo_width)[None, :] < halo_counts[0][:, None]).astype(jnp.int32)
    live = jnp.concatenate(
        [jnp.ones((blocks.shape[0],), jnp.int32), live_halo.reshape(-1), jnp.ones((2 * rim_width,), jnp.int32)]
    )
    extended = jnp.concatenate(
        [blocks, halo_rows.reshape(dom_count * halo_width, cell_count, vec_count), rim_rows], 0
    )
    product = local_product(extended, live, tile_values, tile_cols)
    incoming = jnp.einsum(
        "qsk,qsv->qkv",
        state_in[:, :, vec_count:],
        state_in[:, :, :vec_count],
        preferred_element_type=jnp.float32,
    ).astype(jnp.bfloat16)
    return subtract_incoming(product, well_send, incoming).astype(jnp.bfloat16)


def solution(mesh):
    in_specs = (
        P(("dom", "grp"), None, None),
        P(("dom", "grp"), None, None, None),
        P(("dom", "grp"), None),
        P(("dom", "grp"), None, None),
        P(("dom", "grp"), None),
        P(("dom", "grp"), None, None),
        P(("dom", "grp"), None, None),
        P(("dom", "grp"), None),
        P(("dom", "grp")),
        P(("dom", "grp"), None, None, None),
        P(("dom", "grp"), None, None, None),
        P(("dom", "grp"), None, None),
    )
    out_specs = P(("dom", "grp"), None, None)
    return jax.shard_map(
        on_device, mesh=mesh, in_specs=in_specs, out_specs=out_specs, check_vma=False
    )
```

```python
import jax
import jax.numpy as jnp
from jax import lax
from jax.sharding import PartitionSpec as P
from jax.experimental import pallas as pl
from jax.experimental.pallas import tpu as pltpu


def padded(value, sides, width):
    for axis, dim in sides:
        devices, length = (lax.axis_size(axis), value.shape[dim])
        up = [(i, (i + 1) % devices) for i in range(devices - 1)]
        down = [(j, i) for i, j in up]
        last = lax.slice_in_dim(value, length - width, length, axis=dim)
        leading = lax.slice_in_dim(value, 0, width, axis=dim)
        before = lax.ppermute(last, axis, up)
        after = lax.ppermute(leading, axis, down)
        value = jnp.concatenate([before, value, after], axis=dim)
    return value


def product_kernel(cols_ref, live_ref, ext_ref, tiles_ref, out_ref):
    rows, tiles_per_row = tiles_ref.shape[0], tiles_ref.shape[1]
    first = pl.program_id(0) * rows
    for r in range(rows):
        acc = jnp.zeros(out_ref.shape[1:], jnp.float32)
        for t in range(tiles_per_row):
            col = cols_ref[(first + r) * tiles_per_row + t]
            scale = live_ref[col].astype(jnp.float32)
            acc = acc + scale * jnp.dot(tiles_ref[r, t], ext_ref[col], preferred_element_type=jnp.float32)
        out_ref[r] = acc


def local_product(extended, live, tile_values, tile_cols):
    block_rows, tiles_per_row, cells, _ = tile_values.shape
    ext_blocks, _, vecs = extended.shape
    rows = 4
    grid_spec = pltpu.PrefetchScalarGridSpec(
        num_scalar_prefetch=2,
        grid=(block_rows // rows,),
        in_specs=[
            pl.BlockSpec((ext_blocks, cells, vecs), lambda k, cols, live: (0, 0, 0)),
            pl.BlockSpec((rows, tiles_per_row, cells, cells), lambda k, cols, live: (k, 0, 0, 0)),
        ],
        out_specs=pl.BlockSpec((rows, cells, vecs), lambda k, cols, live: (k, 0, 0)),
    )
    flops = 2 * block_rows * tiles_per_row * cells * cells * vecs
    moved = tile_values.size * 2 + extended.size * 2 + block_rows * cells * vecs * 4
    return pl.pallas_call(
        product_kernel,
        out_shape=jax.ShapeDtypeStruct((block_rows, cells, vecs), jnp.float32),
        grid_spec=grid_spec,
        cost_estimate=pl.CostEstimate(flops=flops, transcendentals=0, bytes_accessed=moved),
    )(tile_cols.reshape(-1), live, extended, tile_values)


def sums_kernel(slot_ref, partial_ref, out_ref):
    couplings = slot_ref.shape[0] // out_ref.shape[0]
    for w in range(out_ref.shape[0]):
        acc = partial_ref[slot_ref[w * couplings]]
        for c in range(1, couplings):
            acc = acc + partial_ref[slot_ref[w * couplings + c]]
        out_ref[w] = acc


def well_sums(slots, partial, wells):
    vmem = pl.BlockSpec(memory_space=pltpu.VMEM)
    return pl.pallas_call(
        sums_kernel,
        out_shape=jax.ShapeDtypeStruct((wells,) + partial.shape[1:], jnp.float32),
        in_specs=[pl.BlockSpec(memory_space=pltpu.SMEM), vmem],
        out_specs=vmem,
    )(slots, partial)


def partial_kernel(index_ref, couple_ref, blocks_ref, out_ref):
    for q in range(out_ref.shape[0]):
        out_ref[q] = jnp.dot(
            couple_ref[q], blocks_ref[index_ref[q]], preferred_element_type=jnp.float32
        )


def partial_sums(index, couple, blocks):
    slots, seg, _ = couple.shape
    vmem = pl.BlockSpec(memory_space=pltpu.VMEM)
    return pl.pallas_call(
        partial_kernel,
        out_shape=jax.ShapeDtypeStruct((slots, seg, blocks.shape[2]), jnp.float32),
        in_specs=[pl.BlockSpec(memory_space=pltpu.SMEM), vmem, vmem],
        out_specs=vmem,
    )(index, couple, blocks)


SIDE = 4
NEAR = ((1, 0), (3, 0), (0, 1), (0, 3), (1, 1), (1, 3), (3, 1), (3, 3))
RELAYED = (
    ((2, 0), (1, 0), 0), ((2, 0), (3, 0), 1),
    ((2, 1), (1, 0), 0), ((2, 1), (3, 0), 1),
    ((2, 3), (1, 0), 0), ((2, 3), (3, 0), 1),
    ((0, 2), (0, 1), 0), ((0, 2), (0, 3), 1),
    ((1, 2), (0, 1), 0), ((1, 2), (0, 3), 1),
    ((3, 2), (0, 1), 0), ((3, 2), (0, 3), 1),
    ((2, 2), (1, 1), 0), ((2, 2), (3, 3), 1),
)


def exchange_kernel(*refs):
    parts = (len(refs) - 7) // 3
    send_refs, recv_refs, relay_refs = refs[:parts], refs[parts : 2 * parts], refs[2 * parts : 3 * parts]
    near_send, near_recv, leg_send, leg_recv, fwd_send, fwd_recv, own_sems = refs[3 * parts :]
    me = lax.axis_index("dom")
    grp = lax.axis_index("grp")
    row, col = me // SIDE, me % SIDE

    def at(offset):
        return ((row + offset[0]) % SIDE) * SIDE + (col + offset[1]) % SIDE

    def remote(src, dst, send_sem, recv_sem, offset):
        return pltpu.make_async_remote_copy(
            src_ref=src, dst_ref=dst, send_sem=send_sem, recv_sem=recv_sem,
            device_id=(at(offset), grp), device_id_type=pl.DeviceIdType.MESH,
        )

    barrier = pltpu.get_barrier_semaphore()
    for offset in NEAR:
        pl.semaphore_signal(
            barrier, inc=1, device_id=(at(offset), grp), device_id_type=pl.DeviceIdType.MESH
        )
    pl.semaphore_wait(barrier, len(NEAR))
    owns = []
    for p in range(parts):
        own = pltpu.make_async_copy(send_refs[p].at[me], recv_refs[p].at[me], own_sems.at[p])
        own.start()
        owns.append(own)
    legs = []
    for k, (target, relay, part) in enumerate(RELAYED):
        for p in range(parts):
            half = send_refs[p].shape[1] // 2
            leg = remote(send_refs[p].at[at(target), pl.ds(part * half, half)], relay_refs[p].at[k],
                         leg_send.at[p, k], leg_recv.at[p, k], relay)
            leg.start()
            legs.append(leg)
    nears = []
    for k, offset in enumerate(NEAR):
        for p in range(parts):
            near = remote(send_refs[p].at[at(offset)], recv_refs[p].at[me],
                          near_send.at[p, k], near_recv.at[p, k], offset)
            near.start()
            nears.append(near)
    fwds = []
    for k, (target, relay, part) in enumerate(RELAYED):
        source = at(((SIDE - relay[0]) % SIDE, (SIDE - relay[1]) % SIDE))
        onward = ((target[0] - relay[0]) % SIDE, (target[1] - relay[1]) % SIDE)
        for p in range(parts):
            half = send_refs[p].shape[1] // 2
            legs[k * parts + p].wait_recv()
            fwd = remote(relay_refs[p].at[k], recv_refs[p].at[source, pl.ds(part * half, half)],
                         fwd_send.at[p, k], fwd_recv.at[p, k], onward)
            fwd.start()
            fwds.append(fwd)
    for leg in legs:
        leg.wait_send()
    for near in nears:
        near.wait_send()
    for near in nears:
        near.wait_recv()
    for fwd in fwds:
        fwd.wait_send()
    for fwd in fwds:
        fwd.wait_recv()
    for own in owns:
        own.wait()


def dom_exchange(values, collective):
    parts = len(values)
    outs = [jax.ShapeDtypeStruct(v.shape, v.dtype) for v in values]
    relays = [jax.ShapeDtypeStruct((len(RELAYED), v.shape[1] // 2, v.shape[2]), v.dtype) for v in values]
    any_spec = pl.BlockSpec(memory_space=pl.ANY)
    result = pl.pallas_call(
        exchange_kernel,
        out_shape=tuple(outs + relays),
        in_specs=[any_spec] * parts,
        out_specs=tuple([any_spec] * (2 * parts)),
        scratch_shapes=[
            pltpu.SemaphoreType.DMA((parts, len(NEAR))),
            pltpu.SemaphoreType.DMA((parts, len(NEAR))),
            pltpu.SemaphoreType.DMA((parts, len(RELAYED))),
            pltpu.SemaphoreType.DMA((parts, len(RELAYED))),
            pltpu.SemaphoreType.DMA((parts, len(RELAYED))),
            pltpu.SemaphoreType.DMA((parts, len(RELAYED))),
            pltpu.SemaphoreType.DMA((parts,)),
        ],
        compiler_params=pltpu.CompilerParams(collective_id=collective, has_side_effects=True),
    )(*values)
    return result[:parts]


def well_states_of(summed, well_inverse, well_count):
    wells = summed.shape[0]
    live_mask = (jnp.arange(wells) < well_count[0]).astype(jnp.float32)
    solved = jnp.einsum("wst,wtv->wsv", well_inverse, summed, precision=lax.Precision.HIGHEST)
    return (solved * live_mask[:, None, None]).astype(jnp.bfloat16)


def subtract_incoming(product, well_send, incoming):
    targets = well_send[0].reshape(-1)
    selector = (targets[None, :] == jnp.arange(product.shape[0])[:, None]).astype(jnp.bfloat16)
    flat_rows = incoming.reshape(targets.shape[0], product.shape[1], product.shape[2])
    return product - jnp.einsum(
        "bq,qkv->bkv", selector, flat_rows, preferred_element_type=jnp.float32
    )


def on_device(
    blocks,
    tile_values,
    tile_cols,
    halo_send,
    halo_counts,
    grp_send,
    well_send,
    well_slot,
    well_count,
    couple_in,
    couple_out,
    well_inverse,
):
    dom_count = lax.axis_size("dom")
    halo_width = halo_send.shape[2]
    rim_width = grp_send.shape[2]
    slot_width = well_send.shape[2]
    cell_count = blocks.shape[1]
    vec_count = blocks.shape[2]
    wells, couplings = well_slot.shape
    seg = couple_in.shape[2]
    slot_total = dom_count * slot_width
    halo_pack = blocks[halo_send[0]]
    rim_pack = blocks[grp_send[0].reshape(-1)]
    rim_ext = padded(rim_pack, (("grp", 0),), rim_width)
    rim_rows = jnp.concatenate([rim_ext[:rim_width], rim_ext[rim_ext.shape[0] - rim_width :]], 0)
    slot_order = jnp.argsort(well_slot.reshape(-1))
    slot_well = slot_order // couplings
    in_slots = couple_in.reshape(wells * couplings, seg, cell_count)[slot_order]
    in_slots = in_slots.reshape(dom_count, slot_width * seg, cell_count)
    halo_flat = halo_pack.reshape(dom_count, halo_width * cell_count, vec_count)
    (in_recv,) = dom_exchange([in_slots], 0)
    in_recv = in_recv.reshape(dom_count, slot_width, seg, cell_count)
    partial = partial_sums(
        well_send[0].reshape(-1), in_recv.reshape(slot_total, seg, cell_count), blocks
    ).reshape(dom_count, slot_width, seg, vec_count)
    partial_in = lax.all_to_all(partial, "dom", split_axis=0, concat_axis=0, tiled=True)
    (halo_recv,) = dom_exchange([halo_flat], 1)
    partial_in = partial_in.reshape(slot_total, seg, vec_count)
    summed = well_sums(well_slot.reshape(-1), partial_in, wells)
    well_state = well_states_of(summed, well_inverse, well_count)
    state_slots = well_state[slot_well]
    out_slots = couple_out.reshape(wells * couplings, seg, cell_count)[slot_order]
    state_pack = jnp.concatenate([state_slots, out_slots], 2)
    state_pack = state_pack.reshape(dom_count, slot_width, seg, vec_count + cell_count)
    state_in = lax.all_to_all(state_pack, "dom", split_axis=0, concat_axis=0, tiled=True)
    state_in = state_in.reshape(slot_total, seg, vec_count + cell_count)
    halo_rows = halo_recv.reshape(dom_count, halo_width, cell_count, vec_count)
    live_halo = (jnp.arange(halo_width)[None, :] < halo_counts[0][:, None]).astype(jnp.int32)
    live = jnp.concatenate(
        [jnp.ones((blocks.shape[0],), jnp.int32), live_halo.reshape(-1), jnp.ones((2 * rim_width,), jnp.int32)]
    )
    extended = jnp.concatenate(
        [blocks, halo_rows.reshape(dom_count * halo_width, cell_count, vec_count), rim_rows], 0
    )
    product = local_product(extended, live, tile_values, tile_cols)
    incoming = jnp.einsum(
        "qsk,qsv->qkv",
        state_in[:, :, vec_count:],
        state_in[:, :, :vec_count],
        preferred_element_type=jnp.float32,
    ).astype(jnp.bfloat16)
    return subtract_incoming(product, well_send, incoming).astype(jnp.bfloat16)


def solution(mesh):
    in_specs = (
        P(("dom", "grp"), None, None),
        P(("dom", "grp"), None, None, None),
        P(("dom", "grp"), None),
        P(("dom", "grp"), None, None),
        P(("dom", "grp"), None),
        P(("dom", "grp"), None, None),
        P(("dom", "grp"), None, None),
        P(("dom", "grp"), None),
        P(("dom", "grp")),
        P(("dom", "grp"), None, None, None),
        P(("dom", "grp"), None, None, None),
        P(("dom", "grp"), None, None),
    )
    out_specs = P(("dom", "grp"), None, None)
    return jax.shard_map(
        on_device, mesh=mesh, in_specs=in_specs, out_specs=out_specs, check_vma=False
    )
```

```python
import functools

import jax
import jax.numpy as jnp
from jax import lax
from jax.sharding import PartitionSpec as P
from jax.experimental import pallas as pl
from jax.experimental.pallas import tpu as pltpu


def padded(value, sides, width):
    for axis, dim in sides:
        devices, length = (lax.axis_size(axis), value.shape[dim])
        up = [(i, (i + 1) % devices) for i in range(devices - 1)]
        down = [(j, i) for i, j in up]
        last = lax.slice_in_dim(value, length - width, length, axis=dim)
        leading = lax.slice_in_dim(value, 0, width, axis=dim)
        before = lax.ppermute(last, axis, up)
        after = lax.ppermute(leading, axis, down)
        value = jnp.concatenate([before, value, after], axis=dim)
    return value


def product_kernel(cols_ref, live_ref, ext_ref, tiles_ref, out_ref):
    rows, tiles_per_row = tiles_ref.shape[0], tiles_ref.shape[1]
    first = pl.program_id(0) * rows
    for r in range(rows):
        acc = None
        for t in range(0, tiles_per_row, 2):
            pair = [cols_ref[(first + r) * tiles_per_row + t + u] for u in range(2)]
            lhs = jnp.concatenate(
                [tiles_ref[r, t + u] * live_ref[pair[u]].astype(tiles_ref.dtype) for u in range(2)], axis=1
            )
            rhs = jnp.concatenate([ext_ref[c] for c in pair], axis=0)
            term = jnp.dot(lhs, rhs, preferred_element_type=jnp.float32)
            acc = term if acc is None else acc + term
        out_ref[r] = acc


def local_product(extended, live, tile_values, tile_cols):
    block_rows, tiles_per_row, cells, _ = tile_values.shape
    ext_blocks, _, vecs = extended.shape
    rows = 16
    grid_spec = pltpu.PrefetchScalarGridSpec(
        num_scalar_prefetch=2,
        grid=(block_rows // rows,),
        in_specs=[
            pl.BlockSpec((ext_blocks, cells, vecs), lambda k, cols, live: (0, 0, 0)),
            pl.BlockSpec((rows, tiles_per_row, cells, cells), lambda k, cols, live: (k, 0, 0, 0)),
        ],
        out_specs=pl.BlockSpec((rows, cells, vecs), lambda k, cols, live: (k, 0, 0)),
    )
    flops = 2 * block_rows * tiles_per_row * cells * cells * vecs
    moved = tile_values.size * 2 + extended.size * 2 + block_rows * cells * vecs * 4
    return pl.pallas_call(
        product_kernel,
        out_shape=jax.ShapeDtypeStruct((block_rows, cells, vecs), jnp.float32),
        grid_spec=grid_spec,
        cost_estimate=pl.CostEstimate(flops=flops, transcendentals=0, bytes_accessed=moved),
    )(tile_cols.reshape(-1), live, extended, tile_values)


def sums_kernel(slot_ref, partial_ref, out_ref):
    couplings = slot_ref.shape[0] // out_ref.shape[0]
    for w in range(out_ref.shape[0]):
        acc = partial_ref[slot_ref[w * couplings]]
        for c in range(1, couplings):
            acc = acc + partial_ref[slot_ref[w * couplings + c]]
        out_ref[w] = acc


def well_sums(slots, partial, wells):
    vmem = pl.BlockSpec(memory_space=pltpu.VMEM)
    return pl.pallas_call(
        sums_kernel,
        out_shape=jax.ShapeDtypeStruct((wells,) + partial.shape[1:], jnp.float32),
        in_specs=[pl.BlockSpec(memory_space=pltpu.SMEM), vmem],
        out_specs=vmem,
    )(slots, partial)


def partial_kernel(index_ref, couple_ref, blocks_ref, out_ref):
    for q in range(out_ref.shape[0]):
        out_ref[q] = jnp.dot(
            couple_ref[q], blocks_ref[index_ref[q]], preferred_element_type=jnp.float32
        )


def partial_sums(index, couple, blocks):
    slots, seg, _ = couple.shape
    vmem = pl.BlockSpec(memory_space=pltpu.VMEM)
    return pl.pallas_call(
        partial_kernel,
        out_shape=jax.ShapeDtypeStruct((slots, seg, blocks.shape[2]), jnp.float32),
        in_specs=[pl.BlockSpec(memory_space=pltpu.SMEM), vmem, vmem],
        out_specs=vmem,
    )(index, couple, blocks)


SIDE = 4
NEAR = ((1, 0), (3, 0), (0, 1), (0, 3), (1, 1), (1, 3), (3, 1), (3, 3))
RELAYED = (
    ((2, 0), (1, 0), 0), ((2, 0), (3, 0), 1),
    ((2, 1), (1, 0), 0), ((2, 1), (3, 0), 1),
    ((2, 3), (1, 0), 0), ((2, 3), (3, 0), 1),
    ((0, 2), (0, 1), 0), ((0, 2), (0, 3), 1),
    ((1, 2), (0, 1), 0), ((1, 2), (0, 3), 1),
    ((3, 2), (0, 1), 0), ((3, 2), (0, 3), 1),
    ((2, 2), (1, 1), 0), ((2, 2), (3, 3), 1),
)


def exchange_kernel(offsets, *refs):
    parts = (len(refs) - 7) // 3
    send_refs, recv_refs, relay_refs = refs[:parts], refs[parts : 2 * parts], refs[2 * parts : 3 * parts]
    near_send, near_recv, leg_send, leg_recv, fwd_send, fwd_recv, own_sems = refs[3 * parts :]
    me = lax.axis_index("dom")
    grp = lax.axis_index("grp")
    row, col = me // SIDE, me % SIDE

    def at(offset):
        return ((row + offset[0]) % SIDE) * SIDE + (col + offset[1]) % SIDE

    def remote(src, dst, send_sem, recv_sem, offset):
        return pltpu.make_async_remote_copy(
            src_ref=src, dst_ref=dst, send_sem=send_sem, recv_sem=recv_sem,
            device_id=(at(offset), grp), device_id_type=pl.DeviceIdType.MESH,
        )

    barrier = pltpu.get_barrier_semaphore()
    for offset in NEAR:
        pl.semaphore_signal(
            barrier, inc=1, device_id=(at(offset), grp), device_id_type=pl.DeviceIdType.MESH
        )
    pl.semaphore_wait(barrier, len(NEAR))
    owns = []
    for p in range(parts):
        own = pltpu.make_async_copy(send_refs[p].at[me], recv_refs[p].at[offsets[p] + me], own_sems.at[p])
        own.start()
        owns.append(own)
    legs = []
    for k, (target, relay, part) in enumerate(RELAYED):
        for p in range(parts):
            half = send_refs[p].shape[1] // 2
            leg = remote(send_refs[p].at[at(target), pl.ds(part * half, half)], relay_refs[p].at[k],
                         leg_send.at[p, k], leg_recv.at[p, k], relay)
            leg.start()
            legs.append(leg)
    nears = []
    for k, offset in enumerate(NEAR):
        for p in range(parts):
            near = remote(send_refs[p].at[at(offset)], recv_refs[p].at[offsets[p] + me],
                          near_send.at[p, k], near_recv.at[p, k], offset)
            near.start()
            nears.append(near)
    fwds = []
    for k, (target, relay, part) in enumerate(RELAYED):
        source = at(((SIDE - relay[0]) % SIDE, (SIDE - relay[1]) % SIDE))
        onward = ((target[0] - relay[0]) % SIDE, (target[1] - relay[1]) % SIDE)
        for p in range(parts):
            half = send_refs[p].shape[1] // 2
            legs[k * parts + p].wait_recv()
            fwd = remote(relay_refs[p].at[k], recv_refs[p].at[offsets[p] + source, pl.ds(part * half, half)],
                         fwd_send.at[p, k], fwd_recv.at[p, k], onward)
            fwd.start()
            fwds.append(fwd)
    for leg in legs:
        leg.wait_send()
    for near in nears:
        near.wait_send()
    for near in nears:
        near.wait_recv()
    for fwd in fwds:
        fwd.wait_send()
    for fwd in fwds:
        fwd.wait_recv()
    for own in owns:
        own.wait()


def dom_exchange(values, collective, frames=None):
    parts = len(values)
    frames = frames or [(0, v.shape[0]) for v in values]
    outs = [jax.ShapeDtypeStruct((n,) + v.shape[1:], v.dtype) for v, (_, n) in zip(values, frames)]
    relays = [jax.ShapeDtypeStruct((len(RELAYED), v.shape[1] // 2, v.shape[2]), v.dtype) for v in values]
    any_spec = pl.BlockSpec(memory_space=pl.ANY)
    result = pl.pallas_call(
        functools.partial(exchange_kernel, tuple(f[0] for f in frames)),
        out_shape=tuple(outs + relays),
        in_specs=[any_spec] * parts,
        out_specs=tuple([any_spec] * (2 * parts)),
        scratch_shapes=[
            pltpu.SemaphoreType.DMA((parts, len(NEAR))),
            pltpu.SemaphoreType.DMA((parts, len(NEAR))),
            pltpu.SemaphoreType.DMA((parts, len(RELAYED))),
            pltpu.SemaphoreType.DMA((parts, len(RELAYED))),
            pltpu.SemaphoreType.DMA((parts, len(RELAYED))),
            pltpu.SemaphoreType.DMA((parts, len(RELAYED))),
            pltpu.SemaphoreType.DMA((parts,)),
        ],
        compiler_params=pltpu.CompilerParams(collective_id=collective, has_side_effects=True),
    )(*values)
    return result[:parts]


def well_states_of(summed, well_inverse, well_count):
    wells = summed.shape[0]
    live_mask = (jnp.arange(wells) < well_count[0]).astype(jnp.float32)
    solved = jnp.einsum("wst,wtv->wsv", well_inverse, summed, precision=lax.Precision.HIGHEST)
    return (solved * live_mask[:, None, None]).astype(jnp.bfloat16)


def subtract_incoming(product, well_send, incoming):
    targets = well_send[0].reshape(-1)
    selector = (targets[None, :] == jnp.arange(product.shape[0])[:, None]).astype(jnp.bfloat16)
    flat_rows = incoming.reshape(targets.shape[0], product.shape[1], product.shape[2])
    return product - jnp.einsum(
        "bq,qkv->bkv", selector, flat_rows, preferred_element_type=jnp.float32
    )


def on_device(
    blocks,
    tile_values,
    tile_cols,
    halo_send,
    halo_counts,
    grp_send,
    well_send,
    well_slot,
    well_count,
    couple_in,
    couple_out,
    well_inverse,
):
    dom_count = lax.axis_size("dom")
    halo_width = halo_send.shape[2]
    rim_width = grp_send.shape[2]
    slot_width = well_send.shape[2]
    cell_count = blocks.shape[1]
    vec_count = blocks.shape[2]
    wells, couplings = well_slot.shape
    seg = couple_in.shape[2]
    slot_total = dom_count * slot_width
    halo_pack = blocks[halo_send[0]]
    rim_pack = blocks[grp_send[0].reshape(-1)]
    rim_ext = padded(rim_pack, (("grp", 0),), rim_width)
    rim_rows = jnp.concatenate([rim_ext[:rim_width], rim_ext[rim_ext.shape[0] - rim_width :]], 0)
    slot_order = jnp.argsort(well_slot.reshape(-1))
    slot_well = slot_order // couplings
    in_slots = couple_in.reshape(wells * couplings, seg, cell_count)[slot_order]
    in_slots = in_slots.reshape(dom_count, slot_width * seg, cell_count)
    halo_flat = halo_pack.reshape(dom_count, halo_width * cell_count, vec_count)
    (in_recv,) = dom_exchange([in_slots], 0)
    in_recv = in_recv.reshape(dom_count, slot_width, seg, cell_count)
    partial = partial_sums(
        well_send[0].reshape(-1), in_recv.reshape(slot_total, seg, cell_count), blocks
    ).reshape(dom_count, slot_width, seg, vec_count)
    partial_in = lax.all_to_all(partial, "dom", split_axis=0, concat_axis=0, tiled=True)
    own_slots = blocks.shape[0] // halo_width
    ext_slots = own_slots + dom_count + 2 * rim_width // halo_width
    (ext_frame,) = dom_exchange([halo_flat], 1, [(own_slots, ext_slots)])
    partial_in = partial_in.reshape(slot_total, seg, vec_count)
    summed = well_sums(well_slot.reshape(-1), partial_in, wells)
    well_state = well_states_of(summed, well_inverse, well_count)
    state_slots = well_state[slot_well]
    out_slots = couple_out.reshape(wells * couplings, seg, cell_count)[slot_order]
    state_pack = jnp.concatenate([state_slots, out_slots], 2)
    state_pack = state_pack.reshape(dom_count, slot_width, seg, vec_count + cell_count)
    state_in = lax.all_to_all(state_pack, "dom", split_axis=0, concat_axis=0, tiled=True)
    state_in = state_in.reshape(slot_total, seg, vec_count + cell_count)
    live_halo = (jnp.arange(halo_width)[None, :] < halo_counts[0][:, None]).astype(jnp.int32)
    live = jnp.concatenate(
        [jnp.ones((blocks.shape[0],), jnp.int32), live_halo.reshape(-1), jnp.ones((2 * rim_width,), jnp.int32)]
    )
    extended = ext_frame.reshape(ext_slots * halo_width, cell_count, vec_count)
    extended = lax.dynamic_update_slice_in_dim(extended, blocks, 0, 0)
    extended = lax.dynamic_update_slice_in_dim(extended, rim_rows, extended.shape[0] - 2 * rim_width, 0)
    product = local_product(extended, live, tile_values, tile_cols)
    incoming = jnp.einsum(
        "qsk,qsv->qkv",
        state_in[:, :, vec_count:],
        state_in[:, :, :vec_count],
        preferred_element_type=jnp.float32,
    ).astype(jnp.bfloat16)
    return subtract_incoming(product, well_send, incoming).astype(jnp.bfloat16)


def solution(mesh):
    in_specs = (
        P(("dom", "grp"), None, None),
        P(("dom", "grp"), None, None, None),
        P(("dom", "grp"), None),
        P(("dom", "grp"), None, None),
        P(("dom", "grp"), None),
        P(("dom", "grp"), None, None),
        P(("dom", "grp"), None, None),
        P(("dom", "grp"), None),
        P(("dom", "grp")),
        P(("dom", "grp"), None, None, None),
        P(("dom", "grp"), None, None, None),
        P(("dom", "grp"), None, None),
    )
    out_specs = P(("dom", "grp"), None, None)
    return jax.shard_map(
        on_device, mesh=mesh, in_specs=in_specs, out_specs=out_specs, check_vma=False
    )
```

```python
import functools

import jax
import jax.numpy as jnp
from jax import lax
from jax.sharding import PartitionSpec as P
from jax.experimental import pallas as pl
from jax.experimental.pallas import tpu as pltpu


def padded(value, sides, width):
    for axis, dim in sides:
        devices, length = (lax.axis_size(axis), value.shape[dim])
        up = [(i, (i + 1) % devices) for i in range(devices - 1)]
        down = [(j, i) for i, j in up]
        last = lax.slice_in_dim(value, length - width, length, axis=dim)
        leading = lax.slice_in_dim(value, 0, width, axis=dim)
        before = lax.ppermute(last, axis, up)
        after = lax.ppermute(leading, axis, down)
        value = jnp.concatenate([before, value, after], axis=dim)
    return value


def product_kernel(cols_ref, live_ref, ext_ref, tiles_ref, out_ref):
    rows, tiles_per_row = tiles_ref.shape[0], tiles_ref.shape[1]
    first = pl.program_id(0) * rows
    for r in range(rows):
        acc = None
        for t in range(0, tiles_per_row, 2):
            pair = [cols_ref[(first + r) * tiles_per_row + t + u] for u in range(2)]
            lhs = jnp.concatenate(
                [tiles_ref[r, t + u] * live_ref[pair[u]].astype(tiles_ref.dtype) for u in range(2)], axis=1
            )
            rhs = jnp.concatenate([ext_ref[c] for c in pair], axis=0)
            term = jnp.dot(lhs, rhs, preferred_element_type=jnp.float32)
            acc = term if acc is None else acc + term
        out_ref[r] = acc


def local_product(extended, live, tile_values, tile_cols):
    block_rows, tiles_per_row, cells, _ = tile_values.shape
    ext_blocks, _, vecs = extended.shape
    rows = 16
    grid_spec = pltpu.PrefetchScalarGridSpec(
        num_scalar_prefetch=2,
        grid=(block_rows // rows,),
        in_specs=[
            pl.BlockSpec((ext_blocks, cells, vecs), lambda k, cols, live: (0, 0, 0)),
            pl.BlockSpec((rows, tiles_per_row, cells, cells), lambda k, cols, live: (k, 0, 0, 0)),
        ],
        out_specs=pl.BlockSpec((rows, cells, vecs), lambda k, cols, live: (k, 0, 0)),
    )
    flops = 2 * block_rows * tiles_per_row * cells * cells * vecs
    moved = tile_values.size * 2 + extended.size * 2 + block_rows * cells * vecs * 4
    return pl.pallas_call(
        product_kernel,
        out_shape=jax.ShapeDtypeStruct((block_rows, cells, vecs), jnp.float32),
        grid_spec=grid_spec,
        cost_estimate=pl.CostEstimate(flops=flops, transcendentals=0, bytes_accessed=moved),
    )(tile_cols.reshape(-1), live, extended, tile_values)


def sums_kernel(slot_ref, partial_ref, out_ref):
    couplings = slot_ref.shape[0] // out_ref.shape[0]
    for w in range(out_ref.shape[0]):
        acc = partial_ref[slot_ref[w * couplings]]
        for c in range(1, couplings):
            acc = acc + partial_ref[slot_ref[w * couplings + c]]
        out_ref[w] = acc


def well_sums(slots, partial, wells):
    vmem = pl.BlockSpec(memory_space=pltpu.VMEM)
    return pl.pallas_call(
        sums_kernel,
        out_shape=jax.ShapeDtypeStruct((wells,) + partial.shape[1:], jnp.float32),
        in_specs=[pl.BlockSpec(memory_space=pltpu.SMEM), vmem],
        out_specs=vmem,
    )(slots, partial)


def partial_kernel(index_ref, couple_ref, blocks_ref, out_ref):
    for q in range(out_ref.shape[0]):
        out_ref[q] = jnp.dot(
            couple_ref[q], blocks_ref[index_ref[q]], preferred_element_type=jnp.float32
        )


def partial_sums(index, couple, blocks):
    slots, seg, _ = couple.shape
    vmem = pl.BlockSpec(memory_space=pltpu.VMEM)
    return pl.pallas_call(
        partial_kernel,
        out_shape=jax.ShapeDtypeStruct((slots, seg, blocks.shape[2]), jnp.float32),
        in_specs=[pl.BlockSpec(memory_space=pltpu.SMEM), vmem, vmem],
        out_specs=vmem,
    )(index, couple, blocks)


SIDE = 4
NEAR = ((1, 0), (3, 0), (0, 1), (0, 3), (1, 1), (1, 3), (3, 1), (3, 3))
RELAYED = (
    ((2, 0), (1, 0), 0), ((2, 0), (3, 0), 1),
    ((2, 1), (1, 0), 0), ((2, 1), (3, 0), 1),
    ((2, 3), (1, 0), 0), ((2, 3), (3, 0), 1),
    ((0, 2), (0, 1), 0), ((0, 2), (0, 3), 1),
    ((1, 2), (0, 1), 0), ((1, 2), (0, 3), 1),
    ((3, 2), (0, 1), 0), ((3, 2), (0, 3), 1),
    ((2, 2), (1, 1), 0), ((2, 2), (3, 3), 1),
)


def exchange_kernel(offsets, *refs):
    parts = (len(refs) - 7) // 3
    send_refs, recv_refs, relay_refs = refs[:parts], refs[parts : 2 * parts], refs[2 * parts : 3 * parts]
    near_send, near_recv, leg_send, leg_recv, fwd_send, fwd_recv, own_sems = refs[3 * parts :]
    me = lax.axis_index("dom")
    grp = lax.axis_index("grp")
    row, col = me // SIDE, me % SIDE

    def at(offset):
        return ((row + offset[0]) % SIDE) * SIDE + (col + offset[1]) % SIDE

    def remote(src, dst, send_sem, recv_sem, offset):
        return pltpu.make_async_remote_copy(
            src_ref=src, dst_ref=dst, send_sem=send_sem, recv_sem=recv_sem,
            device_id=(at(offset), grp), device_id_type=pl.DeviceIdType.MESH,
        )

    barrier = pltpu.get_barrier_semaphore()
    for offset in NEAR:
        pl.semaphore_signal(
            barrier, inc=1, device_id=(at(offset), grp), device_id_type=pl.DeviceIdType.MESH
        )
    pl.semaphore_wait(barrier, len(NEAR))
    owns = []
    for p in range(parts):
        own = pltpu.make_async_copy(send_refs[p].at[me], recv_refs[p].at[offsets[p] + me], own_sems.at[p])
        own.start()
        owns.append(own)
    legs = []
    for k, (target, relay, part) in enumerate(RELAYED):
        for p in range(parts):
            half = send_refs[p].shape[1] // 2
            leg = remote(send_refs[p].at[at(target), pl.ds(part * half, half)], relay_refs[p].at[k],
                         leg_send.at[p, k], leg_recv.at[p, k], relay)
            leg.start()
            legs.append(leg)
    nears = []
    for k, offset in enumerate(NEAR):
        for p in range(parts):
            near = remote(send_refs[p].at[at(offset)], recv_refs[p].at[offsets[p] + me],
                          near_send.at[p, k], near_recv.at[p, k], offset)
            near.start()
            nears.append(near)
    fwds = []
    for k, (target, relay, part) in enumerate(RELAYED):
        source = at(((SIDE - relay[0]) % SIDE, (SIDE - relay[1]) % SIDE))
        onward = ((target[0] - relay[0]) % SIDE, (target[1] - relay[1]) % SIDE)
        for p in range(parts):
            half = send_refs[p].shape[1] // 2
            legs[k * parts + p].wait_recv()
            fwd = remote(relay_refs[p].at[k], recv_refs[p].at[offsets[p] + source, pl.ds(part * half, half)],
                         fwd_send.at[p, k], fwd_recv.at[p, k], onward)
            fwd.start()
            fwds.append(fwd)
    for leg in legs:
        leg.wait_send()
    for near in nears:
        near.wait_send()
    for near in nears:
        near.wait_recv()
    for fwd in fwds:
        fwd.wait_send()
    for fwd in fwds:
        fwd.wait_recv()
    for own in owns:
        own.wait()


def dom_exchange(values, collective, frames=None):
    parts = len(values)
    frames = frames or [(0, v.shape[0]) for v in values]
    outs = [jax.ShapeDtypeStruct((n,) + v.shape[1:], v.dtype) for v, (_, n) in zip(values, frames)]
    relays = [jax.ShapeDtypeStruct((len(RELAYED), v.shape[1] // 2, v.shape[2]), v.dtype) for v in values]
    any_spec = pl.BlockSpec(memory_space=pl.ANY)
    result = pl.pallas_call(
        functools.partial(exchange_kernel, tuple(f[0] for f in frames)),
        out_shape=tuple(outs + relays),
        in_specs=[any_spec] * parts,
        out_specs=tuple([any_spec] * (2 * parts)),
        scratch_shapes=[
            pltpu.SemaphoreType.DMA((parts, len(NEAR))),
            pltpu.SemaphoreType.DMA((parts, len(NEAR))),
            pltpu.SemaphoreType.DMA((parts, len(RELAYED))),
            pltpu.SemaphoreType.DMA((parts, len(RELAYED))),
            pltpu.SemaphoreType.DMA((parts, len(RELAYED))),
            pltpu.SemaphoreType.DMA((parts, len(RELAYED))),
            pltpu.SemaphoreType.DMA((parts,)),
        ],
        compiler_params=pltpu.CompilerParams(collective_id=collective, has_side_effects=True),
    )(*values)
    return result[:parts]


def well_states_of(summed, well_inverse, well_count):
    wells = summed.shape[0]
    live_mask = (jnp.arange(wells) < well_count[0]).astype(jnp.float32)
    solved = jnp.einsum("wst,wtv->wsv", well_inverse, summed, precision=lax.Precision.HIGHEST)
    return (solved * live_mask[:, None, None]).astype(jnp.bfloat16)


def subtract_incoming(product, well_send, incoming):
    targets = well_send[0].reshape(-1)
    selector = (targets[None, :] == jnp.arange(product.shape[0])[:, None]).astype(jnp.bfloat16)
    flat_rows = incoming.reshape(targets.shape[0], product.shape[1], product.shape[2])
    return product - jnp.einsum(
        "bq,qkv->bkv", selector, flat_rows, preferred_element_type=jnp.float32
    )


def on_device(
    blocks,
    tile_values,
    tile_cols,
    halo_send,
    halo_counts,
    grp_send,
    well_send,
    well_slot,
    well_count,
    couple_in,
    couple_out,
    well_inverse,
):
    dom_count = lax.axis_size("dom")
    halo_width = halo_send.shape[2]
    rim_width = grp_send.shape[2]
    slot_width = well_send.shape[2]
    cell_count = blocks.shape[1]
    vec_count = blocks.shape[2]
    wells, couplings = well_slot.shape
    seg = couple_in.shape[2]
    slot_total = dom_count * slot_width
    halo_pack = blocks[halo_send[0]]
    rim_pack = blocks[grp_send[0].reshape(-1)]
    rim_ext = padded(rim_pack, (("grp", 0),), rim_width)
    rim_rows = jnp.concatenate([rim_ext[:rim_width], rim_ext[rim_ext.shape[0] - rim_width :]], 0)
    slot_order = jnp.argsort(well_slot.reshape(-1))
    slot_well = slot_order // couplings
    in_slots = couple_in.reshape(wells * couplings, seg, cell_count)[slot_order]
    in_slots = in_slots.reshape(dom_count, slot_width * seg, cell_count)
    halo_flat = halo_pack.reshape(dom_count, halo_width * cell_count, vec_count)
    (in_recv,) = dom_exchange([in_slots], 0)
    in_recv = in_recv.reshape(dom_count, slot_width, seg, cell_count)
    partial = partial_sums(
        well_send[0].reshape(-1), in_recv.reshape(slot_total, seg, cell_count), blocks
    ).reshape(dom_count, slot_width, seg, vec_count)
    partial_in = lax.all_to_all(partial, "dom", split_axis=0, concat_axis=0, tiled=True)
    own_slots = blocks.shape[0] // halo_width
    ext_slots = own_slots + dom_count + 2 * rim_width // halo_width
    (ext_frame,) = dom_exchange([halo_flat], 1, [(own_slots, ext_slots)])
    partial_in, ext_frame = lax.optimization_barrier((partial_in, ext_frame))
    partial_in = partial_in.reshape(slot_total, seg, vec_count)
    summed = well_sums(well_slot.reshape(-1), partial_in, wells)
    well_state = well_states_of(summed, well_inverse, well_count)
    state_slots = well_state[slot_well]
    out_slots = couple_out.reshape(wells * couplings, seg, cell_count)[slot_order]
    state_pack = jnp.concatenate([state_slots, out_slots], 2)
    state_pack = state_pack.reshape(dom_count, slot_width, seg, vec_count + cell_count)
    state_in = lax.all_to_all(state_pack, "dom", split_axis=0, concat_axis=0, tiled=True)
    state_in = state_in.reshape(slot_total, seg, vec_count + cell_count)
    live_halo = (jnp.arange(halo_width)[None, :] < halo_counts[0][:, None]).astype(jnp.int32)
    live = jnp.concatenate(
        [jnp.ones((blocks.shape[0],), jnp.int32), live_halo.reshape(-1), jnp.ones((2 * rim_width,), jnp.int32)]
    )
    extended = ext_frame.reshape(ext_slots * halo_width, cell_count, vec_count)
    extended = lax.dynamic_update_slice_in_dim(extended, blocks, 0, 0)
    extended = lax.dynamic_update_slice_in_dim(extended, rim_rows, extended.shape[0] - 2 * rim_width, 0)
    product = local_product(extended, live, tile_values, tile_cols)
    incoming = jnp.einsum(
        "qsk,qsv->qkv",
        state_in[:, :, vec_count:],
        state_in[:, :, :vec_count],
        preferred_element_type=jnp.float32,
    ).astype(jnp.bfloat16)
    return subtract_incoming(product, well_send, incoming).astype(jnp.bfloat16)


def solution(mesh):
    in_specs = (
        P(("dom", "grp"), None, None),
        P(("dom", "grp"), None, None, None),
        P(("dom", "grp"), None),
        P(("dom", "grp"), None, None),
        P(("dom", "grp"), None),
        P(("dom", "grp"), None, None),
        P(("dom", "grp"), None, None),
        P(("dom", "grp"), None),
        P(("dom", "grp")),
        P(("dom", "grp"), None, None, None),
        P(("dom", "grp"), None, None, None),
        P(("dom", "grp"), None, None),
    )
    out_specs = P(("dom", "grp"), None, None)
    return jax.shard_map(
        on_device, mesh=mesh, in_specs=in_specs, out_specs=out_specs, check_vma=False
    )
```

```python
import functools

import jax
import jax.numpy as jnp
from jax import lax
from jax.sharding import PartitionSpec as P
from jax.experimental import pallas as pl
from jax.experimental.pallas import tpu as pltpu


def padded(value, sides, width):
    for axis, dim in sides:
        devices, length = (lax.axis_size(axis), value.shape[dim])
        up = [(i, (i + 1) % devices) for i in range(devices - 1)]
        down = [(j, i) for i, j in up]
        last = lax.slice_in_dim(value, length - width, length, axis=dim)
        leading = lax.slice_in_dim(value, 0, width, axis=dim)
        before = lax.ppermute(last, axis, up)
        after = lax.ppermute(leading, axis, down)
        value = jnp.concatenate([before, value, after], axis=dim)
    return value


def product_kernel(cols_ref, live_ref, ext_ref, tiles_ref, out_ref):
    rows, tiles_per_row = tiles_ref.shape[0], tiles_ref.shape[1]
    first = pl.program_id(0) * rows
    for r in range(rows):
        acc = None
        for t in range(0, tiles_per_row, 2):
            pair = [cols_ref[(first + r) * tiles_per_row + t + u] for u in range(2)]
            lhs = jnp.concatenate(
                [tiles_ref[r, t + u] * live_ref[pair[u]].astype(tiles_ref.dtype) for u in range(2)], axis=1
            )
            rhs = jnp.concatenate([ext_ref[c] for c in pair], axis=0)
            term = jnp.dot(lhs, rhs, preferred_element_type=jnp.float32)
            acc = term if acc is None else acc + term
        out_ref[r] = acc


def local_product(extended, live, tile_values, tile_cols):
    block_rows, tiles_per_row, cells, _ = tile_values.shape
    ext_blocks, _, vecs = extended.shape
    rows = 16
    grid_spec = pltpu.PrefetchScalarGridSpec(
        num_scalar_prefetch=2,
        grid=(block_rows // rows,),
        in_specs=[
            pl.BlockSpec((ext_blocks, cells, vecs), lambda k, cols, live: (0, 0, 0)),
            pl.BlockSpec((rows, tiles_per_row, cells, cells), lambda k, cols, live: (k, 0, 0, 0)),
        ],
        out_specs=pl.BlockSpec((rows, cells, vecs), lambda k, cols, live: (k, 0, 0)),
    )
    flops = 2 * block_rows * tiles_per_row * cells * cells * vecs
    moved = tile_values.size * 2 + extended.size * 2 + block_rows * cells * vecs * 4
    return pl.pallas_call(
        product_kernel,
        out_shape=jax.ShapeDtypeStruct((block_rows, cells, vecs), jnp.float32),
        grid_spec=grid_spec,
        cost_estimate=pl.CostEstimate(flops=flops, transcendentals=0, bytes_accessed=moved),
    )(tile_cols.reshape(-1), live, extended, tile_values)


def sums_kernel(slot_ref, partial_ref, out_ref):
    couplings = slot_ref.shape[0] // out_ref.shape[0]
    for w in range(out_ref.shape[0]):
        acc = partial_ref[slot_ref[w * couplings]]
        for c in range(1, couplings):
            acc = acc + partial_ref[slot_ref[w * couplings + c]]
        out_ref[w] = acc


def well_sums(slots, partial, wells):
    vmem = pl.BlockSpec(memory_space=pltpu.VMEM)
    return pl.pallas_call(
        sums_kernel,
        out_shape=jax.ShapeDtypeStruct((wells,) + partial.shape[1:], jnp.float32),
        in_specs=[pl.BlockSpec(memory_space=pltpu.SMEM), vmem],
        out_specs=vmem,
    )(slots, partial)


def partial_kernel(index_ref, couple_ref, blocks_ref, out_ref):
    for q in range(out_ref.shape[0]):
        out_ref[q] = jnp.dot(
            couple_ref[q], blocks_ref[index_ref[q]], preferred_element_type=jnp.float32
        )


def partial_sums(index, couple, blocks):
    slots, seg, _ = couple.shape
    vmem = pl.BlockSpec(memory_space=pltpu.VMEM)
    return pl.pallas_call(
        partial_kernel,
        out_shape=jax.ShapeDtypeStruct((slots, seg, blocks.shape[2]), jnp.float32),
        in_specs=[pl.BlockSpec(memory_space=pltpu.SMEM), vmem, vmem],
        out_specs=vmem,
    )(index, couple, blocks)


SIDE = 4
NEAR = ((1, 0), (3, 0), (0, 1), (0, 3), (1, 1), (1, 3), (3, 1), (3, 3))
RELAYED = (
    ((2, 0), (1, 0), 0), ((2, 0), (3, 0), 1),
    ((2, 1), (1, 0), 0), ((2, 1), (3, 0), 1),
    ((2, 3), (1, 0), 0), ((2, 3), (3, 0), 1),
    ((0, 2), (0, 1), 0), ((0, 2), (0, 3), 1),
    ((1, 2), (0, 1), 0), ((1, 2), (0, 3), 1),
    ((3, 2), (0, 1), 0), ((3, 2), (0, 3), 1),
    ((2, 2), (1, 1), 0), ((2, 2), (3, 3), 1),
)


def exchange_kernel(offsets, *refs):
    parts = (len(refs) - 7) // 3
    send_refs, recv_refs, relay_refs = refs[:parts], refs[parts : 2 * parts], refs[2 * parts : 3 * parts]
    near_send, near_recv, leg_send, leg_recv, fwd_send, fwd_recv, own_sems = refs[3 * parts :]
    me = lax.axis_index("dom")
    grp = lax.axis_index("grp")
    row, col = me // SIDE, me % SIDE

    def at(offset):
        return ((row + offset[0]) % SIDE) * SIDE + (col + offset[1]) % SIDE

    def remote(src, dst, send_sem, recv_sem, offset):
        return pltpu.make_async_remote_copy(
            src_ref=src, dst_ref=dst, send_sem=send_sem, recv_sem=recv_sem,
            device_id=(at(offset), grp), device_id_type=pl.DeviceIdType.MESH,
        )

    barrier = pltpu.get_barrier_semaphore()
    for offset in NEAR:
        pl.semaphore_signal(
            barrier, inc=1, device_id=(at(offset), grp), device_id_type=pl.DeviceIdType.MESH
        )
    pl.semaphore_wait(barrier, len(NEAR))
    owns = []
    for p in range(parts):
        own = pltpu.make_async_copy(send_refs[p].at[me], recv_refs[p].at[offsets[p] + me], own_sems.at[p])
        own.start()
        owns.append(own)
    legs = []
    for k, (target, relay, part) in enumerate(RELAYED):
        for p in range(parts):
            half = send_refs[p].shape[1] // 2
            leg = remote(send_refs[p].at[at(target), pl.ds(part * half, half)], relay_refs[p].at[k],
                         leg_send.at[p, k], leg_recv.at[p, k], relay)
            leg.start()
            legs.append(leg)
    nears = []
    for k, offset in enumerate(NEAR):
        for p in range(parts):
            near = remote(send_refs[p].at[at(offset)], recv_refs[p].at[offsets[p] + me],
                          near_send.at[p, k], near_recv.at[p, k], offset)
            near.start()
            nears.append(near)
    fwds = []
    for k, (target, relay, part) in enumerate(RELAYED):
        source = at(((SIDE - relay[0]) % SIDE, (SIDE - relay[1]) % SIDE))
        onward = ((target[0] - relay[0]) % SIDE, (target[1] - relay[1]) % SIDE)
        for p in range(parts):
            half = send_refs[p].shape[1] // 2
            legs[k * parts + p].wait_recv()
            fwd = remote(relay_refs[p].at[k], recv_refs[p].at[offsets[p] + source, pl.ds(part * half, half)],
                         fwd_send.at[p, k], fwd_recv.at[p, k], onward)
            fwd.start()
            fwds.append(fwd)
    for leg in legs:
        leg.wait_send()
    for near in nears:
        near.wait_send()
    for near in nears:
        near.wait_recv()
    for fwd in fwds:
        fwd.wait_send()
    for fwd in fwds:
        fwd.wait_recv()
    for own in owns:
        own.wait()


def dom_exchange(values, collective, frames=None):
    parts = len(values)
    frames = frames or [(0, v.shape[0]) for v in values]
    outs = [jax.ShapeDtypeStruct((n,) + v.shape[1:], v.dtype) for v, (_, n) in zip(values, frames)]
    relays = [jax.ShapeDtypeStruct((len(RELAYED), v.shape[1] // 2, v.shape[2]), v.dtype) for v in values]
    any_spec = pl.BlockSpec(memory_space=pl.ANY)
    result = pl.pallas_call(
        functools.partial(exchange_kernel, tuple(f[0] for f in frames)),
        out_shape=tuple(outs + relays),
        in_specs=[any_spec] * parts,
        out_specs=tuple([any_spec] * (2 * parts)),
        scratch_shapes=[
            pltpu.SemaphoreType.DMA((parts, len(NEAR))),
            pltpu.SemaphoreType.DMA((parts, len(NEAR))),
            pltpu.SemaphoreType.DMA((parts, len(RELAYED))),
            pltpu.SemaphoreType.DMA((parts, len(RELAYED))),
            pltpu.SemaphoreType.DMA((parts, len(RELAYED))),
            pltpu.SemaphoreType.DMA((parts, len(RELAYED))),
            pltpu.SemaphoreType.DMA((parts,)),
        ],
        compiler_params=pltpu.CompilerParams(collective_id=collective, has_side_effects=True),
    )(*values)
    return result[:parts]


def well_states_of(summed, well_inverse, well_count):
    wells = summed.shape[0]
    live_mask = (jnp.arange(wells) < well_count[0]).astype(jnp.float32)
    solved = jnp.einsum("wst,wtv->wsv", well_inverse, summed, precision=lax.Precision.HIGHEST)
    return (solved * live_mask[:, None, None]).astype(jnp.bfloat16)


def subtract_incoming(product, well_send, incoming):
    targets = well_send[0].reshape(-1)
    selector = (targets[None, :] == jnp.arange(product.shape[0])[:, None]).astype(jnp.bfloat16)
    flat_rows = incoming.reshape(targets.shape[0], product.shape[1], product.shape[2])
    return product - jnp.einsum(
        "bq,qkv->bkv", selector, flat_rows, preferred_element_type=jnp.float32
    )


def on_device(
    blocks,
    tile_values,
    tile_cols,
    halo_send,
    halo_counts,
    grp_send,
    well_send,
    well_slot,
    well_count,
    couple_in,
    couple_out,
    well_inverse,
):
    dom_count = lax.axis_size("dom")
    halo_width = halo_send.shape[2]
    rim_width = grp_send.shape[2]
    slot_width = well_send.shape[2]
    cell_count = blocks.shape[1]
    vec_count = blocks.shape[2]
    wells, couplings = well_slot.shape
    seg = couple_in.shape[2]
    slot_total = dom_count * slot_width
    halo_pack = blocks[halo_send[0]]
    rim_pack = blocks[grp_send[0].reshape(-1)]
    rim_ext = padded(rim_pack, (("grp", 0),), rim_width)
    rim_rows = jnp.concatenate([rim_ext[:rim_width], rim_ext[rim_ext.shape[0] - rim_width :]], 0)
    slot_order = jnp.argsort(well_slot.reshape(-1))
    slot_well = slot_order // couplings
    in_slots = couple_in.reshape(wells * couplings, seg, cell_count)[slot_order]
    in_slots = in_slots.reshape(dom_count, slot_width * seg, cell_count)
    halo_flat = halo_pack.reshape(dom_count, halo_width * cell_count, vec_count)
    out_slots = couple_out.reshape(wells * couplings, seg, cell_count)[slot_order]
    out_slots = out_slots.reshape(dom_count, slot_width * seg, cell_count)
    in_recv, out_recv = dom_exchange([in_slots, out_slots], 0)
    in_recv = in_recv.reshape(dom_count, slot_width, seg, cell_count)
    partial = partial_sums(
        well_send[0].reshape(-1), in_recv.reshape(slot_total, seg, cell_count), blocks
    ).reshape(dom_count, slot_width, seg, vec_count)
    partial_in = lax.all_to_all(partial, "dom", split_axis=0, concat_axis=0, tiled=True)
    own_slots = blocks.shape[0] // halo_width
    ext_slots = own_slots + dom_count + 2 * rim_width // halo_width
    (ext_frame,) = dom_exchange([halo_flat], 1, [(own_slots, ext_slots)])
    partial_in, ext_frame = lax.optimization_barrier((partial_in, ext_frame))
    partial_in = partial_in.reshape(slot_total, seg, vec_count)
    summed = well_sums(well_slot.reshape(-1), partial_in, wells)
    well_state = well_states_of(summed, well_inverse, well_count)
    state_pack = well_state[slot_well].reshape(dom_count, slot_width, seg, vec_count)
    state_in = lax.all_to_all(state_pack, "dom", split_axis=0, concat_axis=0, tiled=True)
    state_in = state_in.reshape(slot_total, seg, vec_count)
    live_halo = (jnp.arange(halo_width)[None, :] < halo_counts[0][:, None]).astype(jnp.int32)
    live = jnp.concatenate(
        [jnp.ones((blocks.shape[0],), jnp.int32), live_halo.reshape(-1), jnp.ones((2 * rim_width,), jnp.int32)]
    )
    extended = ext_frame.reshape(ext_slots * halo_width, cell_count, vec_count)
    extended = lax.dynamic_update_slice_in_dim(extended, blocks, 0, 0)
    extended = lax.dynamic_update_slice_in_dim(extended, rim_rows, extended.shape[0] - 2 * rim_width, 0)
    product = local_product(extended, live, tile_values, tile_cols)
    incoming = jnp.einsum(
        "qsk,qsv->qkv",
        out_recv.reshape(slot_total, seg, cell_count),
        state_in,
        preferred_element_type=jnp.float32,
    ).astype(jnp.bfloat16)
    return subtract_incoming(product, well_send, incoming).astype(jnp.bfloat16)


def solution(mesh):
    in_specs = (
        P(("dom", "grp"), None, None),
        P(("dom", "grp"), None, None, None),
        P(("dom", "grp"), None),
        P(("dom", "grp"), None, None),
        P(("dom", "grp"), None),
        P(("dom", "grp"), None, None),
        P(("dom", "grp"), None, None),
        P(("dom", "grp"), None),
        P(("dom", "grp")),
        P(("dom", "grp"), None, None, None),
        P(("dom", "grp"), None, None, None),
        P(("dom", "grp"), None, None),
    )
    out_specs = P(("dom", "grp"), None, None)
    return jax.shard_map(
        on_device, mesh=mesh, in_specs=in_specs, out_specs=out_specs, check_vma=False
    )
```

```python
import functools

import jax
import jax.numpy as jnp
from jax import lax
from jax.sharding import PartitionSpec as P
from jax.experimental import pallas as pl
from jax.experimental.pallas import tpu as pltpu


def padded(value, sides, width):
    for axis, dim in sides:
        devices, length = (lax.axis_size(axis), value.shape[dim])
        up = [(i, (i + 1) % devices) for i in range(devices - 1)]
        down = [(j, i) for i, j in up]
        last = lax.slice_in_dim(value, length - width, length, axis=dim)
        leading = lax.slice_in_dim(value, 0, width, axis=dim)
        before = lax.ppermute(last, axis, up)
        after = lax.ppermute(leading, axis, down)
        value = jnp.concatenate([before, value, after], axis=dim)
    return value


def product_kernel(cols_ref, live_ref, ext_ref, tiles_ref, out_ref):
    rows, tiles_per_row = tiles_ref.shape[0], tiles_ref.shape[1]
    first = pl.program_id(0) * rows
    for r in range(rows):
        acc = None
        for t in range(0, tiles_per_row, 2):
            pair = [cols_ref[(first + r) * tiles_per_row + t + u] for u in range(2)]
            lhs = jnp.concatenate(
                [tiles_ref[r, t + u] * live_ref[pair[u]].astype(tiles_ref.dtype) for u in range(2)], axis=1
            )
            rhs = jnp.concatenate([ext_ref[c] for c in pair], axis=0)
            term = jnp.dot(lhs, rhs, preferred_element_type=jnp.float32)
            acc = term if acc is None else acc + term
        out_ref[r] = acc


def local_product(extended, live, tile_values, tile_cols):
    block_rows, tiles_per_row, cells, _ = tile_values.shape
    ext_blocks, _, vecs = extended.shape
    rows = 16
    grid_spec = pltpu.PrefetchScalarGridSpec(
        num_scalar_prefetch=2,
        grid=(block_rows // rows,),
        in_specs=[
            pl.BlockSpec((ext_blocks, cells, vecs), lambda k, cols, live: (0, 0, 0)),
            pl.BlockSpec((rows, tiles_per_row, cells, cells), lambda k, cols, live: (k, 0, 0, 0)),
        ],
        out_specs=pl.BlockSpec((rows, cells, vecs), lambda k, cols, live: (k, 0, 0)),
    )
    flops = 2 * block_rows * tiles_per_row * cells * cells * vecs
    moved = tile_values.size * 2 + extended.size * 2 + block_rows * cells * vecs * 4
    return pl.pallas_call(
        product_kernel,
        out_shape=jax.ShapeDtypeStruct((block_rows, cells, vecs), jnp.float32),
        grid_spec=grid_spec,
        cost_estimate=pl.CostEstimate(flops=flops, transcendentals=0, bytes_accessed=moved),
    )(tile_cols.reshape(-1), live, extended, tile_values)


def sums_kernel(slot_ref, partial_ref, out_ref):
    couplings = slot_ref.shape[0] // out_ref.shape[0]
    for w in range(out_ref.shape[0]):
        acc = partial_ref[slot_ref[w * couplings]]
        for c in range(1, couplings):
            acc = acc + partial_ref[slot_ref[w * couplings + c]]
        out_ref[w] = acc


def well_sums(slots, partial, wells):
    vmem = pl.BlockSpec(memory_space=pltpu.VMEM)
    return pl.pallas_call(
        sums_kernel,
        out_shape=jax.ShapeDtypeStruct((wells,) + partial.shape[1:], jnp.float32),
        in_specs=[pl.BlockSpec(memory_space=pltpu.SMEM), vmem],
        out_specs=vmem,
    )(slots, partial)


def partial_kernel(index_ref, couple_ref, blocks_ref, out_ref):
    for q in range(out_ref.shape[0]):
        out_ref[q] = jnp.dot(
            couple_ref[q], blocks_ref[index_ref[q]], preferred_element_type=jnp.float32
        )


def partial_sums(index, couple, blocks):
    slots, seg, _ = couple.shape
    vmem = pl.BlockSpec(memory_space=pltpu.VMEM)
    return pl.pallas_call(
        partial_kernel,
        out_shape=jax.ShapeDtypeStruct((slots, seg, blocks.shape[2]), jnp.float32),
        in_specs=[pl.BlockSpec(memory_space=pltpu.SMEM), vmem, vmem],
        out_specs=vmem,
    )(index, couple, blocks)


SIDE = 4
NEAR = ((1, 0), (3, 0), (0, 1), (0, 3), (1, 1), (1, 3), (3, 1), (3, 3))
RELAYED = (
    ((2, 0), (1, 0), 0), ((2, 0), (3, 0), 1),
    ((2, 1), (1, 0), 0), ((2, 1), (3, 0), 1),
    ((2, 3), (1, 0), 0), ((2, 3), (3, 0), 1),
    ((0, 2), (0, 1), 0), ((0, 2), (0, 3), 1),
    ((1, 2), (0, 1), 0), ((1, 2), (0, 3), 1),
    ((3, 2), (0, 1), 0), ((3, 2), (0, 3), 1),
    ((2, 2), (1, 1), 0), ((2, 2), (3, 3), 1),
)


def exchange_kernel(offsets, *refs):
    parts = (len(refs) - 7) // 3
    send_refs, recv_refs, relay_refs = refs[:parts], refs[parts : 2 * parts], refs[2 * parts : 3 * parts]
    near_send, near_recv, leg_send, leg_recv, fwd_send, fwd_recv, own_sems = refs[3 * parts :]
    me = lax.axis_index("dom")
    grp = lax.axis_index("grp")
    row, col = me // SIDE, me % SIDE

    def at(offset):
        return ((row + offset[0]) % SIDE) * SIDE + (col + offset[1]) % SIDE

    def remote(src, dst, send_sem, recv_sem, offset):
        return pltpu.make_async_remote_copy(
            src_ref=src, dst_ref=dst, send_sem=send_sem, recv_sem=recv_sem,
            device_id=(at(offset), grp), device_id_type=pl.DeviceIdType.MESH,
        )

    barrier = pltpu.get_barrier_semaphore()
    for offset in NEAR:
        pl.semaphore_signal(
            barrier, inc=1, device_id=(at(offset), grp), device_id_type=pl.DeviceIdType.MESH
        )
    pl.semaphore_wait(barrier, len(NEAR))
    owns = []
    for p in range(parts):
        own = pltpu.make_async_copy(send_refs[p].at[me], recv_refs[p].at[offsets[p] + me], own_sems.at[p])
        own.start()
        owns.append(own)
    legs = []
    for k, (target, relay, part) in enumerate(RELAYED):
        for p in range(parts):
            half = send_refs[p].shape[1] // 2
            leg = remote(send_refs[p].at[at(target), pl.ds(part * half, half)], relay_refs[p].at[k],
                         leg_send.at[p, k], leg_recv.at[p, k], relay)
            leg.start()
            legs.append(leg)
    nears = []
    for k, offset in enumerate(NEAR):
        for p in range(parts):
            near = remote(send_refs[p].at[at(offset)], recv_refs[p].at[offsets[p] + me],
                          near_send.at[p, k], near_recv.at[p, k], offset)
            near.start()
            nears.append(near)
    fwds = []
    for k, (target, relay, part) in enumerate(RELAYED):
        source = at(((SIDE - relay[0]) % SIDE, (SIDE - relay[1]) % SIDE))
        onward = ((target[0] - relay[0]) % SIDE, (target[1] - relay[1]) % SIDE)
        for p in range(parts):
            half = send_refs[p].shape[1] // 2
            legs[k * parts + p].wait_recv()
            fwd = remote(relay_refs[p].at[k], recv_refs[p].at[offsets[p] + source, pl.ds(part * half, half)],
                         fwd_send.at[p, k], fwd_recv.at[p, k], onward)
            fwd.start()
            fwds.append(fwd)
    for leg in legs:
        leg.wait_send()
    for near in nears:
        near.wait_send()
    for near in nears:
        near.wait_recv()
    for fwd in fwds:
        fwd.wait_send()
    for fwd in fwds:
        fwd.wait_recv()
    for own in owns:
        own.wait()


def dom_exchange(values, collective, frames=None):
    parts = len(values)
    frames = frames or [(0, v.shape[0]) for v in values]
    outs = [jax.ShapeDtypeStruct((n,) + v.shape[1:], v.dtype) for v, (_, n) in zip(values, frames)]
    relays = [jax.ShapeDtypeStruct((len(RELAYED), v.shape[1] // 2, v.shape[2]), v.dtype) for v in values]
    any_spec = pl.BlockSpec(memory_space=pl.ANY)
    result = pl.pallas_call(
        functools.partial(exchange_kernel, tuple(f[0] for f in frames)),
        out_shape=tuple(outs + relays),
        in_specs=[any_spec] * parts,
        out_specs=tuple([any_spec] * (2 * parts)),
        scratch_shapes=[
            pltpu.SemaphoreType.DMA((parts, len(NEAR))),
            pltpu.SemaphoreType.DMA((parts, len(NEAR))),
            pltpu.SemaphoreType.DMA((parts, len(RELAYED))),
            pltpu.SemaphoreType.DMA((parts, len(RELAYED))),
            pltpu.SemaphoreType.DMA((parts, len(RELAYED))),
            pltpu.SemaphoreType.DMA((parts, len(RELAYED))),
            pltpu.SemaphoreType.DMA((parts,)),
        ],
        compiler_params=pltpu.CompilerParams(collective_id=collective, has_side_effects=True),
    )(*values)
    return result[:parts]


def finish_kernel(targets_ref, product_ref, incoming_ref, out_ref, acc_ref):
    acc_ref[...] = product_ref[...]
    for q in range(incoming_ref.shape[0]):
        target = targets_ref[q]
        acc_ref[target] = acc_ref[target] - incoming_ref[q].astype(jnp.float32)
    out_ref[...] = acc_ref[...].astype(out_ref.dtype)


def finish(product, incoming, targets):
    vmem = pl.BlockSpec(memory_space=pltpu.VMEM)
    return pl.pallas_call(
        finish_kernel,
        out_shape=jax.ShapeDtypeStruct(product.shape, jnp.bfloat16),
        in_specs=[pl.BlockSpec(memory_space=pltpu.SMEM), vmem, vmem],
        out_specs=vmem,
        scratch_shapes=[pltpu.VMEM(product.shape, jnp.float32)],
    )(targets, product, incoming)


def well_states_of(summed, well_inverse, well_count):
    wells = summed.shape[0]
    live_mask = (jnp.arange(wells) < well_count[0]).astype(jnp.float32)
    solved = jnp.einsum("wst,wtv->wsv", well_inverse, summed, precision=lax.Precision.HIGHEST)
    return (solved * live_mask[:, None, None]).astype(jnp.bfloat16)


def subtract_incoming(product, well_send, incoming):
    targets = well_send[0].reshape(-1)
    selector = (targets[None, :] == jnp.arange(product.shape[0])[:, None]).astype(jnp.bfloat16)
    flat_rows = incoming.reshape(targets.shape[0], product.shape[1], product.shape[2])
    return product - jnp.einsum(
        "bq,qkv->bkv", selector, flat_rows, preferred_element_type=jnp.float32
    )


def on_device(
    blocks,
    tile_values,
    tile_cols,
    halo_send,
    halo_counts,
    grp_send,
    well_send,
    well_slot,
    well_count,
    couple_in,
    couple_out,
    well_inverse,
):
    dom_count = lax.axis_size("dom")
    halo_width = halo_send.shape[2]
    rim_width = grp_send.shape[2]
    slot_width = well_send.shape[2]
    cell_count = blocks.shape[1]
    vec_count = blocks.shape[2]
    wells, couplings = well_slot.shape
    seg = couple_in.shape[2]
    slot_total = dom_count * slot_width
    halo_pack = blocks[halo_send[0]]
    rim_pack = blocks[grp_send[0].reshape(-1)]
    rim_ext = padded(rim_pack, (("grp", 0),), rim_width)
    rim_rows = jnp.concatenate([rim_ext[:rim_width], rim_ext[rim_ext.shape[0] - rim_width :]], 0)
    slot_order = jnp.argsort(well_slot.reshape(-1))
    slot_well = slot_order // couplings
    in_slots = couple_in.reshape(wells * couplings, seg, cell_count)[slot_order]
    in_slots = in_slots.reshape(dom_count, slot_width * seg, cell_count)
    halo_flat = halo_pack.reshape(dom_count, halo_width * cell_count, vec_count)
    out_slots = couple_out.reshape(wells * couplings, seg, cell_count)[slot_order]
    out_slots = out_slots.reshape(dom_count, slot_width * seg, cell_count)
    in_recv, out_recv = dom_exchange([in_slots, out_slots], 0)
    in_recv = in_recv.reshape(dom_count, slot_width, seg, cell_count)
    partial = partial_sums(
        well_send[0].reshape(-1), in_recv.reshape(slot_total, seg, cell_count), blocks
    ).reshape(dom_count, slot_width, seg, vec_count)
    partial_in = lax.all_to_all(partial, "dom", split_axis=0, concat_axis=0, tiled=True)
    own_slots = blocks.shape[0] // halo_width
    ext_slots = own_slots + dom_count + 2 * rim_width // halo_width
    (ext_frame,) = dom_exchange([halo_flat], 1, [(own_slots, ext_slots)])
    partial_in, ext_frame = lax.optimization_barrier((partial_in, ext_frame))
    partial_in = partial_in.reshape(slot_total, seg, vec_count)
    summed = well_sums(well_slot.reshape(-1), partial_in, wells)
    well_state = well_states_of(summed, well_inverse, well_count)
    state_pack = well_state[slot_well].reshape(dom_count, slot_width, seg, vec_count)
    state_in = lax.all_to_all(state_pack, "dom", split_axis=0, concat_axis=0, tiled=True)
    state_in = state_in.reshape(slot_total, seg, vec_count)
    live_halo = (jnp.arange(halo_width)[None, :] < halo_counts[0][:, None]).astype(jnp.int32)
    live = jnp.concatenate(
        [jnp.ones((blocks.shape[0],), jnp.int32), live_halo.reshape(-1), jnp.ones((2 * rim_width,), jnp.int32)]
    )
    extended = ext_frame.reshape(ext_slots * halo_width, cell_count, vec_count)
    extended = lax.dynamic_update_slice_in_dim(extended, blocks, 0, 0)
    extended = lax.dynamic_update_slice_in_dim(extended, rim_rows, extended.shape[0] - 2 * rim_width, 0)
    product = local_product(extended, live, tile_values, tile_cols)
    incoming = jnp.einsum(
        "qsk,qsv->qkv",
        out_recv.reshape(slot_total, seg, cell_count),
        state_in,
        preferred_element_type=jnp.float32,
    ).astype(jnp.bfloat16)
    return finish(product, incoming, well_send[0].reshape(-1))


def solution(mesh):
    in_specs = (
        P(("dom", "grp"), None, None),
        P(("dom", "grp"), None, None, None),
        P(("dom", "grp"), None),
        P(("dom", "grp"), None, None),
        P(("dom", "grp"), None),
        P(("dom", "grp"), None, None),
        P(("dom", "grp"), None, None),
        P(("dom", "grp"), None),
        P(("dom", "grp")),
        P(("dom", "grp"), None, None, None),
        P(("dom", "grp"), None, None, None),
        P(("dom", "grp"), None, None),
    )
    out_specs = P(("dom", "grp"), None, None)
    return jax.shard_map(
        on_device, mesh=mesh, in_specs=in_specs, out_specs=out_specs, check_vma=False
    )
```

```python
import functools

import jax
import jax.numpy as jnp
from jax import lax
from jax.sharding import PartitionSpec as P
from jax.experimental import pallas as pl
from jax.experimental.pallas import tpu as pltpu


def padded(value, sides, width):
    for axis, dim in sides:
        devices, length = (lax.axis_size(axis), value.shape[dim])
        up = [(i, (i + 1) % devices) for i in range(devices - 1)]
        down = [(j, i) for i, j in up]
        last = lax.slice_in_dim(value, length - width, length, axis=dim)
        leading = lax.slice_in_dim(value, 0, width, axis=dim)
        before = lax.ppermute(last, axis, up)
        after = lax.ppermute(leading, axis, down)
        value = jnp.concatenate([before, value, after], axis=dim)
    return value


def product_kernel(cols_ref, live_ref, ext_ref, tiles_ref, out_ref):
    rows, tiles_per_row = tiles_ref.shape[0], tiles_ref.shape[1]
    first = pl.program_id(0) * rows
    for r in range(rows):
        acc = None
        for t in range(0, tiles_per_row, 2):
            pair = [cols_ref[(first + r) * tiles_per_row + t + u] for u in range(2)]
            lhs = jnp.concatenate(
                [tiles_ref[r, t + u] * live_ref[pair[u]].astype(tiles_ref.dtype) for u in range(2)], axis=1
            )
            rhs = jnp.concatenate([ext_ref[c] for c in pair], axis=0)
            term = jnp.dot(lhs, rhs, preferred_element_type=jnp.float32)
            acc = term if acc is None else acc + term
        out_ref[r] = acc


def local_product(extended, live, tile_values, tile_cols):
    block_rows, tiles_per_row, cells, _ = tile_values.shape
    ext_blocks, _, vecs = extended.shape
    rows = 16
    grid_spec = pltpu.PrefetchScalarGridSpec(
        num_scalar_prefetch=2,
        grid=(block_rows // rows,),
        in_specs=[
            pl.BlockSpec((ext_blocks, cells, vecs), lambda k, cols, live: (0, 0, 0)),
            pl.BlockSpec((rows, tiles_per_row, cells, cells), lambda k, cols, live: (k, 0, 0, 0)),
        ],
        out_specs=pl.BlockSpec((rows, cells, vecs), lambda k, cols, live: (k, 0, 0)),
    )
    flops = 2 * block_rows * tiles_per_row * cells * cells * vecs
    moved = tile_values.size * 2 + extended.size * 2 + block_rows * cells * vecs * 4
    return pl.pallas_call(
        product_kernel,
        out_shape=jax.ShapeDtypeStruct((block_rows, cells, vecs), jnp.float32),
        grid_spec=grid_spec,
        cost_estimate=pl.CostEstimate(flops=flops, transcendentals=0, bytes_accessed=moved),
    )(tile_cols.reshape(-1), live, extended, tile_values)


def sums_kernel(slot_ref, partial_ref, out_ref):
    couplings = slot_ref.shape[0] // out_ref.shape[0]
    for w in range(out_ref.shape[0]):
        acc = partial_ref[slot_ref[w * couplings]]
        for c in range(1, couplings):
            acc = acc + partial_ref[slot_ref[w * couplings + c]]
        out_ref[w] = acc


def well_sums(slots, partial, wells):
    vmem = pl.BlockSpec(memory_space=pltpu.VMEM)
    return pl.pallas_call(
        sums_kernel,
        out_shape=jax.ShapeDtypeStruct((wells,) + partial.shape[1:], jnp.float32),
        in_specs=[pl.BlockSpec(memory_space=pltpu.SMEM), vmem],
        out_specs=vmem,
    )(slots, partial)


def partial_kernel(index_ref, couple_ref, blocks_ref, out_ref):
    for q in range(out_ref.shape[0]):
        out_ref[q] = jnp.dot(
            couple_ref[q], blocks_ref[index_ref[q]], preferred_element_type=jnp.float32
        )


def partial_sums(index, couple, blocks):
    slots, seg, _ = couple.shape
    vmem = pl.BlockSpec(memory_space=pltpu.VMEM)
    return pl.pallas_call(
        partial_kernel,
        out_shape=jax.ShapeDtypeStruct((slots, seg, blocks.shape[2]), jnp.float32),
        in_specs=[pl.BlockSpec(memory_space=pltpu.SMEM), vmem, vmem],
        out_specs=vmem,
    )(index, couple, blocks)


SIDE = 4
NEAR = ((1, 0), (3, 0), (0, 1), (0, 3), (1, 1), (1, 3), (3, 1), (3, 3))
RELAYED = (
    ((2, 0), (1, 0), 0), ((2, 0), (3, 0), 1),
    ((2, 1), (1, 0), 0), ((2, 1), (3, 0), 1),
    ((2, 3), (1, 0), 0), ((2, 3), (3, 0), 1),
    ((0, 2), (0, 1), 0), ((0, 2), (0, 3), 1),
    ((1, 2), (0, 1), 0), ((1, 2), (0, 3), 1),
    ((3, 2), (0, 1), 0), ((3, 2), (0, 3), 1),
    ((2, 2), (1, 1), 0), ((2, 2), (3, 3), 1),
)


def exchange_kernel(offsets, *refs):
    parts = (len(refs) - 7) // 3
    send_refs, recv_refs, relay_refs = refs[:parts], refs[parts : 2 * parts], refs[2 * parts : 3 * parts]
    near_send, near_recv, leg_send, leg_recv, fwd_send, fwd_recv, own_sems = refs[3 * parts :]
    me = lax.axis_index("dom")
    grp = lax.axis_index("grp")
    row, col = me // SIDE, me % SIDE

    def at(offset):
        return ((row + offset[0]) % SIDE) * SIDE + (col + offset[1]) % SIDE

    def remote(src, dst, send_sem, recv_sem, offset):
        return pltpu.make_async_remote_copy(
            src_ref=src, dst_ref=dst, send_sem=send_sem, recv_sem=recv_sem,
            device_id=(at(offset), grp), device_id_type=pl.DeviceIdType.MESH,
        )

    barrier = pltpu.get_barrier_semaphore()
    for offset in NEAR:
        pl.semaphore_signal(
            barrier, inc=1, device_id=(at(offset), grp), device_id_type=pl.DeviceIdType.MESH
        )
    pl.semaphore_wait(barrier, len(NEAR))
    owns = []
    for p in range(parts):
        own = pltpu.make_async_copy(send_refs[p].at[me], recv_refs[p].at[offsets[p] + me], own_sems.at[p])
        own.start()
        owns.append(own)
    legs = []
    for k, (target, relay, part) in enumerate(RELAYED):
        for p in range(parts):
            half = send_refs[p].shape[1] // 2
            leg = remote(send_refs[p].at[at(target), pl.ds(part * half, half)], relay_refs[p].at[k],
                         leg_send.at[p, k], leg_recv.at[p, k], relay)
            leg.start()
            legs.append(leg)
    nears = []
    for k, offset in enumerate(NEAR):
        for p in range(parts):
            near = remote(send_refs[p].at[at(offset)], recv_refs[p].at[offsets[p] + me],
                          near_send.at[p, k], near_recv.at[p, k], offset)
            near.start()
            nears.append(near)
    fwds = []
    for k, (target, relay, part) in enumerate(RELAYED):
        source = at(((SIDE - relay[0]) % SIDE, (SIDE - relay[1]) % SIDE))
        onward = ((target[0] - relay[0]) % SIDE, (target[1] - relay[1]) % SIDE)
        for p in range(parts):
            half = send_refs[p].shape[1] // 2
            legs[k * parts + p].wait_recv()
            fwd = remote(relay_refs[p].at[k], recv_refs[p].at[offsets[p] + source, pl.ds(part * half, half)],
                         fwd_send.at[p, k], fwd_recv.at[p, k], onward)
            fwd.start()
            fwds.append(fwd)
    for leg in legs:
        leg.wait_send()
    for near in nears:
        near.wait_send()
    for near in nears:
        near.wait_recv()
    for fwd in fwds:
        fwd.wait_send()
    for fwd in fwds:
        fwd.wait_recv()
    for own in owns:
        own.wait()


def dom_exchange(values, collective, frames=None):
    parts = len(values)
    frames = frames or [(0, v.shape[0]) for v in values]
    outs = [jax.ShapeDtypeStruct((n,) + v.shape[1:], v.dtype) for v, (_, n) in zip(values, frames)]
    relays = [jax.ShapeDtypeStruct((len(RELAYED), v.shape[1] // 2, v.shape[2]), v.dtype) for v in values]
    any_spec = pl.BlockSpec(memory_space=pl.ANY)
    result = pl.pallas_call(
        functools.partial(exchange_kernel, tuple(f[0] for f in frames)),
        out_shape=tuple(outs + relays),
        in_specs=[any_spec] * parts,
        out_specs=tuple([any_spec] * (2 * parts)),
        scratch_shapes=[
            pltpu.SemaphoreType.DMA((parts, len(NEAR))),
            pltpu.SemaphoreType.DMA((parts, len(NEAR))),
            pltpu.SemaphoreType.DMA((parts, len(RELAYED))),
            pltpu.SemaphoreType.DMA((parts, len(RELAYED))),
            pltpu.SemaphoreType.DMA((parts, len(RELAYED))),
            pltpu.SemaphoreType.DMA((parts, len(RELAYED))),
            pltpu.SemaphoreType.DMA((parts,)),
        ],
        compiler_params=pltpu.CompilerParams(collective_id=collective, has_side_effects=True),
    )(*values)
    return result[:parts]


def well_states_of(summed, well_inverse, well_count):
    wells = summed.shape[0]
    live_mask = (jnp.arange(wells) < well_count[0]).astype(jnp.float32)
    solved = jnp.einsum("wst,wtv->wsv", well_inverse, summed, precision=lax.Precision.HIGHEST)
    return (solved * live_mask[:, None, None]).astype(jnp.bfloat16)


def subtract_incoming(product, well_send, incoming):
    targets = well_send[0].reshape(-1)
    selector = (targets[None, :] == jnp.arange(product.shape[0])[:, None]).astype(jnp.bfloat16)
    flat_rows = incoming.reshape(targets.shape[0], product.shape[1], product.shape[2])
    return product - jnp.einsum(
        "bq,qkv->bkv", selector, flat_rows, preferred_element_type=jnp.float32
    )


def on_device(
    blocks,
    tile_values,
    tile_cols,
    halo_send,
    halo_counts,
    grp_send,
    well_send,
    well_slot,
    well_count,
    couple_in,
    couple_out,
    well_inverse,
):
    dom_count = lax.axis_size("dom")
    halo_width = halo_send.shape[2]
    rim_width = grp_send.shape[2]
    slot_width = well_send.shape[2]
    cell_count = blocks.shape[1]
    vec_count = blocks.shape[2]
    wells, couplings = well_slot.shape
    seg = couple_in.shape[2]
    slot_total = dom_count * slot_width
    halo_pack = blocks[halo_send[0]]
    rim_pack = blocks[grp_send[0].reshape(-1)]
    rim_ext = padded(rim_pack, (("grp", 0),), rim_width)
    rim_rows = jnp.concatenate([rim_ext[:rim_width], rim_ext[rim_ext.shape[0] - rim_width :]], 0)
    slot_flat = well_slot.reshape(-1)
    slot_order = jnp.zeros_like(slot_flat).at[slot_flat].set(jnp.arange(slot_flat.shape[0], dtype=slot_flat.dtype))
    slot_well = slot_order // couplings
    couple_both = jnp.concatenate(
        [couple_in.reshape(wells * couplings, seg, cell_count), couple_out.reshape(wells * couplings, seg, cell_count)], 2
    )[slot_order]
    halo_flat = halo_pack.reshape(dom_count, halo_width * cell_count, vec_count)
    (both_recv,) = dom_exchange([couple_both.reshape(dom_count, slot_width * seg, 2 * cell_count)], 0)
    both_recv = both_recv.reshape(slot_total, seg, 2 * cell_count)
    in_recv = both_recv[:, :, :cell_count]
    out_recv = both_recv[:, :, cell_count:]
    partial = partial_sums(
        well_send[0].reshape(-1), in_recv.reshape(slot_total, seg, cell_count), blocks
    ).reshape(dom_count, slot_width, seg, vec_count)
    partial_in = lax.all_to_all(partial, "dom", split_axis=0, concat_axis=0, tiled=True)
    own_slots = blocks.shape[0] // halo_width
    ext_slots = own_slots + dom_count + 2 * rim_width // halo_width
    (ext_frame,) = dom_exchange([halo_flat], 1, [(own_slots, ext_slots)])
    partial_in, ext_frame = lax.optimization_barrier((partial_in, ext_frame))
    partial_in = partial_in.reshape(slot_total, seg, vec_count)
    summed = well_sums(well_slot.reshape(-1), partial_in, wells)
    well_state = well_states_of(summed, well_inverse, well_count)
    state_pack = well_state[slot_well].reshape(dom_count, slot_width, seg, vec_count)
    state_in = lax.all_to_all(state_pack, "dom", split_axis=0, concat_axis=0, tiled=True)
    state_in = state_in.reshape(slot_total, seg, vec_count)
    live_halo = (jnp.arange(halo_width)[None, :] < halo_counts[0][:, None]).astype(jnp.int32)
    live = jnp.concatenate(
        [jnp.ones((blocks.shape[0],), jnp.int32), live_halo.reshape(-1), jnp.ones((2 * rim_width,), jnp.int32)]
    )
    extended = ext_frame.reshape(ext_slots * halo_width, cell_count, vec_count)
    extended = lax.dynamic_update_slice_in_dim(extended, blocks, 0, 0)
    extended = lax.dynamic_update_slice_in_dim(extended, rim_rows, extended.shape[0] - 2 * rim_width, 0)
    product = local_product(extended, live, tile_values, tile_cols)
    incoming = jnp.einsum(
        "qsk,qsv->qkv",
        out_recv.reshape(slot_total, seg, cell_count),
        state_in,
        preferred_element_type=jnp.float32,
    ).astype(jnp.bfloat16)
    return subtract_incoming(product, well_send, incoming).astype(jnp.bfloat16)


def solution(mesh):
    in_specs = (
        P(("dom", "grp"), None, None),
        P(("dom", "grp"), None, None, None),
        P(("dom", "grp"), None),
        P(("dom", "grp"), None, None),
        P(("dom", "grp"), None),
        P(("dom", "grp"), None, None),
        P(("dom", "grp"), None, None),
        P(("dom", "grp"), None),
        P(("dom", "grp")),
        P(("dom", "grp"), None, None, None),
        P(("dom", "grp"), None, None, None),
        P(("dom", "grp"), None, None),
    )
    out_specs = P(("dom", "grp"), None, None)
    return jax.shard_map(
        on_device, mesh=mesh, in_specs=in_specs, out_specs=out_specs, check_vma=False
    )
```

```python
import functools

import jax
import jax.numpy as jnp
from jax import lax
from jax.sharding import PartitionSpec as P
from jax.experimental import pallas as pl
from jax.experimental.pallas import tpu as pltpu


def padded(value, sides, width):
    for axis, dim in sides:
        devices, length = (lax.axis_size(axis), value.shape[dim])
        up = [(i, (i + 1) % devices) for i in range(devices - 1)]
        down = [(j, i) for i, j in up]
        last = lax.slice_in_dim(value, length - width, length, axis=dim)
        leading = lax.slice_in_dim(value, 0, width, axis=dim)
        before = lax.ppermute(last, axis, up)
        after = lax.ppermute(leading, axis, down)
        value = jnp.concatenate([before, value, after], axis=dim)
    return value


def product_kernel(cols_ref, live_ref, ext_ref, tiles_ref, out_ref):
    rows, tiles_per_row = tiles_ref.shape[0], tiles_ref.shape[1]
    first = pl.program_id(0) * rows
    for r in range(rows):
        acc = None
        for t in range(0, tiles_per_row, 2):
            pair = [cols_ref[(first + r) * tiles_per_row + t + u] for u in range(2)]
            lhs = jnp.concatenate(
                [tiles_ref[r, t + u] * live_ref[pair[u]].astype(tiles_ref.dtype) for u in range(2)], axis=1
            )
            rhs = jnp.concatenate([ext_ref[c] for c in pair], axis=0)
            term = jnp.dot(lhs, rhs, preferred_element_type=jnp.float32)
            acc = term if acc is None else acc + term
        out_ref[r] = acc


def local_product(extended, live, tile_values, tile_cols):
    block_rows, tiles_per_row, cells, _ = tile_values.shape
    ext_blocks, _, vecs = extended.shape
    rows = 16
    grid_spec = pltpu.PrefetchScalarGridSpec(
        num_scalar_prefetch=2,
        grid=(block_rows // rows,),
        in_specs=[
            pl.BlockSpec((ext_blocks, cells, vecs), lambda k, cols, live: (0, 0, 0)),
            pl.BlockSpec((rows, tiles_per_row, cells, cells), lambda k, cols, live: (k, 0, 0, 0)),
        ],
        out_specs=pl.BlockSpec((rows, cells, vecs), lambda k, cols, live: (k, 0, 0)),
    )
    flops = 2 * block_rows * tiles_per_row * cells * cells * vecs
    moved = tile_values.size * 2 + extended.size * 2 + block_rows * cells * vecs * 4
    return pl.pallas_call(
        product_kernel,
        out_shape=jax.ShapeDtypeStruct((block_rows, cells, vecs), jnp.float32),
        grid_spec=grid_spec,
        cost_estimate=pl.CostEstimate(flops=flops, transcendentals=0, bytes_accessed=moved),
    )(tile_cols.reshape(-1), live, extended, tile_values)


def sums_kernel(slot_ref, partial_ref, out_ref):
    couplings = slot_ref.shape[0] // out_ref.shape[0]
    for w in range(out_ref.shape[0]):
        acc = partial_ref[slot_ref[w * couplings]]
        for c in range(1, couplings):
            acc = acc + partial_ref[slot_ref[w * couplings + c]]
        out_ref[w] = acc


def well_sums(slots, partial, wells):
    vmem = pl.BlockSpec(memory_space=pltpu.VMEM)
    return pl.pallas_call(
        sums_kernel,
        out_shape=jax.ShapeDtypeStruct((wells,) + partial.shape[1:], jnp.float32),
        in_specs=[pl.BlockSpec(memory_space=pltpu.SMEM), vmem],
        out_specs=vmem,
    )(slots, partial)


def partial_kernel(index_ref, couple_ref, blocks_ref, out_ref):
    for q in range(out_ref.shape[0]):
        out_ref[q] = jnp.dot(
            couple_ref[q][:, : blocks_ref.shape[1]], blocks_ref[index_ref[q]], preferred_element_type=jnp.float32
        )


def partial_sums(index, couple, blocks):
    slots, seg, _ = couple.shape
    vmem = pl.BlockSpec(memory_space=pltpu.VMEM)
    return pl.pallas_call(
        partial_kernel,
        out_shape=jax.ShapeDtypeStruct((slots, seg, blocks.shape[2]), jnp.float32),
        in_specs=[pl.BlockSpec(memory_space=pltpu.SMEM), vmem, vmem],
        out_specs=vmem,
    )(index, couple, blocks)


SIDE = 4
NEAR = ((1, 0), (3, 0), (0, 1), (0, 3), (1, 1), (1, 3), (3, 1), (3, 3))
RELAYED = (
    ((2, 0), (1, 0), 0), ((2, 0), (3, 0), 1),
    ((2, 1), (1, 0), 0), ((2, 1), (3, 0), 1),
    ((2, 3), (1, 0), 0), ((2, 3), (3, 0), 1),
    ((0, 2), (0, 1), 0), ((0, 2), (0, 3), 1),
    ((1, 2), (0, 1), 0), ((1, 2), (0, 3), 1),
    ((3, 2), (0, 1), 0), ((3, 2), (0, 3), 1),
    ((2, 2), (1, 1), 0), ((2, 2), (3, 3), 1),
)


def exchange_kernel(offsets, *refs):
    parts = (len(refs) - 7) // 3
    send_refs, recv_refs, relay_refs = refs[:parts], refs[parts : 2 * parts], refs[2 * parts : 3 * parts]
    near_send, near_recv, leg_send, leg_recv, fwd_send, fwd_recv, own_sems = refs[3 * parts :]
    me = lax.axis_index("dom")
    grp = lax.axis_index("grp")
    row, col = me // SIDE, me % SIDE

    def at(offset):
        return ((row + offset[0]) % SIDE) * SIDE + (col + offset[1]) % SIDE

    def remote(src, dst, send_sem, recv_sem, offset):
        return pltpu.make_async_remote_copy(
            src_ref=src, dst_ref=dst, send_sem=send_sem, recv_sem=recv_sem,
            device_id=(at(offset), grp), device_id_type=pl.DeviceIdType.MESH,
        )

    barrier = pltpu.get_barrier_semaphore()
    for offset in NEAR:
        pl.semaphore_signal(
            barrier, inc=1, device_id=(at(offset), grp), device_id_type=pl.DeviceIdType.MESH
        )
    pl.semaphore_wait(barrier, len(NEAR))
    owns = []
    for p in range(parts):
        own = pltpu.make_async_copy(send_refs[p].at[me], recv_refs[p].at[offsets[p] + me], own_sems.at[p])
        own.start()
        owns.append(own)
    legs = []
    for k, (target, relay, part) in enumerate(RELAYED):
        for p in range(parts):
            half = send_refs[p].shape[1] // 2
            leg = remote(send_refs[p].at[at(target), pl.ds(part * half, half)], relay_refs[p].at[k],
                         leg_send.at[p, k], leg_recv.at[p, k], relay)
            leg.start()
            legs.append(leg)
    nears = []
    for k, offset in enumerate(NEAR):
        for p in range(parts):
            near = remote(send_refs[p].at[at(offset)], recv_refs[p].at[offsets[p] + me],
                          near_send.at[p, k], near_recv.at[p, k], offset)
            near.start()
            nears.append(near)
    fwds = []
    for k, (target, relay, part) in enumerate(RELAYED):
        source = at(((SIDE - relay[0]) % SIDE, (SIDE - relay[1]) % SIDE))
        onward = ((target[0] - relay[0]) % SIDE, (target[1] - relay[1]) % SIDE)
        for p in range(parts):
            half = send_refs[p].shape[1] // 2
            legs[k * parts + p].wait_recv()
            fwd = remote(relay_refs[p].at[k], recv_refs[p].at[offsets[p] + source, pl.ds(part * half, half)],
                         fwd_send.at[p, k], fwd_recv.at[p, k], onward)
            fwd.start()
            fwds.append(fwd)
    for leg in legs:
        leg.wait_send()
    for near in nears:
        near.wait_send()
    for near in nears:
        near.wait_recv()
    for fwd in fwds:
        fwd.wait_send()
    for fwd in fwds:
        fwd.wait_recv()
    for own in owns:
        own.wait()


def dom_exchange(values, collective, frames=None):
    parts = len(values)
    frames = frames or [(0, v.shape[0]) for v in values]
    outs = [jax.ShapeDtypeStruct((n,) + v.shape[1:], v.dtype) for v, (_, n) in zip(values, frames)]
    relays = [jax.ShapeDtypeStruct((len(RELAYED), v.shape[1] // 2, v.shape[2]), v.dtype) for v in values]
    any_spec = pl.BlockSpec(memory_space=pl.ANY)
    result = pl.pallas_call(
        functools.partial(exchange_kernel, tuple(f[0] for f in frames)),
        out_shape=tuple(outs + relays),
        in_specs=[any_spec] * parts,
        out_specs=tuple([any_spec] * (2 * parts)),
        scratch_shapes=[
            pltpu.SemaphoreType.DMA((parts, len(NEAR))),
            pltpu.SemaphoreType.DMA((parts, len(NEAR))),
            pltpu.SemaphoreType.DMA((parts, len(RELAYED))),
            pltpu.SemaphoreType.DMA((parts, len(RELAYED))),
            pltpu.SemaphoreType.DMA((parts, len(RELAYED))),
            pltpu.SemaphoreType.DMA((parts, len(RELAYED))),
            pltpu.SemaphoreType.DMA((parts,)),
        ],
        compiler_params=pltpu.CompilerParams(collective_id=collective, has_side_effects=True),
    )(*values)
    return result[:parts]


def well_states_of(summed, well_inverse, well_count):
    wells = summed.shape[0]
    live_mask = (jnp.arange(wells) < well_count[0]).astype(jnp.float32)
    solved = jnp.einsum("wst,wtv->wsv", well_inverse, summed, precision=lax.Precision.HIGHEST)
    return (solved * live_mask[:, None, None]).astype(jnp.bfloat16)


def subtract_incoming(product, well_send, incoming):
    targets = well_send[0].reshape(-1)
    selector = (targets[None, :] == jnp.arange(product.shape[0])[:, None]).astype(jnp.bfloat16)
    flat_rows = incoming.reshape(targets.shape[0], product.shape[1], product.shape[2])
    return product - jnp.einsum(
        "bq,qkv->bkv", selector, flat_rows, preferred_element_type=jnp.float32
    )


def on_device(
    blocks,
    tile_values,
    tile_cols,
    halo_send,
    halo_counts,
    grp_send,
    well_send,
    well_slot,
    well_count,
    couple_in,
    couple_out,
    well_inverse,
):
    dom_count = lax.axis_size("dom")
    halo_width = halo_send.shape[2]
    rim_width = grp_send.shape[2]
    slot_width = well_send.shape[2]
    cell_count = blocks.shape[1]
    vec_count = blocks.shape[2]
    wells, couplings = well_slot.shape
    seg = couple_in.shape[2]
    slot_total = dom_count * slot_width
    halo_pack = blocks[halo_send[0]]
    rim_pack = blocks[grp_send[0].reshape(-1)]
    rim_ext = padded(rim_pack, (("grp", 0),), rim_width)
    rim_rows = jnp.concatenate([rim_ext[:rim_width], rim_ext[rim_ext.shape[0] - rim_width :]], 0)
    slot_flat = well_slot.reshape(-1)
    slot_order = jnp.zeros_like(slot_flat).at[slot_flat].set(jnp.arange(slot_flat.shape[0], dtype=slot_flat.dtype))
    slot_well = slot_order // couplings
    couple_both = jnp.concatenate(
        [couple_in.reshape(wells * couplings, seg, cell_count), couple_out.reshape(wells * couplings, seg, cell_count)], 2
    )[slot_order]
    halo_flat = halo_pack.reshape(dom_count, halo_width * cell_count, vec_count)
    (both_recv,) = dom_exchange([couple_both.reshape(dom_count, slot_width * seg, 2 * cell_count)], 0)
    both_recv = both_recv.reshape(slot_total, seg, 2 * cell_count)
    out_recv = both_recv[:, :, cell_count:]
    partial = partial_sums(well_send[0].reshape(-1), both_recv, blocks).reshape(dom_count, slot_width, seg, vec_count)
    partial_in = lax.all_to_all(partial, "dom", split_axis=0, concat_axis=0, tiled=True)
    own_slots = blocks.shape[0] // halo_width
    ext_slots = own_slots + dom_count + 2 * rim_width // halo_width
    (ext_frame,) = dom_exchange([halo_flat], 1, [(own_slots, ext_slots)])
    partial_in, ext_frame = lax.optimization_barrier((partial_in, ext_frame))
    partial_in = partial_in.reshape(slot_total, seg, vec_count)
    summed = well_sums(well_slot.reshape(-1), partial_in, wells)
    well_state = well_states_of(summed, well_inverse, well_count)
    state_pack = well_state[slot_well].reshape(dom_count, slot_width, seg, vec_count)
    state_in = lax.all_to_all(state_pack, "dom", split_axis=0, concat_axis=0, tiled=True)
    state_in = state_in.reshape(slot_total, seg, vec_count)
    live_halo = (jnp.arange(halo_width)[None, :] < halo_counts[0][:, None]).astype(jnp.int32)
    live = jnp.concatenate(
        [jnp.ones((blocks.shape[0],), jnp.int32), live_halo.reshape(-1), jnp.ones((2 * rim_width,), jnp.int32)]
    )
    extended = ext_frame.reshape(ext_slots * halo_width, cell_count, vec_count)
    extended = lax.dynamic_update_slice_in_dim(extended, blocks, 0, 0)
    extended = lax.dynamic_update_slice_in_dim(extended, rim_rows, extended.shape[0] - 2 * rim_width, 0)
    product = local_product(extended, live, tile_values, tile_cols)
    incoming = jnp.einsum(
        "qsk,qsv->qkv",
        out_recv.reshape(slot_total, seg, cell_count),
        state_in,
        preferred_element_type=jnp.float32,
    ).astype(jnp.bfloat16)
    return subtract_incoming(product, well_send, incoming).astype(jnp.bfloat16)


def solution(mesh):
    in_specs = (
        P(("dom", "grp"), None, None),
        P(("dom", "grp"), None, None, None),
        P(("dom", "grp"), None),
        P(("dom", "grp"), None, None),
        P(("dom", "grp"), None),
        P(("dom", "grp"), None, None),
        P(("dom", "grp"), None, None),
        P(("dom", "grp"), None),
        P(("dom", "grp")),
        P(("dom", "grp"), None, None, None),
        P(("dom", "grp"), None, None, None),
        P(("dom", "grp"), None, None),
    )
    out_specs = P(("dom", "grp"), None, None)
    return jax.shard_map(
        on_device, mesh=mesh, in_specs=in_specs, out_specs=out_specs, check_vma=False
    )
```

```python
import functools

import jax
import jax.numpy as jnp
from jax import lax
from jax.sharding import PartitionSpec as P
from jax.experimental import pallas as pl
from jax.experimental.pallas import tpu as pltpu


def padded(value, sides, width):
    for axis, dim in sides:
        devices, length = (lax.axis_size(axis), value.shape[dim])
        up = [(i, (i + 1) % devices) for i in range(devices - 1)]
        down = [(j, i) for i, j in up]
        last = lax.slice_in_dim(value, length - width, length, axis=dim)
        leading = lax.slice_in_dim(value, 0, width, axis=dim)
        before = lax.ppermute(last, axis, up)
        after = lax.ppermute(leading, axis, down)
        value = jnp.concatenate([before, value, after], axis=dim)
    return value


def product_kernel(cols_ref, live_ref, ext_ref, tiles_ref, out_ref):
    rows, tiles_per_row = tiles_ref.shape[0], tiles_ref.shape[1]
    first = pl.program_id(0) * rows
    for r in range(rows):
        acc = None
        for t in range(0, tiles_per_row, 2):
            pair = [cols_ref[(first + r) * tiles_per_row + t + u] for u in range(2)]
            lhs = jnp.concatenate(
                [tiles_ref[r, t + u] * live_ref[pair[u]].astype(tiles_ref.dtype) for u in range(2)], axis=1
            )
            rhs = jnp.concatenate([ext_ref[c] for c in pair], axis=0)
            term = jnp.dot(lhs, rhs, preferred_element_type=jnp.float32)
            acc = term if acc is None else acc + term
        out_ref[r] = acc


def local_product(extended, live, tile_values, tile_cols):
    block_rows, tiles_per_row, cells, _ = tile_values.shape
    ext_blocks, _, vecs = extended.shape
    rows = 16
    grid_spec = pltpu.PrefetchScalarGridSpec(
        num_scalar_prefetch=2,
        grid=(block_rows // rows,),
        in_specs=[
            pl.BlockSpec((ext_blocks, cells, vecs), lambda k, cols, live: (0, 0, 0)),
            pl.BlockSpec((rows, tiles_per_row, cells, cells), lambda k, cols, live: (k, 0, 0, 0)),
        ],
        out_specs=pl.BlockSpec((rows, cells, vecs), lambda k, cols, live: (k, 0, 0)),
    )
    flops = 2 * block_rows * tiles_per_row * cells * cells * vecs
    moved = tile_values.size * 2 + extended.size * 2 + block_rows * cells * vecs * 4
    return pl.pallas_call(
        product_kernel,
        out_shape=jax.ShapeDtypeStruct((block_rows, cells, vecs), jnp.float32),
        grid_spec=grid_spec,
        cost_estimate=pl.CostEstimate(flops=flops, transcendentals=0, bytes_accessed=moved),
    )(tile_cols.reshape(-1), live, extended, tile_values)


def sums_kernel(slot_ref, partial_ref, out_ref):
    couplings = slot_ref.shape[0] // out_ref.shape[0]
    for w in range(out_ref.shape[0]):
        acc = partial_ref[slot_ref[w * couplings]]
        for c in range(1, couplings):
            acc = acc + partial_ref[slot_ref[w * couplings + c]]
        out_ref[w] = acc


def well_sums(slots, partial, wells):
    vmem = pl.BlockSpec(memory_space=pltpu.VMEM)
    return pl.pallas_call(
        sums_kernel,
        out_shape=jax.ShapeDtypeStruct((wells,) + partial.shape[1:], jnp.float32),
        in_specs=[pl.BlockSpec(memory_space=pltpu.SMEM), vmem],
        out_specs=vmem,
    )(slots, partial)


def partial_kernel(index_ref, couple_ref, blocks_ref, out_ref):
    for q in range(out_ref.shape[0]):
        out_ref[q] = jnp.dot(
            couple_ref[q][:, : blocks_ref.shape[1]], blocks_ref[index_ref[q]], preferred_element_type=jnp.float32
        )


def partial_sums(index, couple, blocks):
    slots, seg, _ = couple.shape
    vmem = pl.BlockSpec(memory_space=pltpu.VMEM)
    return pl.pallas_call(
        partial_kernel,
        out_shape=jax.ShapeDtypeStruct((slots, seg, blocks.shape[2]), jnp.float32),
        in_specs=[pl.BlockSpec(memory_space=pltpu.SMEM), vmem, vmem],
        out_specs=vmem,
    )(index, couple, blocks)


SIDE = 4
NEAR = ((1, 0), (3, 0), (0, 1), (0, 3), (1, 1), (1, 3), (3, 1), (3, 3))
RELAYED = (
    ((2, 0), (1, 0), 0), ((2, 0), (3, 0), 1),
    ((2, 1), (1, 0), 0), ((2, 1), (3, 0), 1),
    ((2, 3), (1, 0), 0), ((2, 3), (3, 0), 1),
    ((0, 2), (0, 1), 0), ((0, 2), (0, 3), 1),
    ((1, 2), (0, 1), 0), ((1, 2), (0, 3), 1),
    ((3, 2), (0, 1), 0), ((3, 2), (0, 3), 1),
    ((2, 2), (1, 1), 0), ((2, 2), (3, 3), 1),
)


def exchange_kernel(offsets, local, *refs):
    if local:
        local_ref, refs = refs[0], refs[1:]
    parts = (len(refs) - 7) // 3
    send_refs, recv_refs, relay_refs = refs[:parts], refs[parts : 2 * parts], refs[2 * parts : 3 * parts]
    near_send, near_recv, leg_send, leg_recv, fwd_send, fwd_recv, own_sems = refs[3 * parts :]
    me = lax.axis_index("dom")
    grp = lax.axis_index("grp")
    row, col = me // SIDE, me % SIDE

    def at(offset):
        return ((row + offset[0]) % SIDE) * SIDE + (col + offset[1]) % SIDE

    def remote(src, dst, send_sem, recv_sem, offset):
        return pltpu.make_async_remote_copy(
            src_ref=src, dst_ref=dst, send_sem=send_sem, recv_sem=recv_sem,
            device_id=(at(offset), grp), device_id_type=pl.DeviceIdType.MESH,
        )

    barrier = pltpu.get_barrier_semaphore()
    for offset in NEAR:
        pl.semaphore_signal(
            barrier, inc=1, device_id=(at(offset), grp), device_id_type=pl.DeviceIdType.MESH
        )
    pl.semaphore_wait(barrier, len(NEAR))
    owns = []
    if local:
        own = pltpu.make_async_copy(local_ref, recv_refs[0].at[pl.ds(0, local_ref.shape[0])], own_sems.at[parts])
        own.start()
        owns.append(own)
    for p in range(parts):
        own = pltpu.make_async_copy(send_refs[p].at[me], recv_refs[p].at[offsets[p] + me], own_sems.at[p])
        own.start()
        owns.append(own)
    legs = []
    for k, (target, relay, part) in enumerate(RELAYED):
        for p in range(parts):
            half = send_refs[p].shape[1] // 2
            leg = remote(send_refs[p].at[at(target), pl.ds(part * half, half)], relay_refs[p].at[k],
                         leg_send.at[p, k], leg_recv.at[p, k], relay)
            leg.start()
            legs.append(leg)
    nears = []
    for k, offset in enumerate(NEAR):
        for p in range(parts):
            near = remote(send_refs[p].at[at(offset)], recv_refs[p].at[offsets[p] + me],
                          near_send.at[p, k], near_recv.at[p, k], offset)
            near.start()
            nears.append(near)
    fwds = []
    for k, (target, relay, part) in enumerate(RELAYED):
        source = at(((SIDE - relay[0]) % SIDE, (SIDE - relay[1]) % SIDE))
        onward = ((target[0] - relay[0]) % SIDE, (target[1] - relay[1]) % SIDE)
        for p in range(parts):
            half = send_refs[p].shape[1] // 2
            legs[k * parts + p].wait_recv()
            fwd = remote(relay_refs[p].at[k], recv_refs[p].at[offsets[p] + source, pl.ds(part * half, half)],
                         fwd_send.at[p, k], fwd_recv.at[p, k], onward)
            fwd.start()
            fwds.append(fwd)
    for leg in legs:
        leg.wait_send()
    for near in nears:
        near.wait_send()
    for near in nears:
        near.wait_recv()
    for fwd in fwds:
        fwd.wait_send()
    for fwd in fwds:
        fwd.wait_recv()
    for own in owns:
        own.wait()


def dom_exchange(values, collective, frames=None, local=None):
    parts = len(values)
    lead = [] if local is None else [local]
    frames = frames or [(0, v.shape[0]) for v in values]
    outs = [jax.ShapeDtypeStruct((n,) + v.shape[1:], v.dtype) for v, (_, n) in zip(values, frames)]
    relays = [jax.ShapeDtypeStruct((len(RELAYED), v.shape[1] // 2, v.shape[2]), v.dtype) for v in values]
    any_spec = pl.BlockSpec(memory_space=pl.ANY)
    result = pl.pallas_call(
        functools.partial(exchange_kernel, tuple(f[0] for f in frames), local is not None),
        out_shape=tuple(outs + relays),
        in_specs=[any_spec] * (parts + len(lead)),
        out_specs=tuple([any_spec] * (2 * parts)),
        scratch_shapes=[
            pltpu.SemaphoreType.DMA((parts, len(NEAR))),
            pltpu.SemaphoreType.DMA((parts, len(NEAR))),
            pltpu.SemaphoreType.DMA((parts, len(RELAYED))),
            pltpu.SemaphoreType.DMA((parts, len(RELAYED))),
            pltpu.SemaphoreType.DMA((parts, len(RELAYED))),
            pltpu.SemaphoreType.DMA((parts, len(RELAYED))),
            pltpu.SemaphoreType.DMA((parts + len(lead),)),
        ],
        compiler_params=pltpu.CompilerParams(collective_id=collective, has_side_effects=True),
    )(*lead, *values)
    return result[:parts]


def well_states_of(summed, well_inverse, well_count):
    wells = summed.shape[0]
    live_mask = (jnp.arange(wells) < well_count[0]).astype(jnp.float32)
    solved = jnp.einsum("wst,wtv->wsv", well_inverse, summed, precision=lax.Precision.HIGHEST)
    return (solved * live_mask[:, None, None]).astype(jnp.bfloat16)


def subtract_incoming(product, well_send, incoming):
    targets = well_send[0].reshape(-1)
    selector = (targets[None, :] == jnp.arange(product.shape[0])[:, None]).astype(jnp.bfloat16)
    flat_rows = incoming.reshape(targets.shape[0], product.shape[1], product.shape[2])
    return product - jnp.einsum(
        "bq,qkv->bkv", selector, flat_rows, preferred_element_type=jnp.float32
    )


def on_device(
    blocks,
    tile_values,
    tile_cols,
    halo_send,
    halo_counts,
    grp_send,
    well_send,
    well_slot,
    well_count,
    couple_in,
    couple_out,
    well_inverse,
):
    dom_count = lax.axis_size("dom")
    halo_width = halo_send.shape[2]
    rim_width = grp_send.shape[2]
    slot_width = well_send.shape[2]
    cell_count = blocks.shape[1]
    vec_count = blocks.shape[2]
    wells, couplings = well_slot.shape
    seg = couple_in.shape[2]
    slot_total = dom_count * slot_width
    halo_pack = blocks[halo_send[0]]
    rim_pack = blocks[grp_send[0].reshape(-1)]
    rim_ext = padded(rim_pack, (("grp", 0),), rim_width)
    rim_rows = jnp.concatenate([rim_ext[:rim_width], rim_ext[rim_ext.shape[0] - rim_width :]], 0)
    slot_flat = well_slot.reshape(-1)
    slot_order = jnp.zeros_like(slot_flat).at[slot_flat].set(jnp.arange(slot_flat.shape[0], dtype=slot_flat.dtype))
    slot_well = slot_order // couplings
    couple_both = jnp.concatenate(
        [couple_in.reshape(wells * couplings, seg, cell_count), couple_out.reshape(wells * couplings, seg, cell_count)], 2
    )[slot_order]
    halo_flat = halo_pack.reshape(dom_count, halo_width * cell_count, vec_count)
    (both_recv,) = dom_exchange([couple_both.reshape(dom_count, slot_width * seg, 2 * cell_count)], 0)
    both_recv = both_recv.reshape(slot_total, seg, 2 * cell_count)
    out_recv = both_recv[:, :, cell_count:]
    partial = partial_sums(well_send[0].reshape(-1), both_recv, blocks).reshape(dom_count, slot_width, seg, vec_count)
    partial_in = lax.all_to_all(partial, "dom", split_axis=0, concat_axis=0, tiled=True)
    own_slots = blocks.shape[0] // halo_width
    ext_slots = own_slots + dom_count + 2 * rim_width // halo_width
    own_frame = blocks.reshape(own_slots, halo_width * cell_count, vec_count)
    (ext_frame,) = dom_exchange([halo_flat], 1, [(own_slots, ext_slots)], own_frame)
    partial_in, ext_frame = lax.optimization_barrier((partial_in, ext_frame))
    partial_in = partial_in.reshape(slot_total, seg, vec_count)
    summed = well_sums(well_slot.reshape(-1), partial_in, wells)
    well_state = well_states_of(summed, well_inverse, well_count)
    state_pack = well_state[slot_well].reshape(dom_count, slot_width, seg, vec_count)
    state_in = lax.all_to_all(state_pack, "dom", split_axis=0, concat_axis=0, tiled=True)
    state_in = state_in.reshape(slot_total, seg, vec_count)
    live_halo = (jnp.arange(halo_width)[None, :] < halo_counts[0][:, None]).astype(jnp.int32)
    live = jnp.concatenate(
        [jnp.ones((blocks.shape[0],), jnp.int32), live_halo.reshape(-1), jnp.ones((2 * rim_width,), jnp.int32)]
    )
    extended = ext_frame.reshape(ext_slots * halo_width, cell_count, vec_count)
    extended = lax.dynamic_update_slice_in_dim(extended, rim_rows, extended.shape[0] - 2 * rim_width, 0)
    product = local_product(extended, live, tile_values, tile_cols)
    incoming = jnp.einsum(
        "qsk,qsv->qkv",
        out_recv.reshape(slot_total, seg, cell_count),
        state_in,
        preferred_element_type=jnp.float32,
    ).astype(jnp.bfloat16)
    return subtract_incoming(product, well_send, incoming).astype(jnp.bfloat16)


def solution(mesh):
    in_specs = (
        P(("dom", "grp"), None, None),
        P(("dom", "grp"), None, None, None),
        P(("dom", "grp"), None),
        P(("dom", "grp"), None, None),
        P(("dom", "grp"), None),
        P(("dom", "grp"), None, None),
        P(("dom", "grp"), None, None),
        P(("dom", "grp"), None),
        P(("dom", "grp")),
        P(("dom", "grp"), None, None, None),
        P(("dom", "grp"), None, None, None),
        P(("dom", "grp"), None, None),
    )
    out_specs = P(("dom", "grp"), None, None)
    return jax.shard_map(
        on_device, mesh=mesh, in_specs=in_specs, out_specs=out_specs, check_vma=False
    )
```

```python
import functools

import jax
import jax.numpy as jnp
from jax import lax
from jax.sharding import PartitionSpec as P
from jax.experimental import pallas as pl
from jax.experimental.pallas import tpu as pltpu


def padded(value, sides, width):
    for axis, dim in sides:
        devices, length = (lax.axis_size(axis), value.shape[dim])
        up = [(i, (i + 1) % devices) for i in range(devices - 1)]
        down = [(j, i) for i, j in up]
        last = lax.slice_in_dim(value, length - width, length, axis=dim)
        leading = lax.slice_in_dim(value, 0, width, axis=dim)
        before = lax.ppermute(last, axis, up)
        after = lax.ppermute(leading, axis, down)
        value = jnp.concatenate([before, value, after], axis=dim)
    return value


def product_kernel(cols_ref, live_ref, ext_ref, tiles_ref, out_ref):
    rows, tiles_per_row = tiles_ref.shape[0], tiles_ref.shape[1]
    first = pl.program_id(0) * rows
    for r in range(rows):
        acc = None
        for t in range(0, tiles_per_row, 2):
            pair = [cols_ref[(first + r) * tiles_per_row + t + u] for u in range(2)]
            lhs = jnp.concatenate(
                [tiles_ref[r, t + u] * live_ref[pair[u]].astype(tiles_ref.dtype) for u in range(2)], axis=1
            )
            rhs = jnp.concatenate([ext_ref[c] for c in pair], axis=0)
            term = jnp.dot(lhs, rhs, preferred_element_type=jnp.float32)
            acc = term if acc is None else acc + term
        out_ref[r] = acc


def local_product(extended, live, tile_values, tile_cols):
    block_rows, tiles_per_row, cells, _ = tile_values.shape
    ext_blocks, _, vecs = extended.shape
    rows = 16
    grid_spec = pltpu.PrefetchScalarGridSpec(
        num_scalar_prefetch=2,
        grid=(block_rows // rows,),
        in_specs=[
            pl.BlockSpec((ext_blocks, cells, vecs), lambda k, cols, live: (0, 0, 0)),
            pl.BlockSpec((rows, tiles_per_row, cells, cells), lambda k, cols, live: (k, 0, 0, 0)),
        ],
        out_specs=pl.BlockSpec((rows, cells, vecs), lambda k, cols, live: (k, 0, 0)),
    )
    flops = 2 * block_rows * tiles_per_row * cells * cells * vecs
    moved = tile_values.size * 2 + extended.size * 2 + block_rows * cells * vecs * 4
    return pl.pallas_call(
        product_kernel,
        out_shape=jax.ShapeDtypeStruct((block_rows, cells, vecs), jnp.float32),
        grid_spec=grid_spec,
        cost_estimate=pl.CostEstimate(flops=flops, transcendentals=0, bytes_accessed=moved),
    )(tile_cols.reshape(-1), live, extended, tile_values)


def sums_kernel(slot_ref, partial_ref, out_ref):
    couplings = slot_ref.shape[0] // out_ref.shape[0]
    for w in range(out_ref.shape[0]):
        acc = partial_ref[slot_ref[w * couplings]]
        for c in range(1, couplings):
            acc = acc + partial_ref[slot_ref[w * couplings + c]]
        out_ref[w] = acc


def well_sums(slots, partial, wells):
    vmem = pl.BlockSpec(memory_space=pltpu.VMEM)
    return pl.pallas_call(
        sums_kernel,
        out_shape=jax.ShapeDtypeStruct((wells,) + partial.shape[1:], jnp.float32),
        in_specs=[pl.BlockSpec(memory_space=pltpu.SMEM), vmem],
        out_specs=vmem,
    )(slots, partial)


def partial_kernel(index_ref, couple_ref, blocks_ref, out_ref):
    for q in range(out_ref.shape[0]):
        out_ref[q] = jnp.dot(
            couple_ref[q][:, : blocks_ref.shape[1]], blocks_ref[index_ref[q]], preferred_element_type=jnp.float32
        )


def partial_sums(index, couple, blocks):
    slots, seg, _ = couple.shape
    vmem = pl.BlockSpec(memory_space=pltpu.VMEM)
    return pl.pallas_call(
        partial_kernel,
        out_shape=jax.ShapeDtypeStruct((slots, seg, blocks.shape[2]), jnp.float32),
        in_specs=[pl.BlockSpec(memory_space=pltpu.SMEM), vmem, vmem],
        out_specs=vmem,
    )(index, couple, blocks)


SIDE = 4
NEAR = ((1, 0), (3, 0), (0, 1), (0, 3), (1, 1), (1, 3), (3, 1), (3, 3))
RELAYED = (
    ((2, 0), (1, 0), 0), ((2, 0), (3, 0), 1),
    ((2, 1), (1, 0), 0), ((2, 1), (3, 0), 1),
    ((2, 3), (1, 0), 0), ((2, 3), (3, 0), 1),
    ((0, 2), (0, 1), 0), ((0, 2), (0, 3), 1),
    ((1, 2), (0, 1), 0), ((1, 2), (0, 3), 1),
    ((3, 2), (0, 1), 0), ((3, 2), (0, 3), 1),
    ((2, 2), (1, 1), 0), ((2, 2), (3, 3), 1),
)


def exchange_kernel(offsets, *refs):
    parts = (len(refs) - 7) // 3
    send_refs, recv_refs, relay_refs = refs[:parts], refs[parts : 2 * parts], refs[2 * parts : 3 * parts]
    near_send, near_recv, leg_send, leg_recv, fwd_send, fwd_recv, own_sems = refs[3 * parts :]
    me = lax.axis_index("dom")
    grp = lax.axis_index("grp")
    row, col = me // SIDE, me % SIDE

    def at(offset):
        return ((row + offset[0]) % SIDE) * SIDE + (col + offset[1]) % SIDE

    def remote(src, dst, send_sem, recv_sem, offset):
        return pltpu.make_async_remote_copy(
            src_ref=src, dst_ref=dst, send_sem=send_sem, recv_sem=recv_sem,
            device_id=(at(offset), grp), device_id_type=pl.DeviceIdType.MESH,
        )

    barrier = pltpu.get_barrier_semaphore()
    for offset in NEAR:
        pl.semaphore_signal(
            barrier, inc=1, device_id=(at(offset), grp), device_id_type=pl.DeviceIdType.MESH
        )
    pl.semaphore_wait(barrier, len(NEAR))
    owns = []
    for p in range(parts):
        own = pltpu.make_async_copy(send_refs[p].at[me], recv_refs[p].at[offsets[p] + me], own_sems.at[p])
        own.start()
        owns.append(own)
    legs = []
    for k, (target, relay, part) in enumerate(RELAYED):
        for p in range(parts):
            half = send_refs[p].shape[1] // 2
            leg = remote(send_refs[p].at[at(target), pl.ds(part * half, half)], relay_refs[p].at[k],
                         leg_send.at[p, k], leg_recv.at[p, k], relay)
            leg.start()
            legs.append(leg)
    nears = []
    for k, offset in enumerate(NEAR):
        for p in range(parts):
            near = remote(send_refs[p].at[at(offset)], recv_refs[p].at[offsets[p] + me],
                          near_send.at[p, k], near_recv.at[p, k], offset)
            near.start()
            nears.append(near)
    fwds = []
    for k, (target, relay, part) in enumerate(RELAYED):
        source = at(((SIDE - relay[0]) % SIDE, (SIDE - relay[1]) % SIDE))
        onward = ((target[0] - relay[0]) % SIDE, (target[1] - relay[1]) % SIDE)
        for p in range(parts):
            half = send_refs[p].shape[1] // 2
            legs[k * parts + p].wait_recv()
            fwd = remote(relay_refs[p].at[k], recv_refs[p].at[offsets[p] + source, pl.ds(part * half, half)],
                         fwd_send.at[p, k], fwd_recv.at[p, k], onward)
            fwd.start()
            fwds.append(fwd)
    for leg in legs:
        leg.wait_send()
    for near in nears:
        near.wait_send()
    for near in nears:
        near.wait_recv()
    for fwd in fwds:
        fwd.wait_send()
    for fwd in fwds:
        fwd.wait_recv()
    for own in owns:
        own.wait()


def dom_exchange(values, collective, frames=None):
    parts = len(values)
    frames = frames or [(0, v.shape[0]) for v in values]
    outs = [jax.ShapeDtypeStruct((n,) + v.shape[1:], v.dtype) for v, (_, n) in zip(values, frames)]
    relays = [jax.ShapeDtypeStruct((len(RELAYED), v.shape[1] // 2, v.shape[2]), v.dtype) for v in values]
    any_spec = pl.BlockSpec(memory_space=pl.ANY)
    result = pl.pallas_call(
        functools.partial(exchange_kernel, tuple(f[0] for f in frames)),
        out_shape=tuple(outs + relays),
        in_specs=[any_spec] * parts,
        out_specs=tuple([any_spec] * (2 * parts)),
        scratch_shapes=[
            pltpu.SemaphoreType.DMA((parts, len(NEAR))),
            pltpu.SemaphoreType.DMA((parts, len(NEAR))),
            pltpu.SemaphoreType.DMA((parts, len(RELAYED))),
            pltpu.SemaphoreType.DMA((parts, len(RELAYED))),
            pltpu.SemaphoreType.DMA((parts, len(RELAYED))),
            pltpu.SemaphoreType.DMA((parts, len(RELAYED))),
            pltpu.SemaphoreType.DMA((parts,)),
        ],
        compiler_params=pltpu.CompilerParams(collective_id=collective, has_side_effects=True),
    )(*values)
    return result[:parts]


def well_states_of(summed, well_inverse, well_count):
    wells = summed.shape[0]
    live_mask = (jnp.arange(wells) < well_count[0]).astype(jnp.float32)
    solved = jnp.einsum("wst,wtv->wsv", well_inverse, summed, precision=lax.Precision.HIGHEST)
    return (solved * live_mask[:, None, None]).astype(jnp.bfloat16)


def subtract_incoming(product, well_send, incoming):
    targets = well_send[0].reshape(-1)
    selector = (targets[None, :] == jnp.arange(product.shape[0])[:, None]).astype(jnp.bfloat16)
    flat_rows = incoming.reshape(targets.shape[0], product.shape[1], product.shape[2])
    return product - jnp.einsum(
        "bq,qkv->bkv", selector, flat_rows, preferred_element_type=jnp.float32
    )


def on_device(
    blocks,
    tile_values,
    tile_cols,
    halo_send,
    halo_counts,
    grp_send,
    well_send,
    well_slot,
    well_count,
    couple_in,
    couple_out,
    well_inverse,
):
    dom_count = lax.axis_size("dom")
    halo_width = halo_send.shape[2]
    rim_width = grp_send.shape[2]
    slot_width = well_send.shape[2]
    cell_count = blocks.shape[1]
    vec_count = blocks.shape[2]
    wells, couplings = well_slot.shape
    seg = couple_in.shape[2]
    slot_total = dom_count * slot_width
    halo_pack = blocks[halo_send[0]]
    rim_pack = blocks[grp_send[0].reshape(-1)]
    rim_ext = padded(rim_pack, (("grp", 0),), rim_width)
    rim_rows = jnp.concatenate([rim_ext[:rim_width], rim_ext[rim_ext.shape[0] - rim_width :]], 0)
    slot_flat = well_slot.reshape(-1)
    slot_order = jnp.zeros_like(slot_flat).at[slot_flat].set(jnp.arange(slot_flat.shape[0], dtype=slot_flat.dtype))
    slot_well = slot_order // couplings
    couple_both = jnp.concatenate(
        [couple_in.reshape(wells * couplings, seg, cell_count), couple_out.reshape(wells * couplings, seg, cell_count)], 2
    )[slot_order]
    halo_flat = halo_pack.reshape(dom_count, halo_width * cell_count, vec_count)
    (both_recv,) = dom_exchange([couple_both.reshape(dom_count, slot_width * seg, 2 * cell_count)], 0)
    both_recv = both_recv.reshape(slot_total, seg, 2 * cell_count)
    out_recv = both_recv[:, :, cell_count:]
    partial = partial_sums(well_send[0].reshape(-1), both_recv, blocks).reshape(dom_count, slot_width, seg, vec_count)
    partial_in = lax.all_to_all(partial, "dom", split_axis=0, concat_axis=0, tiled=True)
    own_slots = blocks.shape[0] // halo_width
    ext_slots = own_slots + dom_count + 2 * rim_width // halo_width
    (ext_frame,) = dom_exchange([halo_flat], 1, [(own_slots, ext_slots)])
    partial_in, ext_frame = lax.optimization_barrier((partial_in, ext_frame))
    partial_in = partial_in.reshape(slot_total, seg, vec_count)
    summed = well_sums(well_slot.reshape(-1), partial_in, wells)
    well_state = well_states_of(summed, well_inverse, well_count)
    state_pack = well_state[slot_well].reshape(dom_count, slot_width, seg, vec_count)
    state_in = lax.all_to_all(state_pack, "dom", split_axis=0, concat_axis=0, tiled=True)
    state_in = state_in.reshape(slot_total, seg, vec_count)
    live_halo = (jnp.arange(halo_width)[None, :] < halo_counts[0][:, None]).astype(jnp.int32)
    live = jnp.concatenate(
        [jnp.ones((blocks.shape[0],), jnp.int32), live_halo.reshape(-1), jnp.ones((2 * rim_width,), jnp.int32)]
    )
    extended = ext_frame.reshape(ext_slots * halo_width, cell_count, vec_count)
    extended = lax.dynamic_update_slice_in_dim(extended, blocks, 0, 0)
    extended = lax.dynamic_update_slice_in_dim(extended, rim_rows, extended.shape[0] - 2 * rim_width, 0)
    product = local_product(extended, live, tile_values, tile_cols)
    incoming = jnp.einsum(
        "qsk,qsv->qkv",
        out_recv.reshape(slot_total, seg, cell_count),
        state_in,
        preferred_element_type=jnp.float32,
    ).astype(jnp.bfloat16)
    targets = well_send[0].reshape(-1)
    return product.at[targets].add(-incoming.astype(jnp.float32)).astype(jnp.bfloat16)


def solution(mesh):
    in_specs = (
        P(("dom", "grp"), None, None),
        P(("dom", "grp"), None, None, None),
        P(("dom", "grp"), None),
        P(("dom", "grp"), None, None),
        P(("dom", "grp"), None),
        P(("dom", "grp"), None, None),
        P(("dom", "grp"), None, None),
        P(("dom", "grp"), None),
        P(("dom", "grp")),
        P(("dom", "grp"), None, None, None),
        P(("dom", "grp"), None, None, None),
        P(("dom", "grp"), None, None),
    )
    out_specs = P(("dom", "grp"), None, None)
    return jax.shard_map(
        on_device, mesh=mesh, in_specs=in_specs, out_specs=out_specs, check_vma=False
    )
```
